1024 devices in a mesh: cell: 64 (over z, core), inst: 16 (over x, y).
Axes of the slice: x: 4, y: 4, z: 32, core: 2. Of those that a mesh axis runs over, the one named last changes fastest.
Arguments:
- residual: float32 [16, 5, 1024, 256], P('inst', None, 'cell'), may hold values from -6 to 6
- diag_gain: float32 [16, 1024, 256], P('inst', 'cell'), may hold values from 2.7 to 3
- flux_jac: float32 [4, 5, 5], replicated, may hold values from -1.75 to 1.75
- omega: float32 [1], replicated, may hold values from 0.04 to 0.12
- shifts: float32 [7], replicated, may hold values from 1.45 to 1.55
Outputs:
- basis_q: float32 [8, 16, 5, 1024, 256], P(None, 'inst', None, 'cell')
- factor_r: float32 [8, 8], replicated
The draws below stay inside these ranges and needn't reach their ends.
All inputs are finite; a program needn't handle non-finite values.
Results may differ from the reference program's by a relative error of at most 0.0003.
Values sent between devices are 32-bit elements; how exact they have to be, the bound alone decides.
No kernel may reach another device: no remote copies, remote signals or barrier semaphores. Data moves between devices by JAX's collectives and lax.ppermute only.
A program may use at most 32 MiB of HBM per device.

```python
import math
import jax
import jax.numpy as jnp
from jax import lax

S = 8
FIELDS = 5
NC = 256
INST = 16
NR = 1024


def level_of(stream_key, shape, shards, low, largest):
    def one(dim, blocks):
        draws = jax.random.uniform(jax.random.fold_in(jax.random.fold_in(stream_key, 6), dim), (blocks,), jnp.float32, low / len(shards), largest / len(shards))
        return jnp.repeat(jnp.exp(draws), shape[dim] // blocks).reshape((-1,) + (1,) * (len(shape) - dim - 1))

    factor_of = one(*shards[0])
    for cut in shards[1:]:
        factor_of = factor_of * one(*cut)
    return factor_of


def scatter_about(key, extent, spread, limit, pieces=(), kind=jnp.bfloat16):
    entries = spread * jax.random.normal(key, extent, jnp.float32)
    if pieces:
        entries = entries * level_of(key, extent, pieces, -0.22, 0.18)
    return jnp.clip(entries, -limit, limit).astype(kind)


def setup_inputs(seed: int = 0) -> dict:
    arg_keys = jax.random.split(jax.random.key(seed), 6)
    return {
        "residual": scatter_about(arg_keys[0], (INST, FIELDS, NR, NC), 1.0, 6.0, ((0, 16), (2, 64)), jnp.float32),
        "diag_gain": jnp.clip(jnp.exp(math.log(3.0) - 0.1053605 * jax.random.uniform(arg_keys[1], (INST, NR, NC), jnp.float32) ** level_of(arg_keys[1], (INST, NR, NC), ((0, 16), (1, 64)), -0.2, 0.2)), 2.7, 3.0),
        "flux_jac": scatter_about(arg_keys[2], (4, FIELDS, FIELDS), 11 ** -0.5, 1.75, (), jnp.float32),
        "omega": jnp.clip(jax.random.uniform(arg_keys[3], (1,), jnp.float32, 0.04, 0.12), 0.04, 0.12),
        "shifts": jnp.clip(jax.random.uniform(arg_keys[4], (S - 1,), jnp.float32, 1.45, 1.55), 1.45, 1.55),
    }


def spectral_matrix(count):
    index = jnp.arange(count, dtype=jnp.int32)
    offset = index[:, None] - index[None, :]
    parity = (1 - 2 * (jnp.abs(offset) % 2)).astype(jnp.float32)
    angle = jnp.pi * offset.astype(jnp.float32) / count
    denom = jnp.where(offset == 0, 1.0, jnp.sin(angle))
    return jnp.where(offset == 0, 0.0, 0.5 * parity * jnp.cos(angle) / denom).astype(jnp.float32)

def operate(field, diag_gain, flux_jac, omega, coupling):
    padded = jnp.pad(field, ((0, 0), (0, 0), (1, 1), (1, 1)))
    neighbours = [padded[:, :, :-2, 1:-1], padded[:, :, 2:, 1:-1], padded[:, :, 1:-1, :-2], padded[:, :, 1:-1, 2:]]
    total = diag_gain[:, None] * field
    for direction in range(4):
        total = total - jnp.einsum('fe,ierc->ifrc', flux_jac[direction], neighbours[direction], precision=lax.Precision.HIGHEST)
    mixed = jnp.einsum('ij,jfrc->ifrc', coupling, field, precision=lax.Precision.HIGHEST)
    return total + omega[0] * mixed

def reference(residual, diag_gain, flux_jac, omega, shifts):
    coupling = spectral_matrix(residual.shape[0])
    vectors = [residual]
    for step in range(S - 1):
        prior = vectors[-1]
        vectors.append(operate(prior, diag_gain, flux_jac, omega, coupling) - shifts[step] * prior)
    stacked = jnp.stack(vectors)
    matrix = stacked.reshape(S, -1)
    gram_one = jnp.dot(matrix, matrix.T, precision=lax.Precision.HIGHEST)
    lower_one = jnp.linalg.cholesky(gram_one)
    whitened = jax.scipy.linalg.solve_triangular(lower_one, matrix, lower=True)
    gram_two = jnp.dot(whitened, whitened.T, precision=lax.Precision.HIGHEST)
    lower_two = jnp.linalg.cholesky(gram_two)
    ortho = jax.scipy.linalg.solve_triangular(lower_two, whitened, lower=True)
    factor_r = jnp.dot(lower_one, lower_two, precision=lax.Precision.HIGHEST).T
    return (ortho.reshape(stacked.shape), factor_r)
```

```python
import functools

import jax
import jax.numpy as jnp
import numpy as np
from jax import lax
from jax.experimental import pallas as pl
from jax.experimental.pallas import tpu as pltpu
from jax.sharding import PartitionSpec as P

S = 8
FIELDS = 5
INST = 16
CELLS = 64
HALO = 8
ROWS = 16
COLS = 16
NC = 256
NR = 1024
STATE = FIELDS + 1
PACKED = FIELDS * 2
VMEM = pl.BlockSpec(memory_space=pltpu.VMEM)
SMEM = pl.BlockSpec(memory_space=pltpu.SMEM)
TILE = (8, 128)


def lanes():
    return lax.broadcasted_iota(jnp.int32, TILE, 1)


def sublanes():
    return lax.broadcasted_iota(jnp.int32, TILE, 0)


def two_sum(a, b):
    total = a + b
    part = total - a
    return total, (a - (total - part)) + (b - part)


def split(a):
    scaled = a * 4097.0
    high = scaled - (scaled - a)
    return high, a - high


def two_prod(a, b):
    product = a * b
    a_high, a_low = split(a)
    b_high, b_low = split(b)
    error = ((a_high * b_high - product) + a_high * b_low + a_low * b_high) + a_low * b_low
    return product, error


def pack_kernel(res_ref, gain_ref, below_ref, above_ref, out_ref):
    lane = lanes()
    group = lane // 32
    for field in range(STATE):
        own = res_ref.at[0, field] if field < FIELDS else gain_ref.at[0]
        rows = [below_ref[field], own[0:8, :], own[8:16, :], above_ref[field]]
        chunks = [None] * INST
        for part in range(4):
            left, right = rows[part][:, :128], rows[part][:, 128:]
            for turn in range(8):
                shift = 16 * turn + 8
                rolled_left = pltpu.roll(left, shift, 1)
                rolled_right = pltpu.roll(right, shift, 1)
                first = lane < shift
                for turns, moved in (
                    (turn, jnp.where(first, rolled_right, rolled_left)),
                    (turn + 8, jnp.where(first, rolled_left, rolled_right)),
                ):
                    chunk = (2 * part - turns) % 16
                    old = chunks[chunk]
                    chunks[chunk] = moved if old is None else jnp.where(group == part, moved, old)
        for chunk in range(INST):
            out_ref[chunk, field * 8 : field * 8 + 8, :] = chunks[chunk]


def merge_pair(first, second, mask, shift, axis):
    high = [jnp.where(mask, second[0], first[0]), jnp.where(mask, first[0], second[0])]
    total, error = two_sum(high[0], pltpu.roll(high[1], shift, axis))
    if first[1] is None:
        return total, error
    low = jnp.where(mask, second[1], first[1]) + pltpu.roll(
        jnp.where(mask, first[1], second[1]), shift, axis
    )
    return total, error + low


def fold_pair(pair, shift, axis):
    total, error = two_sum(pair[0], pltpu.roll(pair[0], shift, axis))
    return total, error + (pair[1] + pltpu.roll(pair[1], shift, axis))


def step_kernel(table, in_ref, jac_ref, omega_ref, shift_ref, out_ref, vec_ref, coef_ref, mix_ref, gain_ref):
    lane, sub = lanes(), sublanes()
    cell, inst = lax.axis_index("cell"), lax.axis_index("inst")
    row = cell * ROWS - HALO + (lane // 32) * 8 + sub
    col = inst * COLS - HALO + lane % 32
    inside = (row >= 0) & (row < NR) & (col >= 0) & (col < NC)
    first_row, last_row = sub == 0, sub == 7
    for d in range(4):
        for f in range(FIELDS):
            for e in range(FIELDS):
                coef_ref[(d * FIELDS + f) * FIELDS + e] = jnp.full(TILE, jac_ref[d, f, e])
    for i in range(INST):
        for f in range(FIELDS):
            vec_ref[0, i, f] = jnp.where(inside, in_ref[i, f * 8 : f * 8 + 8, :], 0.0)
        gain_ref[i] = in_ref[i, FIELDS * 8 : FIELDS * 8 + 8, :]
    weights = [None] + [jnp.full(TILE, omega_ref[0] * table[d]) for d in range(1, 9)]

    def step(n, carry):
        shift = shift_ref[n]
        for f in range(FIELDS):
            v = [vec_ref[n, i, f] for i in range(INST)]
            mixed = [weights[8] * v[(i + 8) % INST] for i in range(INST)]
            for i in range(8):
                for d in range(1, 8):
                    gap = v[(i - d) % INST] - v[(i + d) % INST]
                    mixed[i] = mixed[i] + weights[d] * gap
                    mixed[i + 8] = mixed[i + 8] - weights[8 - d] * gap
            for i in range(INST):
                mix_ref[i, f] = mixed[i]
        for pair in range(0, INST, 2):
            members = (pair, pair + 1)
            near, center = {}, {}
            for i in members:
                for e in range(FIELDS):
                    v = vec_ref[n, i, e]
                    center[i, e] = v
                    down = pltpu.roll(v, 1, 0)
                    up = pltpu.roll(v, 7, 0)
                    near[i, 0, e] = jnp.where(first_row, pltpu.roll(down, 32, 1), down)
                    near[i, 1, e] = jnp.where(last_row, pltpu.roll(up, 96, 1), up)
                    near[i, 2, e] = pltpu.roll(v, 1, 1)
                    near[i, 3, e] = pltpu.roll(v, 127, 1)
            for f in range(FIELDS):
                total = {i: mix_ref[i, f] + (gain_ref[i] - shift) * center[i, f] for i in members}
                for d in range(4):
                    for e in range(FIELDS):
                        c = coef_ref[(d * FIELDS + f) * FIELDS + e]
                        for i in members:
                            total[i] = total[i] - c * near[i, d, e]
                for i in members:
                    vec_ref[n + 1, i, f] = jnp.where(inside, total[i], 0.0)
        return carry

    lax.fori_loop(0, S - 1, step, 0)

    pairs = [(a, b) for a in range(S) for b in range(a, S)]
    seg = lane // 16

    def gather(i, sums):
        sums = list(sums)
        for f in range(FIELDS):
            v = [vec_ref[s, i, f] for s in range(S)]
            for p, (a, b) in enumerate(pairs):
                sums[p] = sums[p] + v[a] * v[b]
            for half in range(2):
                a, b, c, d = v[4 * half : 4 * half + 4]
                a, b, c, d = pltpu.roll(a, 120, 1), pltpu.roll(b, 8, 1), pltpu.roll(c, 56, 1), pltpu.roll(d, 72, 1)
                tile = jnp.where(
                    (seg == 2) | (seg == 4),
                    a,
                    jnp.where((seg == 3) | (seg == 5), b, jnp.where((seg == 0) | (seg == 6), c, d)),
                )
                out_ref[i, (2 * f + half) * 8 : (2 * f + half) * 8 + 8, :] = tile
        return tuple(sums)

    sums = lax.fori_loop(0, INST, gather, tuple(jnp.zeros(TILE, jnp.float32) for _ in pairs))
    column = lane % 32
    own = (lane >= 32) & (lane < 96) & (column >= HALO) & (column < HALO + COLS)
    entry = {}
    for p, (a, b) in enumerate(pairs):
        entry[a, b] = entry[b, a] = (jnp.where(own, sums[p], 0.0), None)
    columns = []
    for b in range(S):
        level = [entry[a, b] for a in range(S)]
        for bit in (1, 2, 4):
            mask = (sub & bit) != 0
            level = [merge_pair(level[2 * q], level[2 * q + 1], mask, bit, 0) for q in range(len(level) // 2)]
        columns.append(level[0])
    for bit in (1, 2, 4):
        mask = (lane & bit) != 0
        columns = [merge_pair(columns[2 * q], columns[2 * q + 1], mask, bit, 1) for q in range(len(columns) // 2)]
    high, low = columns[0]
    for i in range(INST):
        out_ref[i, PACKED * 8 : PACKED * 8 + 8, :] = high
        out_ref[i, PACKED * 8 + 8 : PACKED * 8 + 16, :] = low


def gram_kernel(in_ref, out_ref):
    lane, sub = lanes(), sublanes()
    level = [
        (in_ref[i, PACKED * 8 : PACKED * 8 + 8, :], in_ref[i, PACKED * 8 + 8 : PACKED * 8 + 16, :])
        for i in range(INST)
    ]
    while len(level) > 1:
        merged = []
        for q in range(0, len(level), 2):
            total, error = two_sum(level[q][0], level[q + 1][0])
            merged.append((total, error + (level[q][1] + level[q + 1][1])))
        level = merged
    pair = level[0]
    for shift in (8, 16, 32, 64):
        pair = fold_pair(pair, shift, 1)
    slot = lane // 8
    row = jnp.where(slot == sub, pair[0], jnp.where(slot == sub + 8, pair[1], 0.0))
    row = jnp.broadcast_to(jnp.sum(row, axis=0, keepdims=True), TILE)
    for q in range(CELLS // 8):
        out_ref[q * 8 : q * 8 + 8, :] = row


def unpack_kernel(in_ref, out_ref):
    seg = lanes() // 16
    places = ((2, 1), (3, 1), (0, 0), (1, 0), (0, 1), (1, 1), (2, 0), (3, 0))
    for f in range(FIELDS):
        for half in range(2):
            for wide in range(2):
                start = (2 * f + half) * 8
                tiles = [in_ref[8 * wide + q, start : start + 8, :] for q in range(8)]
                for bit in (1, 2, 4):
                    off = (seg & bit) == 0
                    for q in range(8):
                        if q & bit:
                            continue
                        a, b = tiles[q], tiles[q + bit]
                        tiles[q] = jnp.where(off, a, pltpu.roll(b, 16 * bit, 1))
                        tiles[q + bit] = jnp.where(off, pltpu.roll(a, 128 - 16 * bit, 1), b)
                for q, (s, part) in enumerate(places):
                    out_ref[4 * half + s, 0, f, 8 * part : 8 * part + 8, 128 * wide : 128 * wide + 128] = tiles[q]


def lane_of(x, k):
    return jnp.broadcast_to(x[:, k : k + 1], TILE)


def row_of(x, k):
    return jnp.broadcast_to(x[k : k + 1, :], TILE)


def factor(high, low):
    lane, sub = lanes(), sublanes()
    high = jnp.where(lane < S, high, jnp.where(lane == sub + S, 1.0, 0.0))
    lower, inverse = jnp.zeros(TILE, jnp.float32), jnp.zeros(TILE, jnp.float32)
    for k in range(S):
        full = high if low is None else high + jnp.where(lane < S, low, 0.0)
        pivot = jnp.broadcast_to(full[k : k + 1, k : k + 1], TILE)
        scale = 1.0 / jnp.sqrt(pivot)
        left = jnp.where(sub >= k, lane_of(full, k) * scale, 0.0)
        right = jnp.where((lane >= k) & (lane < 2 * S), row_of(full, k) * scale, 0.0)
        lower = jnp.where(lane == k, left, lower)
        inverse = jnp.where(sub == k, right, inverse)
        if low is None:
            high = high - left * right
        else:
            product, error = two_prod(left, right)
            high, rest = two_sum(high, -product)
            low = low + (rest - error)
    inverse = jnp.where(lane < S, pltpu.roll(inverse, 128 - S, 1), 0.0)
    return lower, inverse, None if low is None else jnp.where(lane < S, high + low, 0.0)


def small_dot(a, b, flip=False):
    dims = (((1,), (1 if flip else 0,)), ((), ()))
    return lax.dot_general(
        a if flip else a[:, :S], b, dims, precision=lax.Precision.HIGHEST, preferred_element_type=jnp.float32
    )


def finish_kernel(rows_ref, vec_ref, out_ref, factor_ref):
    lane, sub = lanes(), sublanes()
    level = [(rows_ref[q * 8 : q * 8 + 8, :], jnp.zeros(TILE, jnp.float32)) for q in range(CELLS // 8)]
    while len(level) > 1:
        merged = []
        for q in range(0, len(level), 2):
            total, error = two_sum(level[q][0], level[q + 1][0])
            merged.append((total, error + (level[q][1] + level[q + 1][1])))
        level = merged
    pair = level[0]
    for shift in (1, 2, 4):
        pair = fold_pair(pair, shift, 0)
    high, low = pair[0], pair[1] + pltpu.roll(pair[0], 64, 1)
    for bit in (1, 2, 4):
        mask = (sub & bit) != 0
        high = jnp.where(mask, pltpu.roll(high, 128 - 8 * bit, 1), high)
        low = jnp.where(mask, pltpu.roll(low, 128 - 8 * bit, 1), low)
    lower_one, inverse_one, rest = factor(high, low)
    half = small_dot(inverse_one, rest)
    square = jnp.zeros(TILE, jnp.float32)
    flipped = jnp.transpose(jnp.concatenate([inverse_one] * 16, axis=0))[:S, :]
    flipped = jnp.where(lane < S, flipped, 0.0)
    square = small_dot(half, flipped)
    gram_two = square + jnp.where(lane == sub, 1.0, 0.0)
    lower_two, inverse_two, _ = factor(gram_two, None)
    factor_ref[...] = small_dot(lower_one, lower_two)[:, :S]
    inverse = small_dot(inverse_two, inverse_one)
    weight = {(a, b): jnp.broadcast_to(inverse[a : a + 1, b : b + 1], TILE) for a in range(S) for b in range(a + 1)}
    for f in range(FIELDS):
        for part in range(2):
            for wide in range(2):
                place = (0, f, pl.ds(8 * part, 8), pl.ds(128 * wide, 128))
                v = [vec_ref[(s, *place)] for s in range(S)]
                for a in range(S):
                    total = weight[a, 0] * v[0]
                    for b in range(1, a + 1):
                        total = total + weight[a, b] * v[b]
                    out_ref[(a, *place)] = total


def call(kernel, out_shape, in_specs, args, scratch=(), flops=10**6):
    shapes = jax.tree.map(lambda s: jax.ShapeDtypeStruct(s, jnp.float32), out_shape, is_leaf=lambda s: isinstance(s[0], int))
    return pl.pallas_call(
        kernel,
        out_shape=shapes,
        in_specs=in_specs,
        out_specs=jax.tree.map(lambda _: VMEM, shapes),
        scratch_shapes=scratch,
        compiler_params=pltpu.CompilerParams(vmem_limit_bytes=40 * 2**20),
        cost_estimate=pl.CostEstimate(flops=flops, transcendentals=0, bytes_accessed=2 * 10**6),
    )(*args)


def coupling_table():
    table = []
    for d in range(9):
        angle = np.float32(np.pi) * np.float32(d) / np.float32(INST)
        sign = -1.0 if d % 2 else 1.0
        table.append(float(np.float32(0.5 * sign * np.cos(angle) / np.sin(angle))) if d else 0.0)
    return tuple(table)


def on_device(residual, diag_gain, flux_jac, omega, shifts):
    def edge(rows):
        return jnp.concatenate([residual[0, :, rows, :], diag_gain[:, rows, :]], axis=0)

    ends = CELLS - 1
    below = lax.ppermute(edge(slice(8, 16)), "cell", [(i, i + 1) for i in range(ends)])
    above = lax.ppermute(edge(slice(0, 8)), "cell", [(i + 1, i) for i in range(ends)])
    chunks = call(pack_kernel, (INST, STATE * 8, 128), [VMEM] * 4, (residual, diag_gain, below, above))
    patches = lax.all_to_all(chunks, "inst", 0, 0, tiled=True)
    vectors = call(
        functools.partial(step_kernel, coupling_table()),
        (INST, PACKED * 8 + 16, 128),
        [VMEM, SMEM, SMEM, SMEM],
        (patches, flux_jac, omega, shifts),
        scratch=[
            pltpu.VMEM((S, INST, FIELDS, *TILE), jnp.float32),
            pltpu.VMEM((4 * FIELDS * FIELDS, *TILE), jnp.float32),
            pltpu.VMEM((INST, FIELDS, *TILE), jnp.float32),
            pltpu.VMEM((INST, *TILE), jnp.float32),
        ],
        flops=10**8,
    )
    back = lax.all_to_all(vectors, "inst", 0, 0, tiled=True)
    rows = lax.all_to_all(call(gram_kernel, (CELLS, 128), [VMEM], (back,)), "cell", 0, 0, tiled=True)
    basis = call(unpack_kernel, (S, 1, FIELDS, ROWS, NC), [VMEM], (back,))
    ortho, factor_l = call(
        finish_kernel, ((S, 1, FIELDS, ROWS, NC), (S, S)), [VMEM, VMEM], (rows, basis)
    )
    return (ortho, factor_l.T)


def solution(mesh):
    in_specs = (P("inst", None, "cell", None), P("inst", "cell", None), P(), P(), P())
    out_specs = (P(None, "inst", None, "cell", None), P())
    return jax.shard_map(
        on_device, mesh=mesh, in_specs=in_specs, out_specs=out_specs, check_vma=False
    )
```

```python
import functools

import jax
import jax.numpy as jnp
import numpy as np
from jax import lax
from jax.experimental import pallas as pl
from jax.experimental.pallas import tpu as pltpu
from jax.sharding import PartitionSpec as P

S = 8
FIELDS = 5
INST = 16
CELLS = 64
HALO = 8
ROWS = 16
COLS = 16
NC = 256
NR = 1024
STATE = FIELDS + 1
VMEM = pl.BlockSpec(memory_space=pltpu.VMEM)
SMEM = pl.BlockSpec(memory_space=pltpu.SMEM)
TILE = (8, 128)


def lanes():
    return lax.broadcasted_iota(jnp.int32, TILE, 1)


def sublanes():
    return lax.broadcasted_iota(jnp.int32, TILE, 0)


def two_sum(a, b):
    total = a + b
    part = total - a
    return total, (a - (total - part)) + (b - part)


def split(a):
    scaled = a * 4097.0
    high = scaled - (scaled - a)
    return high, a - high


def pack_kernel(res_ref, gain_ref, below_ref, above_ref, out_ref):
    lane = lanes()
    group = lane // 32
    for field in range(STATE):
        own = res_ref.at[0, field] if field < FIELDS else gain_ref.at[0]
        rows = [below_ref[field], own[0:8, :], own[8:16, :], above_ref[field]]
        chunks = [None] * INST
        for part in range(4):
            left, right = rows[part][:, :128], rows[part][:, 128:]
            for turn in range(8):
                shift = 16 * turn + 8
                rolled_left = pltpu.roll(left, shift, 1)
                rolled_right = pltpu.roll(right, shift, 1)
                first = lane < shift
                for turns, moved in (
                    (turn, jnp.where(first, rolled_right, rolled_left)),
                    (turn + 8, jnp.where(first, rolled_left, rolled_right)),
                ):
                    chunk = (2 * part - turns) % 16
                    old = chunks[chunk]
                    chunks[chunk] = moved if old is None else jnp.where(group == part, moved, old)
        for chunk in range(INST):
            out_ref[chunk, field * 8 : field * 8 + 8, :] = chunks[chunk]


def merge_pair(first, second, mask, shift, axis):
    high = [jnp.where(mask, second[0], first[0]), jnp.where(mask, first[0], second[0])]
    total, error = two_sum(high[0], pltpu.roll(high[1], shift, axis))
    if first[1] is None:
        return total, error
    low = jnp.where(mask, second[1], first[1]) + pltpu.roll(
        jnp.where(mask, first[1], second[1]), shift, axis
    )
    return total, error + low


def fold_pair(pair, shift, axis):
    total, error = two_sum(pair[0], pltpu.roll(pair[0], shift, axis))
    return total, error + (pair[1] + pltpu.roll(pair[1], shift, axis))


def rotations(table):
    c = [0.0, *table]
    plus = [None] + [c[d] - c[8 - d] for d in (1, 2, 3)]
    minus = [None] + [(c[d] + c[8 - d]) / 2 for d in (1, 2, 3, 4)]
    return ((plus[1] - plus[3]) / 4, (plus[1] + plus[3]) / 4, plus[2] / 2, *minus[1:])


def gap(x, i, d):
    n = len(x)
    before, after = x[(i - d) % n], x[(i + d) % n]
    if i - d < 0:
        return before + after, -1
    return (before - after if i + d < n else before + after), 1


def turned(x, i, weights):
    n = len(x)
    total = None
    for d, weight in enumerate(weights, 1):
        if 2 * d < n:
            value, sign = gap(x, i, d)
        else:
            value, sign = x[(i - d) % n], (1 if i >= d else -1)
        term = weight * value
        if total is None:
            total = term if sign > 0 else -term
        else:
            total = total + term if sign > 0 else total - term
    return total


def coupled(v, weights):
    inner, first, second = weights[:3]
    plus = [v[i] + v[i + 8] for i in range(8)]
    minus = [v[i] - v[i + 8] for i in range(8)]
    sums = [plus[i] + plus[i + 4] for i in range(4)]
    gaps = [plus[i] - plus[i + 4] for i in range(4)]
    even, odd = inner * (sums[3] - sums[1]), inner * (sums[0] - sums[2])
    circle = [even, odd, -even, -odd]
    twisted = [turned(gaps, i, (first, second)) for i in range(4)]
    outer = [circle[i] + twisted[i] for i in range(4)] + [circle[i] - twisted[i] for i in range(4)]
    flipped = [turned(minus, i, weights[3:]) for i in range(8)]
    return [outer[i] + flipped[i] for i in range(8)] + [outer[i] - flipped[i] for i in range(8)]


SLOTS = ((2, 4), (3, 5), (6, 0), (7, 1))
OFFSETS = (0, 1, 4, 5)
MOVES = {(0, 0): (0, 1, 4, 5), (1, 1): (0, 1, 4, 5), (0, 1): (0, 1, 3, 4, 5, 7)}


def in_slot(seg, q):
    return (seg == SLOTS[q][0]) | (seg == SLOTS[q][1])


def pack_four(seg, a, b, c, d):
    a, b, c, d = pltpu.roll(a, 120, 1), pltpu.roll(b, 8, 1), pltpu.roll(c, 56, 1), pltpu.roll(d, 72, 1)
    return jnp.where(in_slot(seg, 0), a, jnp.where(in_slot(seg, 1), b, jnp.where(in_slot(seg, 2), c, d)))


def step_kernel(rotation, in_ref, jac_ref, omega_ref, shift_ref, out_ref, vec_ref, coef_ref, mix_ref, gain_ref):
    lane, sub = lanes(), sublanes()
    seg = lane // 16
    cell, inst = lax.axis_index("cell"), lax.axis_index("inst")
    row = cell * ROWS - HALO + (lane // 32) * 8 + sub
    col = inst * COLS - HALO + lane % 32
    inside = (row >= 0) & (row < NR) & (col >= 0) & (col < NC)
    first_row, last_row = sub == 0, sub == 7
    for d in range(4):
        for f in range(FIELDS):
            for e in range(FIELDS):
                coef_ref[(d * FIELDS + f) * FIELDS + e] = jnp.full(TILE, jac_ref[d, f, e])
    for i in range(INST):
        for f in range(FIELDS):
            vec_ref[0, i, f] = jnp.where(inside, in_ref[i, f * 8 : f * 8 + 8, :], 0.0)
        gain_ref[i] = in_ref[i, FIELDS * 8 : FIELDS * 8 + 8, :]
    weights = [jnp.full(TILE, omega_ref[0] * w) for w in rotation]

    def step(n, carry):
        shift = shift_ref[n]
        for f in range(FIELDS):
            mixed = coupled([vec_ref[n, i, f] for i in range(INST)], weights)
            for i in range(INST):
                mix_ref[i, f] = mixed[i]
        for pair in range(0, INST, 2):
            members = (pair, pair + 1)
            near, center = {}, {}
            for i in members:
                for e in range(FIELDS):
                    v = vec_ref[n, i, e]
                    center[i, e] = v
                    down = pltpu.roll(v, 1, 0)
                    up = pltpu.roll(v, 7, 0)
                    near[i, 0, e] = jnp.where(first_row, pltpu.roll(down, 32, 1), down)
                    near[i, 1, e] = jnp.where(last_row, pltpu.roll(up, 96, 1), up)
                    near[i, 2, e] = pltpu.roll(v, 1, 1)
                    near[i, 3, e] = pltpu.roll(v, 127, 1)
            for f in range(FIELDS):
                total = {i: mix_ref[i, f] + (gain_ref[i] - shift) * center[i, f] for i in members}
                for d in range(4):
                    for e in range(FIELDS):
                        c = coef_ref[(d * FIELDS + f) * FIELDS + e]
                        for i in members:
                            total[i] = total[i] - c * near[i, d, e]
                for i in members:
                    vec_ref[n + 1, i, f] = jnp.where(inside, total[i], 0.0)
        return carry

    lax.fori_loop(0, S - 1, step, 0)

    keys = [(x, y, move) for (x, y), moves in MOVES.items() for move in moves]

    def gather(i, sums):
        sums = list(sums)
        tiles = {}
        for f in range(FIELDS):
            for x in range(2):
                tiles[x, f] = pack_four(seg, *[vec_ref[4 * x + q, i, f] for q in range(4)])
            moved = {}
            for p, (x, y, move) in enumerate(keys):
                if (y, move) not in moved:
                    moved[y, move] = pltpu.roll(tiles[y, f], 16 * move, 1) if move else tiles[y, f]
                sums[p] = sums[p] + tiles[x, f] * moved[y, move]
            out_ref[i, (4 + f) * 8 : (4 + f) * 8 + 8, :] = tiles[1, f]
        for f in range(4):
            tile = tiles[0, f]
            if f < 3:
                move = (OFFSETS[0] - OFFSETS[f + 1]) % 8
                tile = jnp.where(in_slot(seg, 0), pltpu.roll(tiles[0, 4], 16 * move, 1), tile)
            out_ref[i, f * 8 : f * 8 + 8, :] = tile
        return tuple(sums)

    sums = lax.fori_loop(0, INST, gather, tuple(jnp.zeros(TILE, jnp.float32) for _ in keys))
    entry = {}
    for p, (x, y, move) in enumerate(keys):
        for q in range(4):
            for r in range(4):
                a, b = 4 * x + q, 4 * y + r
                if (OFFSETS[q] - OFFSETS[r]) % 8 == move and (a, b) not in entry:
                    entry[a, b] = entry[b, a] = (jnp.where(in_slot(seg, q), sums[p], 0.0), None)
    columns = []
    for b in range(S):
        level = [entry[a, b] for a in range(S)]
        for bit in (1, 2, 4):
            mask = (sub & bit) != 0
            level = [merge_pair(level[2 * q], level[2 * q + 1], mask, bit, 0) for q in range(len(level) // 2)]
        columns.append(level[0])
    for bit in (1, 2, 4):
        mask = (lane & bit) != 0
        columns = [merge_pair(columns[2 * q], columns[2 * q + 1], mask, bit, 1) for q in range(len(columns) // 2)]
    high, low = fold_pair(columns[0], 64, 1)
    pair = jnp.where(lane < 64, high, low)
    for i in range(INST):
        out_ref[i, 72:80, :] = pair


def gram_kernel(in_ref, out_ref):
    lane, sub = lanes(), sublanes()
    total, error = sum_pairs([in_ref[i, 72:80, :] for i in range(INST)])
    lower = lane < 64
    other = pltpu.roll(total, 64, 1)
    low = jnp.where(lower, other, total) + jnp.where(lower, error, pltpu.roll(error, 64, 1))
    pair = (jnp.where(lower, total, other), low)
    for shift in (8, 16, 32):
        pair = fold_pair(pair, shift, 1)
    slot = lane // 8
    row = jnp.where(slot == sub, pair[0], jnp.where(slot == sub + 8, pair[1], 0.0))
    row = jnp.broadcast_to(jnp.sum(row, axis=0, keepdims=True), TILE)
    for q in range(CELLS // 8):
        out_ref[q * 8 : q * 8 + 8, :] = row


def sum_pairs(values):
    level = [(v, None) for v in values]
    while len(level) > 1:
        merged = []
        for q in range(0, len(level), 2):
            total, error = two_sum(level[q][0], level[q + 1][0])
            if level[q][1] is not None:
                error = error + (level[q][1] + level[q + 1][1])
            merged.append((total, error))
        level = merged
    return level[0]


def unpack_kernel(in_ref, out_ref):
    seg = lanes() // 16
    places = {}
    for q, segs in enumerate(SLOTS):
        for part in range(2):
            places[segs[part]] = (q, part)
    for tile in range(9):
        for wide in range(2):
            tiles = [in_ref[8 * wide + q, tile * 8 : tile * 8 + 8, :] for q in range(8)]
            for bit in (1, 2, 4):
                off = (seg & bit) == 0
                for q in range(8):
                    if q & bit:
                        continue
                    a, b = tiles[q], tiles[q + bit]
                    tiles[q] = jnp.where(off, a, pltpu.roll(b, 16 * bit, 1))
                    tiles[q + bit] = jnp.where(off, pltpu.roll(a, 128 - 16 * bit, 1), b)
            for q in range(8):
                s, part = places[q]
                if tile >= 4:
                    s, f = 4 + s, tile - 4
                elif s:
                    f = tile
                elif tile < 3:
                    s, f = tile + 1, 4
                else:
                    continue
                out_ref[s - 1, 0, f, 8 * part : 8 * part + 8, 128 * wide : 128 * wide + 128] = tiles[q]


TRIANGLE = [(i, j) for i in range(S) for j in range(i + 1)]


def inverse_of(lower, scale):
    inverse = {}
    for i in range(S):
        inverse[i, i] = scale[i]
        for j in range(i):
            total = lower[i, j] * inverse[j, j]
            for k in range(j + 1, i):
                total = total + lower[i, k] * inverse[k, j]
            inverse[i, j] = -(scale[i] * total)
    return inverse


def product_of(a, b):
    out = {}
    for i, j in TRIANGLE:
        total = a[i, j] * b[j, j]
        for k in range(j + 1, i + 1):
            total = total + a[i, k] * b[k, j]
        out[i, j] = total
    return out


def factor_pairs(high, low):
    lower, scale = {}, {}
    for k in range(S):
        full = {i: high[i, k] + low[i, k] for i in range(k, S)}
        scale[k] = lax.rsqrt(full[k])
        parts = {}
        for i in range(k, S):
            lower[i, k] = full[i] * scale[k]
            parts[i] = split(lower[i, k])
        for i in range(k, S):
            for j in range(k, i + 1):
                (a_high, a_low), (b_high, b_low) = parts[i], parts[j]
                product = lower[i, k] * lower[j, k]
                error = ((a_high * b_high - product) + a_high * b_low + a_low * b_high) + a_low * b_low
                high[i, j], rest = two_sum(high[i, j], -product)
                low[i, j] = low[i, j] + (rest - error)
    return lower, inverse_of(lower, scale), {at: high[at] + low[at] for at in TRIANGLE}


def factor_plain(matrix):
    lower, scale = {}, {}
    for k in range(S):
        scale[k] = lax.rsqrt(matrix[k, k])
        for i in range(k, S):
            lower[i, k] = matrix[i, k] * scale[k]
        for i in range(k + 1, S):
            for j in range(k + 1, i + 1):
                matrix[i, j] = matrix[i, j] - lower[i, k] * lower[j, k]
    return lower, inverse_of(lower, scale)


def finish_kernel(rows_ref, res_ref, vec_ref, out_ref, factor_ref):
    lane, sub = lanes(), sublanes()
    pair = sum_pairs([rows_ref[q * 8 : q * 8 + 8, :] for q in range(CELLS // 8)])
    for shift in (1, 2, 4):
        pair = fold_pair(pair, shift, 0)
    low_row = pair[1] + pltpu.roll(pair[0], 64, 1)
    high = {(i, j): jnp.broadcast_to(pair[0][:, 8 * i + j : 8 * i + j + 1], TILE) for i, j in TRIANGLE}
    low = {(i, j): jnp.broadcast_to(low_row[:, 8 * i + j : 8 * i + j + 1], TILE) for i, j in TRIANGLE}
    lower_one, inverse_one, rest = factor_pairs(high, low)
    half = {}
    for i in range(S):
        for j in range(i + 1):
            total = None
            for k in range(i + 1):
                term = inverse_one[i, k] * rest[max(k, j), min(k, j)]
                total = term if total is None else total + term
            half[i, j] = total
    square = {}
    for i, j in TRIANGLE:
        total = half[i, 0] * inverse_one[j, 0]
        for k in range(1, j + 1):
            total = total + half[i, k] * inverse_one[j, k]
        square[i, j] = total + 1.0 if i == j else total
    lower_two, inverse_two = factor_plain(square)
    lower = product_of(lower_one, lower_two)
    weight = product_of(inverse_two, inverse_one)
    block = jnp.zeros(TILE, jnp.float32)
    for i, j in TRIANGLE:
        block = jnp.where((sub == j) & (lane == i), lower[i, j], block)
    factor_ref[...] = block[:, :S]
    for f in range(FIELDS):
        for part in range(2):
            for wide in range(2):
                place = (0, f, pl.ds(8 * part, 8), pl.ds(128 * wide, 128))
                v = [res_ref[place]] + [vec_ref[(s, *place)] for s in range(S - 1)]
                for a in range(S):
                    total = weight[a, 0] * v[0]
                    for b in range(1, a + 1):
                        total = total + weight[a, b] * v[b]
                    out_ref[(a, *place)] = total


def edge_kernel(res_ref, gain_ref, tail_ref, head_ref):
    for ref, start in ((tail_ref, 8), (head_ref, 0)):
        for f in range(FIELDS):
            ref[f] = res_ref[0, f, start : start + 8, :]
        ref[FIELDS] = gain_ref[0, start : start + 8, :]


def call(kernel, out_shape, in_specs, args, scratch=(), flops=10**6):
    shapes = jax.tree.map(lambda s: jax.ShapeDtypeStruct(s, jnp.float32), out_shape, is_leaf=lambda s: isinstance(s[0], int))
    return pl.pallas_call(
        kernel,
        out_shape=shapes,
        in_specs=in_specs,
        out_specs=jax.tree.map(lambda _: VMEM, shapes),
        scratch_shapes=scratch,
        compiler_params=pltpu.CompilerParams(vmem_limit_bytes=40 * 2**20),
        cost_estimate=pl.CostEstimate(flops=flops, transcendentals=0, bytes_accessed=2 * 10**6),
    )(*args)


def coupling_table():
    angles = np.pi * np.arange(1, 8) / INST
    return [float(c) for c in 0.5 * (-1.0) ** np.arange(1, 8) * np.cos(angles) / np.sin(angles)]


def on_device(residual, diag_gain, flux_jac, omega, shifts):
    ends = CELLS - 1
    tail, head = call(edge_kernel, ((STATE, 8, NC), (STATE, 8, NC)), [VMEM] * 2, (residual, diag_gain))
    below = lax.ppermute(tail, "cell", [(i, i + 1) for i in range(ends)])
    above = lax.ppermute(head, "cell", [(i + 1, i) for i in range(ends)])
    chunks = call(pack_kernel, (INST, STATE * 8, 128), [VMEM] * 4, (residual, diag_gain, below, above))
    patches = lax.all_to_all(chunks, "inst", 0, 0, tiled=True)
    vectors = call(
        functools.partial(step_kernel, rotations(coupling_table())),
        (INST, 80, 128),
        [VMEM, SMEM, SMEM, SMEM],
        (patches, flux_jac, omega, shifts),
        scratch=[
            pltpu.VMEM((S, INST, FIELDS, *TILE), jnp.float32),
            pltpu.VMEM((4 * FIELDS * FIELDS, *TILE), jnp.float32),
            pltpu.VMEM((INST, FIELDS, *TILE), jnp.float32),
            pltpu.VMEM((INST, *TILE), jnp.float32),
        ],
        flops=10**8,
    )
    back = lax.all_to_all(vectors, "inst", 0, 0, tiled=True)
    rows = lax.all_to_all(call(gram_kernel, (CELLS, 128), [VMEM], (back,)), "cell", 0, 0, tiled=True)
    others = call(unpack_kernel, (S - 1, 1, FIELDS, ROWS, NC), [VMEM], (back,))
    return call(
        finish_kernel, ((S, 1, FIELDS, ROWS, NC), (S, S)), [VMEM] * 3, (rows, residual, others)
    )


def solution(mesh):
    in_specs = (P("inst", None, "cell", None), P("inst", "cell", None), P(), P(), P())
    out_specs = (P(None, "inst", None, "cell", None), P())
    return jax.shard_map(
        on_device, mesh=mesh, in_specs=in_specs, out_specs=out_specs, check_vma=False
    )
```

```python
import functools

import jax
import jax.numpy as jnp
import numpy as np
from jax import lax
from jax.experimental import pallas as pl
from jax.experimental.pallas import tpu as pltpu
from jax.sharding import PartitionSpec as P

S = 8
FIELDS = 5
INST = 16
CELLS = 64
HALO = 8
ROWS = 16
COLS = 16
NC = 256
NR = 1024
STATE = FIELDS + 1
MEETING = [[(i + CELLS // 2) % CELLS for i in range(CELLS)]]
VMEM = pl.BlockSpec(memory_space=pltpu.VMEM)
SMEM = pl.BlockSpec(memory_space=pltpu.SMEM)
TILE = (8, 128)


def lanes():
    return lax.broadcasted_iota(jnp.int32, TILE, 1)


def sublanes():
    return lax.broadcasted_iota(jnp.int32, TILE, 0)


def two_sum(a, b):
    total = a + b
    part = total - a
    return total, (a - (total - part)) + (b - part)


def split(a):
    scaled = a * 4097.0
    high = scaled - (scaled - a)
    return high, a - high


def pack_kernel(res_ref, gain_ref, below_ref, above_ref, out_ref):
    lane = lanes()
    group = lane // 32
    for field in range(STATE):
        own = res_ref.at[0, field] if field < FIELDS else gain_ref.at[0]
        rows = [below_ref[field], own[0:8, :], own[8:16, :], above_ref[field]]
        chunks = [None] * INST
        for part in range(4):
            left, right = rows[part][:, :128], rows[part][:, 128:]
            for turn in range(8):
                shift = 16 * turn + 8
                rolled_left = pltpu.roll(left, shift, 1)
                rolled_right = pltpu.roll(right, shift, 1)
                first = lane < shift
                for turns, moved in (
                    (turn, jnp.where(first, rolled_right, rolled_left)),
                    (turn + 8, jnp.where(first, rolled_left, rolled_right)),
                ):
                    chunk = (2 * part - turns) % 16
                    old = chunks[chunk]
                    chunks[chunk] = moved if old is None else jnp.where(group == part, moved, old)
        for chunk in range(INST):
            out_ref[chunk, field * 8 : field * 8 + 8, :] = chunks[chunk]


def merge_pair(first, second, mask, shift, axis):
    high = [jnp.where(mask, second[0], first[0]), jnp.where(mask, first[0], second[0])]
    total, error = two_sum(high[0], pltpu.roll(high[1], shift, axis))
    if first[1] is None:
        return total, error
    low = jnp.where(mask, second[1], first[1]) + pltpu.roll(
        jnp.where(mask, first[1], second[1]), shift, axis
    )
    return total, error + low


def fold_pair(pair, shift, axis):
    total, error = two_sum(pair[0], pltpu.roll(pair[0], shift, axis))
    return total, error + (pair[1] + pltpu.roll(pair[1], shift, axis))


def rotations(table):
    c = [0.0, *table]
    plus = [None] + [c[d] - c[8 - d] for d in (1, 2, 3)]
    minus = [None] + [(c[d] + c[8 - d]) / 2 for d in (1, 2, 3, 4)]
    return ((plus[1] - plus[3]) / 4, (plus[1] + plus[3]) / 4, plus[2] / 2, *minus[1:])


def gap(x, i, d):
    n = len(x)
    before, after = x[(i - d) % n], x[(i + d) % n]
    if i - d < 0:
        return before + after, -1
    return (before - after if i + d < n else before + after), 1


def turned(x, i, weights):
    n = len(x)
    total = None
    for d, weight in enumerate(weights, 1):
        if 2 * d < n:
            value, sign = gap(x, i, d)
        else:
            value, sign = x[(i - d) % n], (1 if i >= d else -1)
        term = weight * value
        if total is None:
            total = term if sign > 0 else -term
        else:
            total = total + term if sign > 0 else total - term
    return total


def coupled(v, weights):
    inner, first, second = weights[:3]
    plus = [v[i] + v[i + 8] for i in range(8)]
    minus = [v[i] - v[i + 8] for i in range(8)]
    sums = [plus[i] + plus[i + 4] for i in range(4)]
    gaps = [plus[i] - plus[i + 4] for i in range(4)]
    even, odd = inner * (sums[3] - sums[1]), inner * (sums[0] - sums[2])
    circle = [even, odd, -even, -odd]
    twisted = [turned(gaps, i, (first, second)) for i in range(4)]
    outer = [circle[i] + twisted[i] for i in range(4)] + [circle[i] - twisted[i] for i in range(4)]
    flipped = [turned(minus, i, weights[3:]) for i in range(8)]
    return [outer[i] + flipped[i] for i in range(8)] + [outer[i] - flipped[i] for i in range(8)]


SLOTS = ((2, 4), (3, 5), (6, 0), (7, 1))
OFFSETS = (0, 1, 4, 5)
MOVES = {(0, 0): (0, 1, 4, 5), (1, 1): (0, 1, 4, 5), (0, 1): (0, 1, 3, 4, 5, 7)}


def in_slot(seg, q):
    return (seg == SLOTS[q][0]) | (seg == SLOTS[q][1])


def pack_four(seg, a, b, c, d):
    a, b, c, d = pltpu.roll(a, 120, 1), pltpu.roll(b, 8, 1), pltpu.roll(c, 56, 1), pltpu.roll(d, 72, 1)
    return jnp.where(in_slot(seg, 0), a, jnp.where(in_slot(seg, 1), b, jnp.where(in_slot(seg, 2), c, d)))


def step_kernel(rotation, in_ref, jac_ref, omega_ref, shift_ref, out_ref, vec_ref, coef_ref, mix_ref, gain_ref):
    lane, sub = lanes(), sublanes()
    seg = lane // 16
    cell, inst = lax.axis_index("cell"), lax.axis_index("inst")
    row = cell * ROWS - HALO + (lane // 32) * 8 + sub
    col = inst * COLS - HALO + lane % 32
    inside = (row >= 0) & (row < NR) & (col >= 0) & (col < NC)
    first_row, last_row = sub == 0, sub == 7
    for d in range(4):
        for f in range(FIELDS):
            for e in range(FIELDS):
                coef_ref[(d * FIELDS + f) * FIELDS + e] = jnp.full(TILE, jac_ref[d, f, e])
    for i in range(INST):
        for f in range(FIELDS):
            vec_ref[0, i, f] = jnp.where(inside, in_ref[i, f * 8 : f * 8 + 8, :], 0.0)
        gain_ref[i] = in_ref[i, FIELDS * 8 : FIELDS * 8 + 8, :]
    weights = [jnp.full(TILE, omega_ref[0] * w) for w in rotation]

    def step(n, carry):
        shift = shift_ref[n]
        for f in range(FIELDS):
            mixed = coupled([vec_ref[n, i, f] for i in range(INST)], weights)
            for i in range(INST):
                mix_ref[i, f] = mixed[i]
        for pair in range(0, INST, 2):
            members = (pair, pair + 1)
            near, center = {}, {}
            for i in members:
                for e in range(FIELDS):
                    v = vec_ref[n, i, e]
                    center[i, e] = v
                    down = pltpu.roll(v, 1, 0)
                    up = pltpu.roll(v, 7, 0)
                    near[i, 0, e] = jnp.where(first_row, pltpu.roll(down, 32, 1), down)
                    near[i, 1, e] = jnp.where(last_row, pltpu.roll(up, 96, 1), up)
                    near[i, 2, e] = pltpu.roll(v, 1, 1)
                    near[i, 3, e] = pltpu.roll(v, 127, 1)
            for f in range(FIELDS):
                total = {i: mix_ref[i, f] + (gain_ref[i] - shift) * center[i, f] for i in members}
                for d in range(4):
                    for e in range(FIELDS):
                        c = coef_ref[(d * FIELDS + f) * FIELDS + e]
                        for i in members:
                            total[i] = total[i] - c * near[i, d, e]
                for i in members:
                    vec_ref[n + 1, i, f] = jnp.where(inside, total[i], 0.0)
        return carry

    lax.fori_loop(0, S - 1, step, 0)

    keys = [(x, y, move) for (x, y), moves in MOVES.items() for move in moves]

    def gather(i, sums):
        sums = list(sums)
        tiles = {}
        for f in range(FIELDS):
            for x in range(2):
                tiles[x, f] = pack_four(seg, *[vec_ref[4 * x + q, i, f] for q in range(4)])
            moved = {}
            for p, (x, y, move) in enumerate(keys):
                if (y, move) not in moved:
                    moved[y, move] = pltpu.roll(tiles[y, f], 16 * move, 1) if move else tiles[y, f]
                sums[p] = sums[p] + tiles[x, f] * moved[y, move]
            out_ref[i, (4 + f) * 8 : (4 + f) * 8 + 8, :] = tiles[1, f]
        for f in range(4):
            tile = tiles[0, f]
            if f < 3:
                move = (OFFSETS[0] - OFFSETS[f + 1]) % 8
                tile = jnp.where(in_slot(seg, 0), pltpu.roll(tiles[0, 4], 16 * move, 1), tile)
            out_ref[i, f * 8 : f * 8 + 8, :] = tile
        return tuple(sums)

    sums = lax.fori_loop(0, INST, gather, tuple(jnp.zeros(TILE, jnp.float32) for _ in keys))
    entry = {}
    for p, (x, y, move) in enumerate(keys):
        for q in range(4):
            for r in range(4):
                a, b = 4 * x + q, 4 * y + r
                if (OFFSETS[q] - OFFSETS[r]) % 8 == move and (a, b) not in entry:
                    entry[a, b] = entry[b, a] = (jnp.where(in_slot(seg, q), sums[p], 0.0), None)
    columns = []
    for b in range(S):
        level = [entry[a, b] for a in range(S)]
        for bit in (1, 2, 4):
            mask = (sub & bit) != 0
            level = [merge_pair(level[2 * q], level[2 * q + 1], mask, bit, 0) for q in range(len(level) // 2)]
        columns.append(level[0])
    for bit in (1, 2, 4):
        mask = (lane & bit) != 0
        columns = [merge_pair(columns[2 * q], columns[2 * q + 1], mask, bit, 1) for q in range(len(columns) // 2)]
    high, low = fold_pair(columns[0], 64, 1)
    pair = jnp.where(lane < 64, high, low)
    for i in range(INST):
        out_ref[i, 72:80, :] = pair


def gram_kernel(in_ref, out_ref):
    lane, sub = lanes(), sublanes()
    total, error = sum_pairs([in_ref[i, 72:80, :] for i in range(INST)])
    lower = lane < 64
    other = pltpu.roll(total, 64, 1)
    low = jnp.where(lower, other, total) + jnp.where(lower, error, pltpu.roll(error, 64, 1))
    pair = (jnp.where(lower, total, other), low)
    for shift in (8, 16, 32):
        pair = fold_pair(pair, shift, 1)
    slot = lane // 8
    row = jnp.where(slot == sub, pair[0], jnp.where(slot == sub + 8, pair[1], 0.0))
    row = jnp.broadcast_to(jnp.sum(row, axis=0, keepdims=True), TILE)
    for q in range(CELLS // 8):
        out_ref[q * 8 : q * 8 + 8, :] = row


def sum_pairs(values):
    level = [(v, None) for v in values]
    while len(level) > 1:
        merged = []
        for q in range(0, len(level), 2):
            total, error = two_sum(level[q][0], level[q + 1][0])
            if level[q][1] is not None:
                error = error + (level[q][1] + level[q + 1][1])
            merged.append((total, error))
        level = merged
    return level[0]


def unpack_kernel(in_ref, out_ref):
    seg = lanes() // 16
    places = {}
    for q, segs in enumerate(SLOTS):
        for part in range(2):
            places[segs[part]] = (q, part)
    for tile in range(9):
        for wide in range(2):
            tiles = [in_ref[8 * wide + q, tile * 8 : tile * 8 + 8, :] for q in range(8)]
            for bit in (1, 2, 4):
                off = (seg & bit) == 0
                for q in range(8):
                    if q & bit:
                        continue
                    a, b = tiles[q], tiles[q + bit]
                    tiles[q] = jnp.where(off, a, pltpu.roll(b, 16 * bit, 1))
                    tiles[q + bit] = jnp.where(off, pltpu.roll(a, 128 - 16 * bit, 1), b)
            for q in range(8):
                s, part = places[q]
                if tile >= 4:
                    s, f = 4 + s, tile - 4
                elif s:
                    f = tile
                elif tile < 3:
                    s, f = tile + 1, 4
                else:
                    continue
                out_ref[s - 1, 0, f, 8 * part : 8 * part + 8, 128 * wide : 128 * wide + 128] = tiles[q]


TRIANGLE = [(i, j) for i in range(S) for j in range(i + 1)]


def inverse_of(lower, scale):
    inverse = {}
    for i in range(S):
        inverse[i, i] = scale[i]
        for j in range(i):
            total = lower[i, j] * inverse[j, j]
            for k in range(j + 1, i):
                total = total + lower[i, k] * inverse[k, j]
            inverse[i, j] = -(scale[i] * total)
    return inverse


def product_of(a, b):
    out = {}
    for i, j in TRIANGLE:
        total = a[i, j] * b[j, j]
        for k in range(j + 1, i + 1):
            total = total + a[i, k] * b[k, j]
        out[i, j] = total
    return out


def factor_pairs(high, low):
    lower, scale = {}, {}
    for k in range(S):
        full = {i: high[i, k] + low[i, k] for i in range(k, S)}
        scale[k] = lax.rsqrt(full[k])
        parts = {}
        for i in range(k, S):
            lower[i, k] = full[i] * scale[k]
            parts[i] = split(lower[i, k])
        for i in range(k, S):
            for j in range(k, i + 1):
                (a_high, a_low), (b_high, b_low) = parts[i], parts[j]
                product = lower[i, k] * lower[j, k]
                error = ((a_high * b_high - product) + a_high * b_low + a_low * b_high) + a_low * b_low
                high[i, j], rest = two_sum(high[i, j], -product)
                low[i, j] = low[i, j] + (rest - error)
    return lower, inverse_of(lower, scale), {at: high[at] + low[at] for at in TRIANGLE}


def factor_plain(matrix):
    lower, scale = {}, {}
    for k in range(S):
        scale[k] = lax.rsqrt(matrix[k, k])
        for i in range(k, S):
            lower[i, k] = matrix[i, k] * scale[k]
        for i in range(k + 1, S):
            for j in range(k + 1, i + 1):
                matrix[i, j] = matrix[i, j] - lower[i, k] * lower[j, k]
    return lower, inverse_of(lower, scale)


def finish_kernel(rows_ref, res_ref, vec_ref, out_ref, factor_ref):
    lane, sub = lanes(), sublanes()
    pair = sum_pairs([rows_ref[q * 8 : q * 8 + 8, :] for q in range(CELLS // 8)])
    for shift in (1, 2, 4):
        pair = fold_pair(pair, shift, 0)
    low_row = pair[1] + pltpu.roll(pair[0], 64, 1)
    high = {(i, j): jnp.broadcast_to(pair[0][:, 8 * i + j : 8 * i + j + 1], TILE) for i, j in TRIANGLE}
    low = {(i, j): jnp.broadcast_to(low_row[:, 8 * i + j : 8 * i + j + 1], TILE) for i, j in TRIANGLE}
    lower_one, inverse_one, rest = factor_pairs(high, low)
    half = {}
    for i in range(S):
        for j in range(i + 1):
            total = None
            for k in range(i + 1):
                term = inverse_one[i, k] * rest[max(k, j), min(k, j)]
                total = term if total is None else total + term
            half[i, j] = total
    square = {}
    for i, j in TRIANGLE:
        total = half[i, 0] * inverse_one[j, 0]
        for k in range(1, j + 1):
            total = total + half[i, k] * inverse_one[j, k]
        square[i, j] = total + 1.0 if i == j else total
    lower_two, inverse_two = factor_plain(square)
    lower = product_of(lower_one, lower_two)
    weight = product_of(inverse_two, inverse_one)
    block = jnp.zeros(TILE, jnp.float32)
    for i, j in TRIANGLE:
        block = jnp.where((sub == j) & (lane == i), lower[i, j], block)
    factor_ref[...] = block[:, :S]
    for f in range(FIELDS):
        for part in range(2):
            for wide in range(2):
                place = (0, f, pl.ds(8 * part, 8), pl.ds(128 * wide, 128))
                v = [res_ref[place]] + [vec_ref[(s, *place)] for s in range(S - 1)]
                for a in range(S):
                    total = weight[a, 0] * v[0]
                    for b in range(1, a + 1):
                        total = total + weight[a, b] * v[b]
                    out_ref[(a, *place)] = total


def edge_kernel(res_ref, gain_ref, tail_ref, head_ref):
    for ref, start in ((tail_ref, 8), (head_ref, 0)):
        for f in range(FIELDS):
            ref[f] = res_ref[0, f, start : start + 8, :]
        ref[FIELDS] = gain_ref[0, start : start + 8, :]


def call(kernel, out_shape, in_specs, args, scratch=(), flops=10**6):
    shapes = jax.tree.map(lambda s: jax.ShapeDtypeStruct(s, jnp.float32), out_shape, is_leaf=lambda s: isinstance(s[0], int))
    return pl.pallas_call(
        kernel,
        out_shape=shapes,
        in_specs=in_specs,
        out_specs=jax.tree.map(lambda _: VMEM, shapes),
        scratch_shapes=scratch,
        compiler_params=pltpu.CompilerParams(vmem_limit_bytes=40 * 2**20),
        cost_estimate=pl.CostEstimate(flops=flops, transcendentals=0, bytes_accessed=2 * 10**6),
    )(*args)


def coupling_table():
    angles = np.pi * np.arange(1, 8) / INST
    return [float(c) for c in 0.5 * (-1.0) ** np.arange(1, 8) * np.cos(angles) / np.sin(angles)]


def on_device(residual, diag_gain, flux_jac, omega, shifts):
    ends = CELLS - 1
    tail, head = call(edge_kernel, ((STATE, 8, NC), (STATE, 8, NC)), [VMEM] * 2, (residual, diag_gain))
    below = lax.ppermute(tail, "cell", [(i, i + 1) for i in range(ends)])
    above = lax.ppermute(head, "cell", [(i + 1, i) for i in range(ends)])
    chunks = call(pack_kernel, (INST, STATE * 8, 128), [VMEM] * 4, (residual, diag_gain, below, above))
    patches = lax.all_to_all(chunks, "inst", 0, 0, tiled=True)
    vectors = call(
        functools.partial(step_kernel, rotations(coupling_table())),
        (INST, 80, 128),
        [VMEM, SMEM, SMEM, SMEM],
        (patches, flux_jac, omega, shifts),
        scratch=[
            pltpu.VMEM((S, INST, FIELDS, *TILE), jnp.float32),
            pltpu.VMEM((4 * FIELDS * FIELDS, *TILE), jnp.float32),
            pltpu.VMEM((INST, FIELDS, *TILE), jnp.float32),
            pltpu.VMEM((INST, *TILE), jnp.float32),
        ],
        flops=10**8,
    )
    back = lax.all_to_all(vectors, "inst", 0, 0, tiled=True)
    row = call(gram_kernel, (CELLS, 128), [VMEM], (back,))
    rows = lax.all_to_all(row, "cell", 0, 0, axis_index_groups=MEETING, tiled=True)
    others = call(unpack_kernel, (S - 1, 1, FIELDS, ROWS, NC), [VMEM], (back,))
    return call(
        finish_kernel, ((S, 1, FIELDS, ROWS, NC), (S, S)), [VMEM] * 3, (rows, residual, others)
    )


def solution(mesh):
    in_specs = (P("inst", None, "cell", None), P("inst", "cell", None), P(), P(), P())
    out_specs = (P(None, "inst", None, "cell", None), P())
    return jax.shard_map(
        on_device, mesh=mesh, in_specs=in_specs, out_specs=out_specs, check_vma=False
    )
```

```python
import functools

import jax
import jax.numpy as jnp
import numpy as np
from jax import lax
from jax.experimental import pallas as pl
from jax.experimental.pallas import tpu as pltpu
from jax.sharding import PartitionSpec as P

S = 8
FIELDS = 5
INST = 16
CELLS = 64
HALO = 8
ROWS = 16
COLS = 16
NC = 256
NR = 1024
STATE = FIELDS + 1
MEETING = [[(i + CELLS // 2) % CELLS for i in range(CELLS)]]
VMEM = pl.BlockSpec(memory_space=pltpu.VMEM)
SMEM = pl.BlockSpec(memory_space=pltpu.SMEM)
TILE = (8, 128)


def lanes():
    return lax.broadcasted_iota(jnp.int32, TILE, 1)


def sublanes():
    return lax.broadcasted_iota(jnp.int32, TILE, 0)


def two_sum(a, b):
    total = a + b
    part = total - a
    return total, (a - (total - part)) + (b - part)


def split(a):
    scaled = a * 4097.0
    high = scaled - (scaled - a)
    return high, a - high


def pack_kernel(res_ref, gain_ref, below_ref, above_ref, out_ref):
    lane = lanes()
    group, place = lane // 32, lane % 32
    for field in range(STATE):
        own = res_ref.at[0, field] if field < FIELDS else gain_ref.at[0]
        rows = [below_ref[field], own[0:8, :], own[8:16, :], above_ref[field]]
        for parity in range(2):
            moved = []
            for part in range(4):
                shift = (32 * part + HALO - COLS * parity) % 128
                moved.append([pltpu.roll(rows[part][:, 128 * h : 128 * h + 128], shift, 1) for h in range(2)])
            for inst in range(parity, INST, 2):
                chunk = None
                for part in range(4):
                    left, right = moved[part]
                    piece = left if inst < 8 else right
                    if inst in (7, 8):
                        piece = jnp.where(place < (24 if inst == 7 else 8), left, right)
                    chunk = piece if chunk is None else jnp.where(group == (part + inst // 2) % 4, piece, chunk)
                out_ref[inst, field * 8 : field * 8 + 8, :] = chunk


def merge_pair(first, second, mask, shift, axis):
    high = [jnp.where(mask, second[0], first[0]), jnp.where(mask, first[0], second[0])]
    total, error = two_sum(high[0], pltpu.roll(high[1], shift, axis))
    if first[1] is None:
        return total, error
    low = jnp.where(mask, second[1], first[1]) + pltpu.roll(
        jnp.where(mask, first[1], second[1]), shift, axis
    )
    return total, error + low


def fold_pair(pair, shift, axis):
    total, error = two_sum(pair[0], pltpu.roll(pair[0], shift, axis))
    return total, error + (pair[1] + pltpu.roll(pair[1], shift, axis))


def rotations(table):
    c = [0.0, *table]
    plus = [None] + [c[d] - c[8 - d] for d in (1, 2, 3)]
    minus = [None] + [(c[d] + c[8 - d]) / 2 for d in (1, 2, 3, 4)]
    return ((plus[1] - plus[3]) / 4, (plus[1] + plus[3]) / 4, plus[2] / 2, *minus[1:])


def gap(x, i, d):
    n = len(x)
    before, after = x[(i - d) % n], x[(i + d) % n]
    if i - d < 0:
        return before + after, -1
    return (before - after if i + d < n else before + after), 1


def turned(x, i, weights):
    n = len(x)
    total = None
    for d, weight in enumerate(weights, 1):
        if 2 * d < n:
            value, sign = gap(x, i, d)
        else:
            value, sign = x[(i - d) % n], (1 if i >= d else -1)
        term = weight * value
        if total is None:
            total = term if sign > 0 else -term
        else:
            total = total + term if sign > 0 else total - term
    return total


def coupled(v, weights):
    inner, first, second = weights[:3]
    plus = [v[i] + v[i + 8] for i in range(8)]
    minus = [v[i] - v[i + 8] for i in range(8)]
    sums = [plus[i] + plus[i + 4] for i in range(4)]
    gaps = [plus[i] - plus[i + 4] for i in range(4)]
    even, odd = inner * (sums[3] - sums[1]), inner * (sums[0] - sums[2])
    circle = [even, odd, -even, -odd]
    twisted = [turned(gaps, i, (first, second)) for i in range(4)]
    outer = [circle[i] + twisted[i] for i in range(4)] + [circle[i] - twisted[i] for i in range(4)]
    flipped = [turned(minus, i, weights[3:]) for i in range(8)]
    return [outer[i] + flipped[i] for i in range(8)] + [outer[i] - flipped[i] for i in range(8)]


SLOTS = ((2, 4), (3, 5), (6, 0), (7, 1))
SLOT_MOVES = (0, 16, 64, 80)


def segments():
    return ((lanes() + 128 - HALO) % 128) // 16


def in_slot(seg, q):
    return (seg == SLOTS[q][0]) | (seg == SLOTS[q][1])


TILES = INST * FIELDS
PITCH = 16


def tile_at(i, f):
    return PITCH * (i * FIELDS + f) + 8


def step_kernel(rotation, in_ref, jac_ref, omega_ref, shift_ref, out_ref, vec_ref, coef_ref, mix_ref, gain_ref, slot_ref):
    lane, sub = lanes(), sublanes()
    seg = segments()
    cell, inst = lax.axis_index("cell"), lax.axis_index("inst")
    turn = lax.rem(inst // 2, 4)
    part = (lane // 32 + 4 - turn) % 4
    row = cell * ROWS - HALO + part * 8 + sub
    col = inst * COLS - HALO + lane % 32
    inside = (row >= 0) & (row < NR) & (col >= 0) & (col < NC)
    for d in range(4):
        for f in range(FIELDS):
            for e in range(FIELDS):
                coef_ref[(d * FIELDS + f) * FIELDS + e] = jnp.full(TILE, jac_ref[d, f, e])
    for i in range(INST):
        for f in range(FIELDS):
            vec_ref[0, pl.ds(tile_at(i, f), 8), :] = jnp.where(inside, in_ref[i, f * 8 : f * 8 + 8, :], 0.0)
        gain_ref[i] = in_ref[i, FIELDS * 8 : FIELDS * 8 + 8, :]
    weights = [jnp.full(TILE, omega_ref[0] * w) for w in rotation]

    def step(n, carry):
        shift = shift_ref[n]
        slot = lax.rem(n, 4)
        aligned = lax.rem(lax.rem(slot, 2) * 16 + (slot // 2) * 64 + 128 - 32 * turn, 128)
        now, later = vec_ref.at[n], vec_ref.at[n + 1]
        for group in range(TILES // 8):
            start = PITCH * 8 * group
            last = now[pl.ds(start + 15, 8, stride=PITCH), :]
            now[pl.ds(start + 7, 8, stride=PITCH), :] = pltpu.roll(last, 32, 1)
            first = now[pl.ds(start + 8, 8, stride=PITCH), :]
            now[pl.ds(start + 16, 8, stride=PITCH), :] = pltpu.roll(first, 96, 1)
        for f in range(FIELDS):
            mixed = coupled([now[pl.ds(tile_at(i, f), 8), :] for i in range(INST)], weights)
            for i in range(INST):
                mix_ref[i, f] = mixed[i]
        for pair in range(0, INST, 2):
            members = (pair, pair + 1)
            near, center, gain = {}, {}, {}
            for i in members:
                gain[i] = gain_ref[i] - shift
                for e in range(FIELDS):
                    at = tile_at(i, e)
                    v = now[pl.ds(at, 8), :]
                    center[i, e] = v
                    slot_ref[n, i, e] = pltpu.roll(v, aligned, 1)
                    near[i, 0, e] = now[pl.ds(at - 1, 8), :]
                    near[i, 1, e] = now[pl.ds(at + 1, 8), :]
                    near[i, 2, e] = pltpu.roll(v, 1, 1)
                    near[i, 3, e] = pltpu.roll(v, 127, 1)
            for f in range(FIELDS):
                total = {i: mix_ref[i, f] + gain[i] * center[i, f] for i in members}
                for d in range(4):
                    for e in range(FIELDS):
                        c = coef_ref[(d * FIELDS + f) * FIELDS + e]
                        for i in members:
                            total[i] = total[i] - c * near[i, d, e]
                for i in members:
                    later[pl.ds(tile_at(i, f), 8), :] = jnp.where(inside, total[i], 0.0)
        return carry

    lax.fori_loop(0, S - 1, step, 0)

    pairs = [(a, b) for a in range(S) for b in range(a, S)]
    last_move = lax.rem(SLOT_MOVES[3] + 128 - 32 * turn, 128)

    def gather(quarter, sums):
        sums = list(sums)
        for i in [quarter * 4 + q for q in range(4)]:
            tiles = {}
            for f in range(FIELDS):
                at = pl.multiple_of(PITCH * FIELDS * i + tile_at(0, f), 8)
                v = [vec_ref[s, pl.ds(at, 8), :] for s in range(S)]
                for p, (a, b) in enumerate(pairs):
                    sums[p] = sums[p] + v[a] * v[b]
                moved = [slot_ref[s, i, f] for s in range(S - 1)] + [pltpu.roll(v[S - 1], last_move, 1)]
                for x in range(2):
                    a, b, c, d = moved[4 * x : 4 * x + 4]
                    tiles[x, f] = jnp.where(
                        in_slot(seg, 0), a, jnp.where(in_slot(seg, 1), b, jnp.where(in_slot(seg, 2), c, d))
                    )
                out_ref[i, (4 + f) * 8 : (4 + f) * 8 + 8, :] = tiles[1, f]
            for f in range(4):
                tile = tiles[0, f]
                if f < 3:
                    move = (SLOT_MOVES[0] - SLOT_MOVES[f + 1]) % 128
                    tile = jnp.where(in_slot(seg, 0), pltpu.roll(tiles[0, 4], move, 1), tile)
                out_ref[i, f * 8 : f * 8 + 8, :] = tile
        return tuple(sums)

    sums = lax.fori_loop(0, INST // 4, gather, tuple(jnp.zeros(TILE, jnp.float32) for _ in pairs))
    column = lane % 32
    own = ((part == 1) | (part == 2)) & (column >= HALO) & (column < HALO + COLS)
    entry = {}
    for p, (a, b) in enumerate(pairs):
        entry[a, b] = entry[b, a] = (jnp.where(own, sums[p], 0.0), None)
    columns = []
    for b in range(S):
        level = [entry[a, b] for a in range(S)]
        for bit in (1, 2, 4):
            mask = (sub & bit) != 0
            level = [merge_pair(level[2 * q], level[2 * q + 1], mask, bit, 0) for q in range(len(level) // 2)]
        columns.append(level[0])
    for bit in (1, 2, 4):
        mask = (lane & bit) != 0
        columns = [merge_pair(columns[2 * q], columns[2 * q + 1], mask, bit, 1) for q in range(len(columns) // 2)]
    high, low = fold_pair(columns[0], 64, 1)
    pair = jnp.where(lane < 64, high, low)
    for i in range(INST):
        out_ref[i, 72:80, :] = pair


def gram_kernel(in_ref, out_ref):
    lane, sub = lanes(), sublanes()
    total, error = sum_pairs([in_ref[i, 72:80, :] for i in range(INST)])
    lower = lane < 64
    other = pltpu.roll(total, 64, 1)
    low = jnp.where(lower, other, total) + jnp.where(lower, error, pltpu.roll(error, 64, 1))
    pair = (jnp.where(lower, total, other), low)
    for shift in (8, 16, 32):
        pair = fold_pair(pair, shift, 1)
    slot = lane // 8
    row = jnp.where(slot == sub, pair[0], jnp.where(slot == sub + 8, pair[1], 0.0))
    row = jnp.broadcast_to(jnp.sum(row, axis=0, keepdims=True), TILE)
    for q in range(CELLS // 8):
        out_ref[q * 8 : q * 8 + 8, :] = row


def sum_pairs(values):
    level = [(v, None) for v in values]
    while len(level) > 1:
        merged = []
        for q in range(0, len(level), 2):
            total, error = two_sum(level[q][0], level[q + 1][0])
            if level[q][1] is not None:
                error = error + (level[q][1] + level[q + 1][1])
            merged.append((total, error))
        level = merged
    return level[0]


def unpack_kernel(in_ref, out_ref):
    seg = lanes() // 16
    places = {}
    for q, segs in enumerate(SLOTS):
        for part in range(2):
            places[segs[part]] = (q, part)
    for tile in range(9):
        for wide in range(2):
            tiles = [pltpu.roll(in_ref[8 * wide + q, tile * 8 : tile * 8 + 8, :], 128 - HALO, 1) for q in range(8)]
            for bit in (1, 2, 4):
                off = (seg & bit) == 0
                for q in range(8):
                    if q & bit:
                        continue
                    a, b = tiles[q], tiles[q + bit]
                    tiles[q] = jnp.where(off, a, pltpu.roll(b, 16 * bit, 1))
                    tiles[q + bit] = jnp.where(off, pltpu.roll(a, 128 - 16 * bit, 1), b)
            for q in range(8):
                s, part = places[q]
                if tile >= 4:
                    s, f = 4 + s, tile - 4
                elif s:
                    f = tile
                elif tile < 3:
                    s, f = tile + 1, 4
                else:
                    continue
                out_ref[s - 1, 0, f, 8 * part : 8 * part + 8, 128 * wide : 128 * wide + 128] = tiles[q]


TRIANGLE = [(i, j) for i in range(S) for j in range(i + 1)]


def inverse_of(lower, scale):
    inverse = {}
    for i in range(S):
        inverse[i, i] = scale[i]
        for j in range(i):
            total = lower[i, j] * inverse[j, j]
            for k in range(j + 1, i):
                total = total + lower[i, k] * inverse[k, j]
            inverse[i, j] = -(scale[i] * total)
    return inverse


def product_of(a, b):
    out = {}
    for i, j in TRIANGLE:
        total = a[i, j] * b[j, j]
        for k in range(j + 1, i + 1):
            total = total + a[i, k] * b[k, j]
        out[i, j] = total
    return out


def factor_pairs(high, low):
    lower, scale = {}, {}
    for k in range(S):
        full = {i: high[i, k] + low[i, k] for i in range(k, S)}
        scale[k] = lax.rsqrt(full[k])
        parts = {}
        for i in range(k, S):
            lower[i, k] = full[i] * scale[k]
            parts[i] = split(lower[i, k])
        for i in range(k, S):
            for j in range(k, i + 1):
                (a_high, a_low), (b_high, b_low) = parts[i], parts[j]
                product = lower[i, k] * lower[j, k]
                error = ((a_high * b_high - product) + a_high * b_low + a_low * b_high) + a_low * b_low
                high[i, j], rest = two_sum(high[i, j], -product)
                low[i, j] = low[i, j] + (rest - error)
    return lower, inverse_of(lower, scale), {at: high[at] + low[at] for at in TRIANGLE}


def factor_plain(matrix):
    lower, scale = {}, {}
    for k in range(S):
        scale[k] = lax.rsqrt(matrix[k, k])
        for i in range(k, S):
            lower[i, k] = matrix[i, k] * scale[k]
        for i in range(k + 1, S):
            for j in range(k + 1, i + 1):
                matrix[i, j] = matrix[i, j] - lower[i, k] * lower[j, k]
    return lower, inverse_of(lower, scale)


def finish_kernel(rows_ref, res_ref, vec_ref, out_ref, factor_ref):
    lane, sub = lanes(), sublanes()
    pair = sum_pairs([rows_ref[q * 8 : q * 8 + 8, :] for q in range(CELLS // 8)])
    for shift in (1, 2, 4):
        pair = fold_pair(pair, shift, 0)
    low_row = pair[1] + pltpu.roll(pair[0], 64, 1)
    high = {(i, j): jnp.broadcast_to(pair[0][:, 8 * i + j : 8 * i + j + 1], TILE) for i, j in TRIANGLE}
    low = {(i, j): jnp.broadcast_to(low_row[:, 8 * i + j : 8 * i + j + 1], TILE) for i, j in TRIANGLE}
    lower_one, inverse_one, rest = factor_pairs(high, low)
    half = {}
    for i in range(S):
        for j in range(i + 1):
            total = None
            for k in range(i + 1):
                term = inverse_one[i, k] * rest[max(k, j), min(k, j)]
                total = term if total is None else total + term
            half[i, j] = total
    square = {}
    for i, j in TRIANGLE:
        total = half[i, 0] * inverse_one[j, 0]
        for k in range(1, j + 1):
            total = total + half[i, k] * inverse_one[j, k]
        square[i, j] = total + 1.0 if i == j else total
    lower_two, inverse_two = factor_plain(square)
    lower = product_of(lower_one, lower_two)
    weight = product_of(inverse_two, inverse_one)
    block = jnp.zeros(TILE, jnp.float32)
    for i, j in TRIANGLE:
        block = jnp.where((sub == j) & (lane == i), lower[i, j], block)
    factor_ref[...] = block[:, :S]
    for f in range(FIELDS):
        for part in range(2):
            for wide in range(2):
                place = (0, f, pl.ds(8 * part, 8), pl.ds(128 * wide, 128))
                v = [res_ref[place]] + [vec_ref[(s, *place)] for s in range(S - 1)]
                for a in range(S):
                    total = weight[a, 0] * v[0]
                    for b in range(1, a + 1):
                        total = total + weight[a, b] * v[b]
                    out_ref[(a, *place)] = total


def edge_kernel(res_ref, gain_ref, tail_ref, head_ref, sems):
    copies = []
    for ref, start in ((tail_ref, 8), (head_ref, 0)):
        rows = pl.ds(start, 8)
        for source, target in ((res_ref.at[0, :, rows, :], ref.at[pl.ds(0, FIELDS)]), (gain_ref.at[:, rows, :], ref.at[pl.ds(FIELDS, 1)])):
            copies.append(pltpu.make_async_copy(source, target, sems.at[len(copies)]))
    for copy in copies:
        copy.start()
    for copy in copies:
        copy.wait()


def call(kernel, out_shape, in_specs, args, scratch=(), flops=10**6):
    shapes = jax.tree.map(lambda s: jax.ShapeDtypeStruct(s, jnp.float32), out_shape, is_leaf=lambda s: isinstance(s[0], int))
    return pl.pallas_call(
        kernel,
        out_shape=shapes,
        in_specs=in_specs,
        out_specs=jax.tree.map(lambda _: VMEM, shapes),
        scratch_shapes=scratch,
        compiler_params=pltpu.CompilerParams(vmem_limit_bytes=40 * 2**20),
        cost_estimate=pl.CostEstimate(flops=flops, transcendentals=0, bytes_accessed=2 * 10**6),
    )(*args)


def coupling_table():
    angles = np.pi * np.arange(1, 8) / INST
    return [float(c) for c in 0.5 * (-1.0) ** np.arange(1, 8) * np.cos(angles) / np.sin(angles)]


def on_device(residual, diag_gain, flux_jac, omega, shifts):
    ends = CELLS - 1
    tail, head = call(
        edge_kernel,
        ((STATE, 8, NC), (STATE, 8, NC)),
        [pl.BlockSpec(memory_space=pl.ANY)] * 2,
        (residual, diag_gain),
        scratch=[pltpu.SemaphoreType.DMA((4,))],
    )
    below = lax.ppermute(tail, "cell", [(i, i + 1) for i in range(ends)])
    above = lax.ppermute(head, "cell", [(i + 1, i) for i in range(ends)])
    chunks = call(pack_kernel, (INST, STATE * 8, 128), [VMEM] * 4, (residual, diag_gain, below, above))
    patches = lax.all_to_all(chunks, "inst", 0, 0, tiled=True)
    vectors = call(
        functools.partial(step_kernel, rotations(coupling_table())),
        (INST, 80, 128),
        [VMEM, SMEM, SMEM, SMEM],
        (patches, flux_jac, omega, shifts),
        scratch=[
            pltpu.VMEM((S, PITCH * (TILES + 1), 128), jnp.float32),
            pltpu.VMEM((4 * FIELDS * FIELDS, *TILE), jnp.float32),
            pltpu.VMEM((INST, FIELDS, *TILE), jnp.float32),
            pltpu.VMEM((INST, *TILE), jnp.float32),
            pltpu.VMEM((S - 1, INST, FIELDS, *TILE), jnp.float32),
        ],
        flops=10**8,
    )
    back = lax.all_to_all(vectors, "inst", 0, 0, tiled=True)
    row = call(gram_kernel, (CELLS, 128), [VMEM], (back,))
    rows = lax.all_to_all(row, "cell", 0, 0, axis_index_groups=MEETING, tiled=True)
    others = call(unpack_kernel, (S - 1, 1, FIELDS, ROWS, NC), [VMEM], (back,))
    return call(
        finish_kernel, ((S, 1, FIELDS, ROWS, NC), (S, S)), [VMEM] * 3, (rows, residual, others)
    )


def solution(mesh):
    in_specs = (P("inst", None, "cell", None), P("inst", "cell", None), P(), P(), P())
    out_specs = (P(None, "inst", None, "cell", None), P())
    return jax.shard_map(
        on_device, mesh=mesh, in_specs=in_specs, out_specs=out_specs, check_vma=False
    )
```

```python
import functools

import jax
import jax.numpy as jnp
import numpy as np
from jax import lax
from jax.experimental import pallas as pl
from jax.experimental.pallas import tpu as pltpu
from jax.sharding import PartitionSpec as P

S = 8
FIELDS = 5
INST = 16
CELLS = 64
HALO = 8
ROWS = 16
COLS = 16
NC = 256
NR = 1024
STATE = FIELDS + 1
MEETING = [[(i + CELLS // 2) % CELLS for i in range(CELLS)]]
VMEM = pl.BlockSpec(memory_space=pltpu.VMEM)
SMEM = pl.BlockSpec(memory_space=pltpu.SMEM)
TILE = (8, 128)


def lanes():
    return lax.broadcasted_iota(jnp.int32, TILE, 1)


def sublanes():
    return lax.broadcasted_iota(jnp.int32, TILE, 0)


def two_sum(a, b):
    total = a + b
    part = total - a
    return total, (a - (total - part)) + (b - part)


def split(a):
    scaled = a * 4097.0
    high = scaled - (scaled - a)
    return high, a - high


def pack_kernel(res_ref, gain_ref, below_ref, above_ref, out_ref):
    lane = lanes()
    group, place = lane // 32, lane % 32
    for field in range(STATE):
        own = res_ref.at[0, field] if field < FIELDS else gain_ref.at[0]
        rows = [below_ref[field], own[0:8, :], own[8:16, :], above_ref[field]]
        for parity in range(2):
            moved = []
            for part in range(4):
                shift = (32 * part + HALO - COLS * parity) % 128
                moved.append([pltpu.roll(rows[part][:, 128 * h : 128 * h + 128], shift, 1) for h in range(2)])
            for inst in range(parity, INST, 2):
                chunk = None
                for part in range(4):
                    left, right = moved[part]
                    piece = left if inst < 8 else right
                    if inst in (7, 8):
                        piece = jnp.where(place < (24 if inst == 7 else 8), left, right)
                    chunk = piece if chunk is None else jnp.where(group == (part + inst // 2) % 4, piece, chunk)
                out_ref[inst, field * 8 : field * 8 + 8, :] = chunk


def merge_pair(first, second, mask, shift, axis):
    high = [jnp.where(mask, second[0], first[0]), jnp.where(mask, first[0], second[0])]
    total, error = two_sum(high[0], pltpu.roll(high[1], shift, axis))
    if first[1] is None:
        return total, error
    low = jnp.where(mask, second[1], first[1]) + pltpu.roll(
        jnp.where(mask, first[1], second[1]), shift, axis
    )
    return total, error + low


def fold_pair(pair, shift, axis):
    total, error = two_sum(pair[0], pltpu.roll(pair[0], shift, axis))
    return total, error + (pair[1] + pltpu.roll(pair[1], shift, axis))


def rotations(table):
    c = [0.0, *table]
    plus = [None] + [c[d] - c[8 - d] for d in (1, 2, 3)]
    minus = [None] + [(c[d] + c[8 - d]) / 2 for d in (1, 2, 3, 4)]
    return ((plus[1] - plus[3]) / 4, (plus[1] + plus[3]) / 4, plus[2] / 2, *minus[1:])


def gap(x, i, d):
    n = len(x)
    before, after = x[(i - d) % n], x[(i + d) % n]
    if i - d < 0:
        return before + after, -1
    return (before - after if i + d < n else before + after), 1


def turned(x, i, weights):
    n = len(x)
    total = None
    for d, weight in enumerate(weights, 1):
        if 2 * d < n:
            value, sign = gap(x, i, d)
        else:
            value, sign = x[(i - d) % n], (1 if i >= d else -1)
        term = weight * value
        if total is None:
            total = term if sign > 0 else -term
        else:
            total = total + term if sign > 0 else total - term
    return total


def coupled(v, weights):
    inner, first, second = weights[:3]
    plus = [v[i] + v[i + 8] for i in range(8)]
    minus = [v[i] - v[i + 8] for i in range(8)]
    sums = [plus[i] + plus[i + 4] for i in range(4)]
    gaps = [plus[i] - plus[i + 4] for i in range(4)]
    even, odd = inner * (sums[3] - sums[1]), inner * (sums[0] - sums[2])
    circle = [even, odd, -even, -odd]
    twisted = [turned(gaps, i, (first, second)) for i in range(4)]
    outer = [circle[i] + twisted[i] for i in range(4)] + [circle[i] - twisted[i] for i in range(4)]
    flipped = [turned(minus, i, weights[3:]) for i in range(8)]
    return [outer[i] + flipped[i] for i in range(8)] + [outer[i] - flipped[i] for i in range(8)]


SLOTS = ((2, 4), (3, 5), (6, 0), (7, 1))
SLOT_MOVES = (0, 16, 64, 80)


def segments():
    return ((lanes() + 128 - HALO) % 128) // 16


def in_slot(seg, q):
    return (seg == SLOTS[q][0]) | (seg == SLOTS[q][1])


TILES = INST * FIELDS
PITCH = 16


def tile_at(i, f):
    return PITCH * (i * FIELDS + f) + 8


def step_kernel(rotation, in_ref, jac_ref, omega_ref, shift_ref, out_ref, vec_ref, coef_ref, mix_ref, gain_ref, slot_ref):
    lane, sub = lanes(), sublanes()
    seg = segments()
    cell, inst = lax.axis_index("cell"), lax.axis_index("inst")
    turn = lax.rem(inst // 2, 4)
    part = (lane // 32 + 4 - turn) % 4
    row = cell * ROWS - HALO + part * 8 + sub
    col = inst * COLS - HALO + lane % 32
    inside = (row >= 0) & (row < NR) & (col >= 0) & (col < NC)
    for d in range(4):
        for f in range(FIELDS):
            for e in range(FIELDS):
                coef_ref[(d * FIELDS + f) * FIELDS + e] = jnp.full(TILE, jac_ref[d, f, e])
    for i in range(INST):
        for f in range(FIELDS):
            vec_ref[0, pl.ds(tile_at(i, f), 8), :] = jnp.where(inside, in_ref[i, f * 8 : f * 8 + 8, :], 0.0)
        gain_ref[i] = in_ref[i, FIELDS * 8 : FIELDS * 8 + 8, :]
    weights = [jnp.full(TILE, omega_ref[0] * w) for w in rotation]

    def step(n, carry):
        shift = shift_ref[n]
        slot = lax.rem(n, 4)
        aligned = lax.rem(lax.rem(slot, 2) * 16 + (slot // 2) * 64 + 128 - 32 * turn, 128)
        now, later = vec_ref.at[n], vec_ref.at[n + 1]
        for group in range(TILES // 8):
            start = PITCH * 8 * group
            last = now[pl.ds(start + 15, 8, stride=PITCH), :]
            now[pl.ds(start + 7, 8, stride=PITCH), :] = pltpu.roll(last, 32, 1)
            first = now[pl.ds(start + 8, 8, stride=PITCH), :]
            now[pl.ds(start + 16, 8, stride=PITCH), :] = pltpu.roll(first, 96, 1)
        for f in range(FIELDS):
            mixed = coupled([now[pl.ds(tile_at(i, f), 8), :] for i in range(INST)], weights)
            for i in range(INST):
                mix_ref[i, f] = mixed[i]
        for pair in range(0, INST, 2):
            members = (pair, pair + 1)
            near, center, gain = {}, {}, {}
            for i in members:
                gain[i] = gain_ref[i] - shift
                for e in range(FIELDS):
                    at = tile_at(i, e)
                    v = now[pl.ds(at, 8), :]
                    center[i, e] = v
                    slot_ref[n, i, e] = pltpu.roll(v, aligned, 1)
                    near[i, 0, e] = now[pl.ds(at - 1, 8), :]
                    near[i, 1, e] = now[pl.ds(at + 1, 8), :]
                    near[i, 2, e] = pltpu.roll(v, 1, 1)
                    near[i, 3, e] = pltpu.roll(v, 127, 1)
            for f in range(FIELDS):
                total = {i: mix_ref[i, f] + gain[i] * center[i, f] for i in members}
                for d in range(4):
                    for e in range(FIELDS):
                        c = coef_ref[(d * FIELDS + f) * FIELDS + e]
                        for i in members:
                            total[i] = total[i] - c * near[i, d, e]
                for i in members:
                    later[pl.ds(tile_at(i, f), 8), :] = jnp.where(inside, total[i], 0.0)
        return carry

    lax.fori_loop(0, S - 1, step, 0)

    packed = {}
    for x, y in ((0, 0), (1, 1), (0, 1)):
        for half in range(2):
            packed[x, y, half] = [(4 * x + q, 4 * y + (q + 2 * half) % 4, q) for q in range(4)]
    covered = {(min(a, b), max(a, b)) for entries in packed.values() for a, b, _ in entries}
    plain = [(a, b) for a in range(S) for b in range(a, S) if (a, b) not in covered]
    last_move = lax.rem(SLOT_MOVES[3] + 128 - 32 * turn, 128)

    def gather(quarter, sums):
        sums = list(sums)
        for i in [quarter * 4 + q for q in range(4)]:
            tiles = {}
            for f in range(FIELDS):
                at = pl.multiple_of(PITCH * FIELDS * i + tile_at(0, f), 8)
                v = [vec_ref[s, pl.ds(at, 8), :] for s in range(S)]
                moved = [slot_ref[s, i, f] for s in range(S - 1)] + [pltpu.roll(v[S - 1], last_move, 1)]
                for x in range(2):
                    a, b, c, d = moved[4 * x : 4 * x + 4]
                    tiles[x, f] = jnp.where(
                        in_slot(seg, 0), a, jnp.where(in_slot(seg, 1), b, jnp.where(in_slot(seg, 2), c, d))
                    )
                turned_tiles = [pltpu.roll(tiles[x, f], 64, 1) for x in range(2)]
                for p, (a, b) in enumerate(plain):
                    sums[p] = sums[p] + v[a] * v[b]
                for p, (x, y, half) in enumerate(packed, len(plain)):
                    sums[p] = sums[p] + tiles[x, f] * (turned_tiles[y] if half else tiles[y, f])
                out_ref[i, (4 + f) * 8 : (4 + f) * 8 + 8, :] = tiles[1, f]
            for f in range(4):
                tile = tiles[0, f]
                if f < 3:
                    move = (SLOT_MOVES[0] - SLOT_MOVES[f + 1]) % 128
                    tile = jnp.where(in_slot(seg, 0), pltpu.roll(tiles[0, 4], move, 1), tile)
                out_ref[i, f * 8 : f * 8 + 8, :] = tile
        return tuple(sums)

    start = tuple(jnp.zeros(TILE, jnp.float32) for _ in range(len(plain) + len(packed)))
    sums = lax.fori_loop(0, INST // 4, gather, start)
    column = lane % 32
    own = ((part == 1) | (part == 2)) & (column >= HALO) & (column < HALO + COLS)
    entry = {}
    for p, (a, b) in enumerate(plain):
        entry[a, b] = entry[b, a] = (jnp.where(own, sums[p], 0.0), None)
    for p, entries in enumerate(packed.values(), len(plain)):
        for a, b, q in entries:
            if (a, b) not in entry:
                entry[a, b] = entry[b, a] = (jnp.where(in_slot(seg, q), sums[p], 0.0), None)
    columns = []
    for b in range(S):
        level = [entry[a, b] for a in range(S)]
        for bit in (1, 2, 4):
            mask = (sub & bit) != 0
            level = [merge_pair(level[2 * q], level[2 * q + 1], mask, bit, 0) for q in range(len(level) // 2)]
        columns.append(level[0])
    for bit in (1, 2, 4):
        mask = (lane & bit) != 0
        columns = [merge_pair(columns[2 * q], columns[2 * q + 1], mask, bit, 1) for q in range(len(columns) // 2)]
    high, low = fold_pair(columns[0], 64, 1)
    pair = jnp.where(lane < 64, high, low)
    for i in range(INST):
        out_ref[i, 72:80, :] = pair


def gram_kernel(in_ref, out_ref):
    lane, sub = lanes(), sublanes()
    total, error = sum_pairs([in_ref[i, 72:80, :] for i in range(INST)])
    lower = lane < 64
    other = pltpu.roll(total, 64, 1)
    low = jnp.where(lower, other, total) + jnp.where(lower, error, pltpu.roll(error, 64, 1))
    pair = (jnp.where(lower, total, other), low)
    for shift in (8, 16, 32):
        pair = fold_pair(pair, shift, 1)
    slot = lane // 8
    row = jnp.where(slot == sub, pair[0], jnp.where(slot == sub + 8, pair[1], 0.0))
    row = jnp.broadcast_to(jnp.sum(row, axis=0, keepdims=True), TILE)
    for q in range(CELLS // 8):
        out_ref[q * 8 : q * 8 + 8, :] = row


def sum_pairs(values):
    level = [(v, None) for v in values]
    while len(level) > 1:
        merged = []
        for q in range(0, len(level), 2):
            total, error = two_sum(level[q][0], level[q + 1][0])
            if level[q][1] is not None:
                error = error + (level[q][1] + level[q + 1][1])
            merged.append((total, error))
        level = merged
    return level[0]


def unpack_kernel(in_ref, out_ref):
    seg = lanes() // 16
    places = {}
    for q, segs in enumerate(SLOTS):
        for part in range(2):
            places[segs[part]] = (q, part)
    for tile in range(9):
        for wide in range(2):
            tiles = [pltpu.roll(in_ref[8 * wide + q, tile * 8 : tile * 8 + 8, :], 128 - HALO, 1) for q in range(8)]
            for bit in (1, 2, 4):
                off = (seg & bit) == 0
                for q in range(8):
                    if q & bit:
                        continue
                    a, b = tiles[q], tiles[q + bit]
                    tiles[q] = jnp.where(off, a, pltpu.roll(b, 16 * bit, 1))
                    tiles[q + bit] = jnp.where(off, pltpu.roll(a, 128 - 16 * bit, 1), b)
            for q in range(8):
                s, part = places[q]
                if tile >= 4:
                    s, f = 4 + s, tile - 4
                elif s:
                    f = tile
                elif tile < 3:
                    s, f = tile + 1, 4
                else:
                    continue
                out_ref[s - 1, 0, f, 8 * part : 8 * part + 8, 128 * wide : 128 * wide + 128] = tiles[q]


TRIANGLE = [(i, j) for i in range(S) for j in range(i + 1)]


def inverse_of(lower, scale):
    inverse = {}
    for i in range(S):
        inverse[i, i] = scale[i]
        for j in range(i):
            total = lower[i, j] * inverse[j, j]
            for k in range(j + 1, i):
                total = total + lower[i, k] * inverse[k, j]
            inverse[i, j] = -(scale[i] * total)
    return inverse


def product_of(a, b):
    out = {}
    for i, j in TRIANGLE:
        total = a[i, j] * b[j, j]
        for k in range(j + 1, i + 1):
            total = total + a[i, k] * b[k, j]
        out[i, j] = total
    return out


def factor_pairs(high, low):
    lower, scale = {}, {}
    for k in range(S):
        full = {i: high[i, k] + low[i, k] for i in range(k, S)}
        scale[k] = lax.rsqrt(full[k])
        parts = {}
        for i in range(k, S):
            lower[i, k] = full[i] * scale[k]
            parts[i] = split(lower[i, k])
        for i in range(k, S):
            for j in range(k, i + 1):
                (a_high, a_low), (b_high, b_low) = parts[i], parts[j]
                high[i, j], rest = two_sum(high[i, j], -(a_high * b_high))
                low[i, j] = low[i, j] + (rest - (a_high * b_low + a_low * lower[j, k]))
    return lower, inverse_of(lower, scale), {at: high[at] + low[at] for at in TRIANGLE}


def factor_plain(matrix):
    lower, scale = {}, {}
    for k in range(S):
        scale[k] = lax.rsqrt(matrix[k, k])
        for i in range(k, S):
            lower[i, k] = matrix[i, k] * scale[k]
        for i in range(k + 1, S):
            for j in range(k + 1, i + 1):
                matrix[i, j] = matrix[i, j] - lower[i, k] * lower[j, k]
    return lower, inverse_of(lower, scale)


def finish_kernel(rows_ref, res_ref, vec_ref, out_ref, factor_ref):
    lane, sub = lanes(), sublanes()
    pair = sum_pairs([rows_ref[q * 8 : q * 8 + 8, :] for q in range(CELLS // 8)])
    for shift in (1, 2, 4):
        pair = fold_pair(pair, shift, 0)
    low_row = pair[1] + pltpu.roll(pair[0], 64, 1)
    high = {(i, j): jnp.broadcast_to(pair[0][:, 8 * i + j : 8 * i + j + 1], TILE) for i, j in TRIANGLE}
    low = {(i, j): jnp.broadcast_to(low_row[:, 8 * i + j : 8 * i + j + 1], TILE) for i, j in TRIANGLE}
    lower_one, inverse_one, rest = factor_pairs(high, low)
    half = {}
    for i in range(S):
        for j in range(i + 1):
            total = None
            for k in range(i + 1):
                term = inverse_one[i, k] * rest[max(k, j), min(k, j)]
                total = term if total is None else total + term
            half[i, j] = total
    square = {}
    for i, j in TRIANGLE:
        total = half[i, 0] * inverse_one[j, 0]
        for k in range(1, j + 1):
            total = total + half[i, k] * inverse_one[j, k]
        square[i, j] = total + 1.0 if i == j else total
    lower_two, inverse_two = factor_plain(square)
    lower = product_of(lower_one, lower_two)
    weight = product_of(inverse_two, inverse_one)
    block = jnp.zeros(TILE, jnp.float32)
    for i, j in TRIANGLE:
        block = jnp.where((sub == j) & (lane == i), lower[i, j], block)
    factor_ref[...] = block[:, :S]
    for f in range(FIELDS):
        for part in range(2):
            for wide in range(2):
                place = (0, f, pl.ds(8 * part, 8), pl.ds(128 * wide, 128))
                v = [res_ref[place]] + [vec_ref[(s, *place)] for s in range(S - 1)]
                for a in range(S):
                    total = weight[a, 0] * v[0]
                    for b in range(1, a + 1):
                        total = total + weight[a, b] * v[b]
                    out_ref[(a, *place)] = total


def edge_kernel(res_ref, gain_ref, tail_ref, head_ref, sems):
    copies = []
    for ref, start in ((tail_ref, 8), (head_ref, 0)):
        rows = pl.ds(start, 8)
        for source, target in ((res_ref.at[0, :, rows, :], ref.at[pl.ds(0, FIELDS)]), (gain_ref.at[:, rows, :], ref.at[pl.ds(FIELDS, 1)])):
            copies.append(pltpu.make_async_copy(source, target, sems.at[len(copies)]))
    for copy in copies:
        copy.start()
    for copy in copies:
        copy.wait()


def call(kernel, out_shape, in_specs, args, scratch=(), flops=10**6):
    shapes = jax.tree.map(lambda s: jax.ShapeDtypeStruct(s, jnp.float32), out_shape, is_leaf=lambda s: isinstance(s[0], int))
    return pl.pallas_call(
        kernel,
        out_shape=shapes,
        in_specs=in_specs,
        out_specs=jax.tree.map(lambda _: VMEM, shapes),
        scratch_shapes=scratch,
        compiler_params=pltpu.CompilerParams(vmem_limit_bytes=40 * 2**20),
        cost_estimate=pl.CostEstimate(flops=flops, transcendentals=0, bytes_accessed=2 * 10**6),
    )(*args)


def coupling_table():
    angles = np.pi * np.arange(1, 8) / INST
    return [float(c) for c in 0.5 * (-1.0) ** np.arange(1, 8) * np.cos(angles) / np.sin(angles)]


def on_device(residual, diag_gain, flux_jac, omega, shifts):
    ends = CELLS - 1
    tail, head = call(
        edge_kernel,
        ((STATE, 8, NC), (STATE, 8, NC)),
        [pl.BlockSpec(memory_space=pltpu.HBM)] * 2,
        [pltpu.with_memory_space_constraint(x, pltpu.HBM) for x in (residual, diag_gain)],
        scratch=[pltpu.SemaphoreType.DMA((4,))],
    )
    below = lax.ppermute(tail, "cell", [(i, i + 1) for i in range(ends)])
    above = lax.ppermute(head, "cell", [(i + 1, i) for i in range(ends)])
    chunks = call(pack_kernel, (INST, STATE * 8, 128), [VMEM] * 4, (residual, diag_gain, below, above))
    patches = lax.all_to_all(chunks, "inst", 0, 0, tiled=True)
    vectors = call(
        functools.partial(step_kernel, rotations(coupling_table())),
        (INST, 80, 128),
        [VMEM, SMEM, SMEM, SMEM],
        (patches, flux_jac, omega, shifts),
        scratch=[
            pltpu.VMEM((S, PITCH * (TILES + 1), 128), jnp.float32),
            pltpu.VMEM((4 * FIELDS * FIELDS, *TILE), jnp.float32),
            pltpu.VMEM((INST, FIELDS, *TILE), jnp.float32),
            pltpu.VMEM((INST, *TILE), jnp.float32),
            pltpu.VMEM((S - 1, INST, FIELDS, *TILE), jnp.float32),
        ],
        flops=10**8,
    )
    back = lax.all_to_all(vectors, "inst", 0, 0, tiled=True)
    row = call(gram_kernel, (CELLS, 128), [VMEM], (back,))
    rows = lax.all_to_all(row, "cell", 0, 0, axis_index_groups=MEETING, tiled=True)
    others = call(unpack_kernel, (S - 1, 1, FIELDS, ROWS, NC), [VMEM], (back,))
    return call(
        finish_kernel, ((S, 1, FIELDS, ROWS, NC), (S, S)), [VMEM] * 3, (rows, residual, others)
    )


def solution(mesh):
    in_specs = (P("inst", None, "cell", None), P("inst", "cell", None), P(), P(), P())
    out_specs = (P(None, "inst", None, "cell", None), P())
    return jax.shard_map(
        on_device, mesh=mesh, in_specs=in_specs, out_specs=out_specs, check_vma=False
    )
```

```python
import functools

import jax
import jax.numpy as jnp
import numpy as np
from jax import lax
from jax.experimental import pallas as pl
from jax.experimental.pallas import tpu as pltpu
from jax.sharding import PartitionSpec as P

S = 8
FIELDS = 5
INST = 16
CELLS = 64
HALO = 8
ROWS = 16
COLS = 16
NC = 256
NR = 1024
STATE = FIELDS + 1
MEETING = [[(i + CELLS // 2) % CELLS for i in range(CELLS)]]
VMEM = pl.BlockSpec(memory_space=pltpu.VMEM)
SMEM = pl.BlockSpec(memory_space=pltpu.SMEM)
HBM = pl.BlockSpec(memory_space=pltpu.HBM)
TILE = (8, 128)


def lanes():
    return lax.broadcasted_iota(jnp.int32, TILE, 1)


def sublanes():
    return lax.broadcasted_iota(jnp.int32, TILE, 0)


def two_sum(a, b):
    total = a + b
    part = total - a
    return total, (a - (total - part)) + (b - part)


def split(a):
    scaled = a * 4097.0
    high = scaled - (scaled - a)
    return high, a - high


def pack_kernel(res_ref, gain_ref, near_ref, far_ref, jac_ref, omega_ref, shift_ref, out_ref, coef_ref):
    lane = lanes()
    first = lax.rem(lax.axis_index("cell"), 2) == 0
    numbers = [jac_ref[d, f, e] for d in range(4) for f in range(FIELDS) for e in range(FIELDS)]
    numbers += [shift_ref[n] for n in range(S - 1)] + [omega_ref[0]]
    for at, number in enumerate(numbers):
        coef_ref[at : at + 1, :] = jnp.full((1, 128), number)
    group, place = lane // 32, lane % 32
    for field in range(STATE):
        own = res_ref.at[0, field] if field < FIELDS else gain_ref.at[0]
        below = jnp.where(first, far_ref[field], near_ref[field])
        above = jnp.where(first, near_ref[field], far_ref[field])
        rows = [below, own[0:8, :], own[8:16, :], above]
        for parity in range(2):
            moved = []
            for part in range(4):
                shift = (32 * part + HALO - COLS * parity) % 128
                moved.append([pltpu.roll(rows[part][:, 128 * h : 128 * h + 128], shift, 1) for h in range(2)])
            for inst in range(parity, INST, 2):
                chunk = None
                for part in range(4):
                    left, right = moved[part]
                    piece = left if inst < 8 else right
                    if inst in (7, 8):
                        piece = jnp.where(place < (24 if inst == 7 else 8), left, right)
                    chunk = piece if chunk is None else jnp.where(group == (part + inst // 2) % 4, piece, chunk)
                out_ref[inst, field * 8 : field * 8 + 8, :] = chunk


def merge_pair(first, second, mask, shift, axis):
    high = [jnp.where(mask, second[0], first[0]), jnp.where(mask, first[0], second[0])]
    total, error = two_sum(high[0], pltpu.roll(high[1], shift, axis))
    if first[1] is None:
        return total, error
    low = jnp.where(mask, second[1], first[1]) + pltpu.roll(
        jnp.where(mask, first[1], second[1]), shift, axis
    )
    return total, error + low


def fold_pair(pair, shift, axis):
    total, error = two_sum(pair[0], pltpu.roll(pair[0], shift, axis))
    return total, error + (pair[1] + pltpu.roll(pair[1], shift, axis))


def rotations(table):
    c = [0.0, *table]
    plus = [None] + [c[d] - c[8 - d] for d in (1, 2, 3)]
    minus = [None] + [(c[d] + c[8 - d]) / 2 for d in (1, 2, 3, 4)]
    return ((plus[1] - plus[3]) / 4, (plus[1] + plus[3]) / 4, plus[2] / 2, *minus[1:])


def gap(x, i, d):
    n = len(x)
    before, after = x[(i - d) % n], x[(i + d) % n]
    if i - d < 0:
        return before + after, -1
    return (before - after if i + d < n else before + after), 1


def turned(x, i, weights):
    n = len(x)
    total = None
    for d, weight in enumerate(weights, 1):
        if 2 * d < n:
            value, sign = gap(x, i, d)
        else:
            value, sign = x[(i - d) % n], (1 if i >= d else -1)
        term = weight * value
        if total is None:
            total = term if sign > 0 else -term
        else:
            total = total + term if sign > 0 else total - term
    return total


def coupled(v, weights):
    inner, first, second = weights[:3]
    plus = [v[i] + v[i + 8] for i in range(8)]
    minus = [v[i] - v[i + 8] for i in range(8)]
    sums = [plus[i] + plus[i + 4] for i in range(4)]
    gaps = [plus[i] - plus[i + 4] for i in range(4)]
    even, odd = inner * (sums[3] - sums[1]), inner * (sums[0] - sums[2])
    circle = [even, odd, -even, -odd]
    twisted = [turned(gaps, i, (first, second)) for i in range(4)]
    outer = [circle[i] + twisted[i] for i in range(4)] + [circle[i] - twisted[i] for i in range(4)]
    flipped = [turned(minus, i, weights[3:]) for i in range(8)]
    return [outer[i] + flipped[i] for i in range(8)] + [outer[i] - flipped[i] for i in range(8)]


SLOTS = ((2, 4), (3, 5), (6, 0), (7, 1))
SLOT_MOVES = (0, 16, 64, 80)


def segments():
    return ((lanes() + 128 - HALO) % 128) // 16


def in_slot(seg, q):
    return (seg == SLOTS[q][0]) | (seg == SLOTS[q][1])


TILES = INST * FIELDS
JAC = 4 * FIELDS * FIELDS
PITCH = 16


def tile_at(i, f):
    return PITCH * (i * FIELDS + f) + 8


def step_kernel(rotation, in_ref, number_ref, out_ref, vec_ref, coef_ref, mix_ref, gain_ref, slot_ref):
    lane, sub = lanes(), sublanes()
    seg = segments()
    cell, inst = lax.axis_index("cell"), lax.axis_index("inst")
    turn = lax.rem(inst // 2, 4)
    part = (lane // 32 + 4 - turn) % 4
    row = cell * ROWS - HALO + part * 8 + sub
    col = inst * COLS - HALO + lane % 32
    inside = (row >= 0) & (row < NR) & (col >= 0) & (col < NC)
    for at in range(JAC):
        coef_ref[at] = jnp.broadcast_to(number_ref[at : at + 1, :], TILE)
    for i in range(INST):
        for f in range(FIELDS):
            vec_ref[0, pl.ds(tile_at(i, f), 8), :] = jnp.where(inside, in_ref[i, f * 8 : f * 8 + 8, :], 0.0)
        gain_ref[i] = in_ref[i, FIELDS * 8 : FIELDS * 8 + 8, :]
    omega = jnp.broadcast_to(number_ref[JAC + S - 1 : JAC + S, :], TILE)
    weights = [omega * w for w in rotation]

    def step(n, carry):
        shift = jnp.broadcast_to(number_ref[pl.ds(JAC + n, 1), :], TILE)
        slot = lax.rem(n, 4)
        aligned = lax.rem(lax.rem(slot, 2) * 16 + (slot // 2) * 64 + 128 - 32 * turn, 128)
        now, later = vec_ref.at[n], vec_ref.at[n + 1]
        for group in range(TILES // 8):
            start = PITCH * 8 * group
            last = now[pl.ds(start + 15, 8, stride=PITCH), :]
            now[pl.ds(start + 7, 8, stride=PITCH), :] = pltpu.roll(last, 32, 1)
            first = now[pl.ds(start + 8, 8, stride=PITCH), :]
            now[pl.ds(start + 16, 8, stride=PITCH), :] = pltpu.roll(first, 96, 1)
        for f in range(FIELDS):
            mixed = coupled([now[pl.ds(tile_at(i, f), 8), :] for i in range(INST)], weights)
            for i in range(INST):
                mix_ref[i, f] = mixed[i]
        for pair in range(0, INST, 2):
            members = (pair, pair + 1)
            near, center, gain = {}, {}, {}
            for i in members:
                gain[i] = gain_ref[i] - shift
                for e in range(FIELDS):
                    at = tile_at(i, e)
                    v = now[pl.ds(at, 8), :]
                    center[i, e] = v
                    slot_ref[n, i, e] = pltpu.roll(v, aligned, 1)
                    near[i, 0, e] = now[pl.ds(at - 1, 8), :]
                    near[i, 1, e] = now[pl.ds(at + 1, 8), :]
                    near[i, 2, e] = pltpu.roll(v, 1, 1)
                    near[i, 3, e] = pltpu.roll(v, 127, 1)
            for f in range(FIELDS):
                total = {i: mix_ref[i, f] + gain[i] * center[i, f] for i in members}
                for d in range(4):
                    for e in range(FIELDS):
                        c = coef_ref[(d * FIELDS + f) * FIELDS + e]
                        for i in members:
                            total[i] = total[i] - c * near[i, d, e]
                for i in members:
                    later[pl.ds(tile_at(i, f), 8), :] = jnp.where(inside, total[i], 0.0)
        return carry

    lax.fori_loop(0, S - 1, step, 0)

    packed = {}
    for x, y in ((0, 0), (1, 1), (0, 1)):
        for half in range(2):
            packed[x, y, half] = [(4 * x + q, 4 * y + (q + 2 * half) % 4, q) for q in range(4)]
    covered = {(min(a, b), max(a, b)) for entries in packed.values() for a, b, _ in entries}
    plain = [(a, b) for a in range(S) for b in range(a, S) if (a, b) not in covered]
    last_move = lax.rem(SLOT_MOVES[3] + 128 - 32 * turn, 128)

    def gather(quarter, sums):
        sums = list(sums)
        for i in [quarter * 4 + q for q in range(4)]:
            tiles = {}
            for f in range(FIELDS):
                at = pl.multiple_of(PITCH * FIELDS * i + tile_at(0, f), 8)
                v = [vec_ref[s, pl.ds(at, 8), :] for s in range(S)]
                moved = [slot_ref[s, i, f] for s in range(S - 1)] + [pltpu.roll(v[S - 1], last_move, 1)]
                for x in range(2):
                    a, b, c, d = moved[4 * x : 4 * x + 4]
                    tiles[x, f] = jnp.where(
                        in_slot(seg, 0), a, jnp.where(in_slot(seg, 1), b, jnp.where(in_slot(seg, 2), c, d))
                    )
                turned_tiles = [pltpu.roll(tiles[x, f], 64, 1) for x in range(2)]
                for p, (a, b) in enumerate(plain):
                    sums[p] = sums[p] + v[a] * v[b]
                for p, (x, y, half) in enumerate(packed, len(plain)):
                    sums[p] = sums[p] + tiles[x, f] * (turned_tiles[y] if half else tiles[y, f])
                out_ref[i, (4 + f) * 8 : (4 + f) * 8 + 8, :] = tiles[1, f]
            for f in range(4):
                tile = tiles[0, f]
                if f < 3:
                    move = (SLOT_MOVES[0] - SLOT_MOVES[f + 1]) % 128
                    tile = jnp.where(in_slot(seg, 0), pltpu.roll(tiles[0, 4], move, 1), tile)
                out_ref[i, f * 8 : f * 8 + 8, :] = tile
        return tuple(sums)

    start = tuple(jnp.zeros(TILE, jnp.float32) for _ in range(len(plain) + len(packed)))
    sums = lax.fori_loop(0, INST // 4, gather, start)
    column = lane % 32
    own = ((part == 1) | (part == 2)) & (column >= HALO) & (column < HALO + COLS)
    entry = {}
    for p, (a, b) in enumerate(plain):
        entry[a, b] = entry[b, a] = (jnp.where(own, sums[p], 0.0), None)
    for p, entries in enumerate(packed.values(), len(plain)):
        for a, b, q in entries:
            if (a, b) not in entry:
                entry[a, b] = entry[b, a] = (jnp.where(in_slot(seg, q), sums[p], 0.0), None)
    columns = []
    for b in range(S):
        level = [entry[a, b] for a in range(S)]
        for bit in (1, 2, 4):
            mask = (sub & bit) != 0
            level = [merge_pair(level[2 * q], level[2 * q + 1], mask, bit, 0) for q in range(len(level) // 2)]
        columns.append(level[0])
    for bit in (1, 2, 4):
        mask = (lane & bit) != 0
        columns = [merge_pair(columns[2 * q], columns[2 * q + 1], mask, bit, 1) for q in range(len(columns) // 2)]
    pair = columns[0]
    for shift in (64, 32, 16):
        pair = fold_pair(pair, shift, 1)
    pair = jnp.where(seg == SLOTS[0][0], pair[0], pair[1])
    for i in range(INST):
        out_ref[i, 24:32, :] = jnp.where(in_slot(seg, 0), pair, out_ref[i, 24:32, :])


def gram_kernel(in_ref, out_ref):
    lane, sub = lanes(), sublanes()
    total, error = sum_pairs([in_ref[i, 24:32, :] for i in range(INST)])
    high, low = fold_pair((total, error + pltpu.roll(total, 96, 1)), 8, 1)
    here = (lane >= 48) & (lane < 56)
    both = jnp.where(here, high, 0.0) + pltpu.roll(jnp.where(here, low, 0.0), 8, 1)
    for shift in (16, 32, 64):
        both = both + pltpu.roll(both, shift, 1)
    row = jnp.where(lane // 16 == sub, both, 0.0)
    row = jnp.broadcast_to(jnp.sum(row, axis=0, keepdims=True), TILE)
    for q in range(CELLS // 8):
        out_ref[q * 8 : q * 8 + 8, :] = row


def sum_pairs(values):
    level = [(v, None) for v in values]
    while len(level) > 1:
        merged = []
        for q in range(0, len(level), 2):
            total, error = two_sum(level[q][0], level[q + 1][0])
            if level[q][1] is not None:
                error = error + (level[q][1] + level[q + 1][1])
            merged.append((total, error))
        level = merged
    return level[0]


def unpack_kernel(in_ref, out_ref):
    seg = lanes() // 16
    places = {}
    for q, segs in enumerate(SLOTS):
        for part in range(2):
            places[segs[part]] = (q, part)
    for tile in range(9):
        for wide in range(2):
            tiles = [pltpu.roll(in_ref[8 * wide + q, tile * 8 : tile * 8 + 8, :], 128 - HALO, 1) for q in range(8)]
            for bit in (1, 2, 4):
                off = (seg & bit) == 0
                for q in range(8):
                    if q & bit:
                        continue
                    a, b = tiles[q], tiles[q + bit]
                    tiles[q] = jnp.where(off, a, pltpu.roll(b, 16 * bit, 1))
                    tiles[q + bit] = jnp.where(off, pltpu.roll(a, 128 - 16 * bit, 1), b)
            for q in range(8):
                s, part = places[q]
                if tile >= 4:
                    s, f = 4 + s, tile - 4
                elif s:
                    f = tile
                elif tile < 3:
                    s, f = tile + 1, 4
                else:
                    continue
                out_ref[s - 1, 0, f, 8 * part : 8 * part + 8, 128 * wide : 128 * wide + 128] = tiles[q]


TRIANGLE = [(i, j) for i in range(S) for j in range(i + 1)]


def inverse_of(lower, scale):
    inverse = {}
    for i in range(S):
        inverse[i, i] = scale[i]
        for j in range(i):
            total = lower[i, j] * inverse[j, j]
            for k in range(j + 1, i):
                total = total + lower[i, k] * inverse[k, j]
            inverse[i, j] = -(scale[i] * total)
    return inverse


def product_of(a, b):
    out = {}
    for i, j in TRIANGLE:
        total = a[i, j] * b[j, j]
        for k in range(j + 1, i + 1):
            total = total + a[i, k] * b[k, j]
        out[i, j] = total
    return out


def factor_pairs(high, low):
    lower, scale = {}, {}
    for k in range(S):
        full = {i: high[i, k] + low[i, k] for i in range(k, S)}
        scale[k] = lax.rsqrt(full[k])
        parts = {}
        for i in range(k, S):
            lower[i, k] = full[i] * scale[k]
            parts[i] = split(lower[i, k])
        for i in range(k, S):
            for j in range(k, i + 1):
                (a_high, a_low), (b_high, b_low) = parts[i], parts[j]
                high[i, j], rest = two_sum(high[i, j], -(a_high * b_high))
                low[i, j] = low[i, j] + (rest - (a_high * b_low + a_low * lower[j, k]))
    return lower, inverse_of(lower, scale), {at: high[at] + low[at] for at in TRIANGLE}


def factor_plain(matrix):
    lower, scale = {}, {}
    for k in range(S):
        scale[k] = lax.rsqrt(matrix[k, k])
        for i in range(k, S):
            lower[i, k] = matrix[i, k] * scale[k]
        for i in range(k + 1, S):
            for j in range(k + 1, i + 1):
                matrix[i, j] = matrix[i, j] - lower[i, k] * lower[j, k]
    return lower, inverse_of(lower, scale)


def finish_kernel(rows_ref, res_ref, vec_ref, out_ref, factor_ref, done_ref, sems):
    lane, sub = lanes(), sublanes()
    pair = sum_pairs([rows_ref[q * 8 : q * 8 + 8, :] for q in range(CELLS // 8)])
    for shift in (1, 2, 4):
        pair = fold_pair(pair, shift, 0)
    low_row = pair[1] + pltpu.roll(pair[0], 128 - S, 1)
    high = {(i, j): jnp.broadcast_to(pair[0][:, 16 * i + j : 16 * i + j + 1], TILE) for i, j in TRIANGLE}
    low = {(i, j): jnp.broadcast_to(low_row[:, 16 * i + j : 16 * i + j + 1], TILE) for i, j in TRIANGLE}
    lower_one, inverse_one, rest = factor_pairs(high, low)
    half = {}
    for i in range(S):
        for j in range(i + 1):
            total = None
            for k in range(i + 1):
                term = inverse_one[i, k] * rest[max(k, j), min(k, j)]
                total = term if total is None else total + term
            half[i, j] = total
    square = {}
    for i, j in TRIANGLE:
        total = half[i, 0] * inverse_one[j, 0]
        for k in range(1, j + 1):
            total = total + half[i, k] * inverse_one[j, k]
        square[i, j] = total + 1.0 if i == j else total
    lower_two, inverse_two = factor_plain(square)
    lower = product_of(lower_one, lower_two)
    weight = product_of(inverse_two, inverse_one)
    block = jnp.zeros(TILE, jnp.float32)
    for i, j in TRIANGLE:
        block = jnp.where((sub == j) & (lane == i), lower[i, j], block)
    factor_ref[...] = block[:, :S]
    copies = [pltpu.make_async_copy(done_ref.at[:, :, f], out_ref.at[:, :, f], sems.at[f]) for f in range(FIELDS)]
    for f in range(FIELDS):
        for part in range(2):
            for wide in range(2):
                place = (0, f, pl.ds(8 * part, 8), pl.ds(128 * wide, 128))
                v = [res_ref[place]] + [vec_ref[(s, *place)] for s in range(S - 1)]
                for a in range(S):
                    total = weight[a, 0] * v[0]
                    for b in range(1, a + 1):
                        total = total + weight[a, b] * v[b]
                    done_ref[(a, *place)] = total
        copies[f].start()
    for copy in copies:
        copy.wait()


def edge_kernel(res_ref, gain_ref, near_ref, far_ref, sems):
    odd = lax.rem(lax.axis_index("cell"), 2)
    copies = []
    for ref, start in ((near_ref, 8 * (1 - odd)), (far_ref, 8 * odd)):
        rows = pl.ds(pl.multiple_of(start, 8), 8)
        for source, target in ((res_ref.at[0, :, rows, :], ref.at[pl.ds(0, FIELDS)]), (gain_ref.at[:, rows, :], ref.at[pl.ds(FIELDS, 1)])):
            copies.append(pltpu.make_async_copy(source, target, sems.at[len(copies)]))
    for copy in copies:
        copy.start()
    for copy in copies:
        copy.wait()


def call(kernel, out_shape, in_specs, args, scratch=(), flops=10**6, out_specs=None):
    shapes = jax.tree.map(lambda s: jax.ShapeDtypeStruct(s, jnp.float32), out_shape, is_leaf=lambda s: isinstance(s[0], int))
    return pl.pallas_call(
        kernel,
        out_shape=shapes,
        in_specs=in_specs,
        out_specs=out_specs or jax.tree.map(lambda _: VMEM, shapes),
        scratch_shapes=scratch,
        compiler_params=pltpu.CompilerParams(vmem_limit_bytes=40 * 2**20),
        cost_estimate=pl.CostEstimate(flops=flops, transcendentals=0, bytes_accessed=2 * 10**6),
    )(*args)


def coupling_table():
    angles = np.pi * np.arange(1, 8) / INST
    return [float(c) for c in 0.5 * (-1.0) ** np.arange(1, 8) * np.cos(angles) / np.sin(angles)]


def on_device(residual, diag_gain, flux_jac, omega, shifts):
    pairs = [(i, i + 1) for i in range(CELLS - 1)]
    pairs = [pairs[0::2], pairs[1::2]]
    near, far = call(
        edge_kernel,
        ((STATE, 8, NC), (STATE, 8, NC)),
        [HBM] * 2,
        [pltpu.with_memory_space_constraint(x, pltpu.HBM) for x in (residual, diag_gain)],
        scratch=[pltpu.SemaphoreType.DMA((4,))],
    )
    near, far = [
        lax.ppermute(x, "cell", p + [(b, a) for a, b in p]) for x, p in zip((near, far), pairs)
    ]
    chunks, numbers = call(
        pack_kernel,
        ((INST, STATE * 8, 128), (JAC + 12, 128)),
        [VMEM] * 4 + [SMEM] * 3,
        (residual, diag_gain, near, far, flux_jac, omega, shifts),
    )
    patches = lax.all_to_all(chunks, "inst", 0, 0, tiled=True)
    vectors = call(
        functools.partial(step_kernel, rotations(coupling_table())),
        (INST, 72, 128),
        [VMEM, VMEM],
        (patches, numbers),
        scratch=[
            pltpu.VMEM((S, PITCH * (TILES + 1), 128), jnp.float32),
            pltpu.VMEM((4 * FIELDS * FIELDS, *TILE), jnp.float32),
            pltpu.VMEM((INST, FIELDS, *TILE), jnp.float32),
            pltpu.VMEM((INST, *TILE), jnp.float32),
            pltpu.VMEM((S - 1, INST, FIELDS, *TILE), jnp.float32),
        ],
        flops=10**8,
    )
    back = lax.all_to_all(vectors, "inst", 0, 0, tiled=True)
    row = call(gram_kernel, (CELLS, 128), [VMEM], (back,))
    rows = lax.all_to_all(row, "cell", 0, 0, axis_index_groups=MEETING, tiled=True)
    others = call(unpack_kernel, (S - 1, 1, FIELDS, ROWS, NC), [VMEM], (back,))
    return call(
        finish_kernel,
        ((S, 1, FIELDS, ROWS, NC), (S, S)),
        [VMEM] * 3,
        (rows, residual, others),
        scratch=[pltpu.VMEM((S, 1, FIELDS, ROWS, NC), jnp.float32), pltpu.SemaphoreType.DMA((FIELDS,))],
        out_specs=(HBM, VMEM),
    )


def solution(mesh):
    in_specs = (P("inst", None, "cell", None), P("inst", "cell", None), P(), P(), P())
    out_specs = (P(None, "inst", None, "cell", None), P())
    return jax.shard_map(
        on_device, mesh=mesh, in_specs=in_specs, out_specs=out_specs, check_vma=False
    )
```

```python
import functools

import jax
import jax.numpy as jnp
import numpy as np
from jax import lax
from jax.experimental import pallas as pl
from jax.experimental.pallas import tpu as pltpu
from jax.sharding import PartitionSpec as P


S = 8
FIELDS = 5
INST = 16
CELLS = 64
HALO = 8
ROWS = 16
COLS = 16
NC = 256
NR = 1024
STATE = FIELDS + 1
MEETING = [[(i + CELLS // 2) % CELLS for i in range(CELLS)]]
VMEM = pl.BlockSpec(memory_space=pltpu.VMEM)
HBM = pl.BlockSpec(memory_space=pltpu.HBM)
TILE = (8, 128)
JAC = 4 * FIELDS * FIELDS
NUMBERS = JAC + S - 1 + 7


def lanes():
    return lax.broadcasted_iota(jnp.int32, TILE, 1)


def sublanes():
    return lax.broadcasted_iota(jnp.int32, TILE, 0)


def two_sum(a, b):
    total = a + b
    part = total - a
    return total, (a - (total - part)) + (b - part)


def split(a):
    scaled = a * 4097.0
    high = scaled - (scaled - a)
    return high, a - high


def pack_kernel(rotation, res_ref, gain_ref, near_ref, far_ref, jac_ref, scalar_ref, out_ref, coef_ref):
    lane = lanes()
    first = lax.rem(lax.axis_index("cell"), 2) == 0
    group, place = lane // 32, lane % 32
    for f in range(FIELDS):
        for e in range(FIELDS):
            at = 4 * (f * FIELDS + e)
            coef_ref[at : at + 4, :] = jnp.broadcast_to(jac_ref[f, :, e : e + 1], (4, 128))
    for n in range(S - 1):
        coef_ref[JAC + n : JAC + n + 1, :] = jnp.broadcast_to(scalar_ref[:, n : n + 1], (1, 128))
    omega = jnp.broadcast_to(scalar_ref[:, S - 1 : S], (1, 128))
    for at, weight in enumerate(rotation, JAC + S - 1):
        coef_ref[at : at + 1, :] = omega * weight
    for field in range(STATE):
        own = res_ref.at[0, field] if field < FIELDS else gain_ref.at[0]
        below = jnp.where(first, far_ref[field], near_ref[field])
        above = jnp.where(first, near_ref[field], far_ref[field])
        rows = [below, own[0:8, :], own[8:16, :], above]
        for parity in range(2):
            moved = []
            for part in range(4):
                shift = (32 * part + HALO - COLS * parity) % 128
                moved.append([pltpu.roll(rows[part][:, 128 * h : 128 * h + 128], shift, 1) for h in range(2)])
            for inst in range(parity, INST, 2):
                chunk = None
                for part in range(4):
                    left, right = moved[part]
                    piece = left if inst < 8 else right
                    if inst in (7, 8):
                        piece = jnp.where(place < (24 if inst == 7 else 8), left, right)
                    chunk = piece if chunk is None else jnp.where(group == (part + inst // 2) % 4, piece, chunk)
                out_ref[inst, field * 8 : field * 8 + 8, :] = chunk


def merge_pair(first, second, mask, shift, axis):
    high = [jnp.where(mask, second[0], first[0]), jnp.where(mask, first[0], second[0])]
    total, error = two_sum(high[0], pltpu.roll(high[1], shift, axis))
    if first[1] is None:
        return total, error
    low = jnp.where(mask, second[1], first[1]) + pltpu.roll(
        jnp.where(mask, first[1], second[1]), shift, axis
    )
    return total, error + low


def fold_pair(pair, shift, axis):
    total, error = two_sum(pair[0], pltpu.roll(pair[0], shift, axis))
    return total, error + (pair[1] + pltpu.roll(pair[1], shift, axis))


def rotations(table):
    c = [0.0, *table]
    plus = [None] + [c[d] - c[8 - d] for d in (1, 2, 3)]
    minus = [None] + [(c[d] + c[8 - d]) / 2 for d in (1, 2, 3, 4)]
    return ((plus[1] - plus[3]) / 4, (plus[1] + plus[3]) / 4, plus[2] / 2, *minus[1:])


def gap(x, i, d):
    n = len(x)
    before, after = x[(i - d) % n], x[(i + d) % n]
    if i - d < 0:
        return before + after, -1
    return (before - after if i + d < n else before + after), 1


def turned(x, i, weights):
    n = len(x)
    total = None
    for d, weight in enumerate(weights, 1):
        if 2 * d < n:
            value, sign = gap(x, i, d)
        else:
            value, sign = x[(i - d) % n], (1 if i >= d else -1)
        term = weight * value
        if total is None:
            total = term if sign > 0 else -term
        else:
            total = total + term if sign > 0 else total - term
    return total


def coupled(v, weights):
    inner, first, second = weights[:3]
    plus = [v[i] + v[i + 8] for i in range(8)]
    minus = [v[i] - v[i + 8] for i in range(8)]
    sums = [plus[i] + plus[i + 4] for i in range(4)]
    gaps = [plus[i] - plus[i + 4] for i in range(4)]
    even, odd = inner * (sums[3] - sums[1]), inner * (sums[0] - sums[2])
    circle = [even, odd, -even, -odd]
    twisted = [turned(gaps, i, (first, second)) for i in range(4)]
    outer = [circle[i] + twisted[i] for i in range(4)] + [circle[i] - twisted[i] for i in range(4)]
    flipped = [turned(minus, i, weights[3:]) for i in range(8)]
    return [outer[i] + flipped[i] for i in range(8)] + [outer[i] - flipped[i] for i in range(8)]


SLOTS = ((2, 4), (3, 5), (6, 0), (7, 1))
SLOT_MOVES = (0, 16, 64, 80)


def segments():
    return ((lanes() + 128 - HALO) % 128) // 16


def in_slot(seg, q):
    return (seg == SLOTS[q][0]) | (seg == SLOTS[q][1])


TILES = INST * FIELDS
PITCH = 16


def tile_at(i, f):
    return PITCH * (i * FIELDS + f) + 8


def step_kernel(in_ref, number_ref, out_ref, vec_ref, coef_ref, mix_ref, gain_ref, slot_ref):
    lane, sub = lanes(), sublanes()
    seg = segments()
    cell, inst = lax.axis_index("cell"), lax.axis_index("inst")
    turn = lax.rem(inst // 2, 4)
    part = (lane // 32 + 4 - turn) % 4
    row = cell * ROWS - HALO + part * 8 + sub
    col = inst * COLS - HALO + lane % 32
    inside = (row >= 0) & (row < NR) & (col >= 0) & (col < NC)
    for d in range(4):
        for f in range(FIELDS):
            for e in range(FIELDS):
                at = 4 * (f * FIELDS + e) + d
                coef_ref[(d * FIELDS + f) * FIELDS + e] = jnp.broadcast_to(number_ref[at : at + 1, :], TILE)
    for i in range(INST):
        for f in range(FIELDS):
            vec_ref[0, pl.ds(tile_at(i, f), 8), :] = jnp.where(inside, in_ref[i, f * 8 : f * 8 + 8, :], 0.0)
        gain_ref[i] = in_ref[i, FIELDS * 8 : FIELDS * 8 + 8, :]

    weights = [jnp.broadcast_to(number_ref[at : at + 1, :], TILE) for at in range(JAC + S - 1, NUMBERS)]

    def step(n, carry):
        shift = jnp.broadcast_to(number_ref[pl.ds(JAC + n, 1), :], TILE)
        slot = lax.rem(n, 4)
        aligned = lax.rem(lax.rem(slot, 2) * 16 + (slot // 2) * 64 + 128 - 32 * turn, 128)
        now, later = vec_ref.at[n], vec_ref.at[n + 1]
        for group in range(TILES // 8):
            start = PITCH * 8 * group
            last = now[pl.ds(start + 15, 8, stride=PITCH), :]
            now[pl.ds(start + 7, 8, stride=PITCH), :] = pltpu.roll(last, 32, 1)
            first = now[pl.ds(start + 8, 8, stride=PITCH), :]
            now[pl.ds(start + 16, 8, stride=PITCH), :] = pltpu.roll(first, 96, 1)
        for f in range(FIELDS):
            mixed = coupled([now[pl.ds(tile_at(i, f), 8), :] for i in range(INST)], weights)
            for i in range(INST):
                mix_ref[i, f] = mixed[i]
        for pair in range(0, INST, 2):
            members = (pair, pair + 1)
            near, center, gain = {}, {}, {}
            for i in members:
                gain[i] = gain_ref[i] - shift
                for e in range(FIELDS):
                    at = tile_at(i, e)
                    v = now[pl.ds(at, 8), :]
                    center[i, e] = v
                    slot_ref[n, i, e] = pltpu.roll(v, aligned, 1)
                    near[i, 0, e] = now[pl.ds(at - 1, 8), :]
                    near[i, 1, e] = now[pl.ds(at + 1, 8), :]
                    near[i, 2, e] = pltpu.roll(v, 1, 1)
                    near[i, 3, e] = pltpu.roll(v, 127, 1)
            for f in range(FIELDS):
                total = {i: mix_ref[i, f] + gain[i] * center[i, f] for i in members}
                for d in range(4):
                    for e in range(FIELDS):
                        c = coef_ref[(d * FIELDS + f) * FIELDS + e]
                        for i in members:
                            total[i] = total[i] - c * near[i, d, e]
                for i in members:
                    later[pl.ds(tile_at(i, f), 8), :] = jnp.where(inside, total[i], 0.0)
        return carry

    lax.fori_loop(0, S - 1, step, 0)

    packed = {}
    for x, y in ((0, 0), (1, 1), (0, 1)):
        for half in range(2):
            packed[x, y, half] = [(4 * x + q, 4 * y + (q + 2 * half) % 4, q) for q in range(4)]
    covered = {(min(a, b), max(a, b)) for entries in packed.values() for a, b, _ in entries}
    plain = [(a, b) for a in range(S) for b in range(a, S) if (a, b) not in covered]
    last_move = lax.rem(SLOT_MOVES[3] + 128 - 32 * turn, 128)

    def gather(quarter, sums):
        sums = list(sums)
        for i in [quarter * 4 + q for q in range(4)]:
            tiles = {}
            for f in range(FIELDS):
                at = pl.multiple_of(PITCH * FIELDS * i + tile_at(0, f), 8)
                v = [vec_ref[s, pl.ds(at, 8), :] for s in range(S)]
                moved = [slot_ref[s, i, f] for s in range(S - 1)] + [pltpu.roll(v[S - 1], last_move, 1)]
                for x in range(2):
                    a, b, c, d = moved[4 * x : 4 * x + 4]
                    tiles[x, f] = jnp.where(
                        in_slot(seg, 0), a, jnp.where(in_slot(seg, 1), b, jnp.where(in_slot(seg, 2), c, d))
                    )
                turned_tiles = [pltpu.roll(tiles[x, f], 64, 1) for x in range(2)]
                for p, (a, b) in enumerate(plain):
                    sums[p] = sums[p] + v[a] * v[b]
                for p, (x, y, half) in enumerate(packed, len(plain)):
                    sums[p] = sums[p] + tiles[x, f] * (turned_tiles[y] if half else tiles[y, f])
                out_ref[i, (4 + f) * 8 : (4 + f) * 8 + 8, :] = tiles[1, f]
            for f in range(4):
                tile = tiles[0, f]
                if f < 3:
                    move = (SLOT_MOVES[0] - SLOT_MOVES[f + 1]) % 128
                    tile = jnp.where(in_slot(seg, 0), pltpu.roll(tiles[0, 4], move, 1), tile)
                out_ref[i, f * 8 : f * 8 + 8, :] = tile
        return tuple(sums)

    start = tuple(jnp.zeros(TILE, jnp.float32) for _ in range(len(plain) + len(packed)))
    sums = lax.fori_loop(0, INST // 4, gather, start)
    column = lane % 32
    own = ((part == 1) | (part == 2)) & (column >= HALO) & (column < HALO + COLS)
    entry = {}
    for p, (a, b) in enumerate(plain):
        entry[a, b] = entry[b, a] = (jnp.where(own, sums[p], 0.0), None)
    for p, entries in enumerate(packed.values(), len(plain)):
        for a, b, q in entries:
            if (a, b) not in entry:
                entry[a, b] = entry[b, a] = (jnp.where(in_slot(seg, q), sums[p], 0.0), None)
    columns = []
    for b in range(S):
        level = [entry[a, b] for a in range(S)]
        for bit in (1, 2, 4):
            mask = (sub & bit) != 0
            level = [merge_pair(level[2 * q], level[2 * q + 1], mask, bit, 0) for q in range(len(level) // 2)]
        columns.append(level[0])
    for bit in (1, 2, 4):
        mask = (lane & bit) != 0
        columns = [merge_pair(columns[2 * q], columns[2 * q + 1], mask, bit, 1) for q in range(len(columns) // 2)]
    pair = columns[0]
    for shift in (64, 32, 16):
        pair = fold_pair(pair, shift, 1)
    pair = jnp.where(seg == SLOTS[0][0], pair[0], pair[1])
    for i in range(INST):
        out_ref[i, 24:32, :] = jnp.where(in_slot(seg, 0), pair, out_ref[i, 24:32, :])


def gram_kernel(in_ref, out_ref):
    lane, sub = lanes(), sublanes()
    total, error = sum_pairs([in_ref[i, 24:32, :] for i in range(INST)])
    high, low = fold_pair((total, error + pltpu.roll(total, 96, 1)), 8, 1)
    here = (lane >= 48) & (lane < 56)
    both = jnp.where(here, high, 0.0) + pltpu.roll(jnp.where(here, low, 0.0), 8, 1)
    for shift in (16, 32, 64):
        both = both + pltpu.roll(both, shift, 1)
    row = jnp.where(lane // 16 == sub, both, 0.0)
    row = jnp.broadcast_to(jnp.sum(row, axis=0, keepdims=True), TILE)
    for q in range(CELLS // 8):
        out_ref[q * 8 : q * 8 + 8, :] = row


def sum_pairs(values):
    level = [(v, None) for v in values]
    while len(level) > 1:
        merged = []
        for q in range(0, len(level), 2):
            total, error = two_sum(level[q][0], level[q + 1][0])
            if level[q][1] is not None:
                error = error + (level[q][1] + level[q + 1][1])
            merged.append((total, error))
        level = merged
    return level[0]


def unpack_kernel(in_ref, out_ref):
    seg = lanes() // 16
    places = {}
    for q, segs in enumerate(SLOTS):
        for part in range(2):
            places[segs[part]] = (q, part)
    for tile in range(9):
        for wide in range(2):
            tiles = [pltpu.roll(in_ref[8 * wide + q, tile * 8 : tile * 8 + 8, :], 128 - HALO, 1) for q in range(8)]
            for bit in (1, 2, 4):
                off = (seg & bit) == 0
                for q in range(8):
                    if q & bit:
                        continue
                    a, b = tiles[q], tiles[q + bit]
                    tiles[q] = jnp.where(off, a, pltpu.roll(b, 16 * bit, 1))
                    tiles[q + bit] = jnp.where(off, pltpu.roll(a, 128 - 16 * bit, 1), b)
            for q in range(8):
                s, part = places[q]
                if tile >= 4:
                    s, f = 4 + s, tile - 4
                elif s:
                    f = tile
                elif tile < 3:
                    s, f = tile + 1, 4
                else:
                    continue
                out_ref[s - 1, 0, f, 8 * part : 8 * part + 8, 128 * wide : 128 * wide + 128] = tiles[q]


TRIANGLE = [(i, j) for i in range(S) for j in range(i + 1)]


def inverse_of(lower, scale):
    inverse = {}
    for i in range(S):
        inverse[i, i] = scale[i]
        for j in range(i):
            total = lower[i, j] * inverse[j, j]
            for k in range(j + 1, i):
                total = total + lower[i, k] * inverse[k, j]
            inverse[i, j] = -(scale[i] * total)
    return inverse


def product_of(a, b):
    out = {}
    for i, j in TRIANGLE:
        total = a[i, j] * b[j, j]
        for k in range(j + 1, i + 1):
            total = total + a[i, k] * b[k, j]
        out[i, j] = total
    return out


def factor_pairs(high, low):
    lower, scale = {}, {}
    for k in range(S):
        full = {i: high[i, k] + low[i, k] for i in range(k, S)}
        scale[k] = lax.rsqrt(full[k])
        parts = {}
        for i in range(k, S):
            lower[i, k] = full[i] * scale[k]
            parts[i] = split(lower[i, k])
        for i in range(k, S):
            for j in range(k, i + 1):
                (a_high, a_low), (b_high, b_low) = parts[i], parts[j]
                high[i, j], rest = two_sum(high[i, j], -(a_high * b_high))
                low[i, j] = low[i, j] + (rest - (a_high * b_low + a_low * lower[j, k]))
    return lower, inverse_of(lower, scale), {at: high[at] + low[at] for at in TRIANGLE}


def factor_plain(matrix):
    lower, scale = {}, {}
    for k in range(S):
        scale[k] = lax.rsqrt(matrix[k, k])
        for i in range(k, S):
            lower[i, k] = matrix[i, k] * scale[k]
        for i in range(k + 1, S):
            for j in range(k + 1, i + 1):
                matrix[i, j] = matrix[i, j] - lower[i, k] * lower[j, k]
    return lower, inverse_of(lower, scale)


def finish_kernel(rows_ref, res_ref, vec_ref, out_ref, factor_ref):
    lane, sub = lanes(), sublanes()
    pair = sum_pairs([rows_ref[q * 8 : q * 8 + 8, :] for q in range(CELLS // 8)])
    for shift in (1, 2, 4):
        pair = fold_pair(pair, shift, 0)
    low_row = pair[1] + pltpu.roll(pair[0], 128 - S, 1)
    high = {(i, j): jnp.broadcast_to(pair[0][:, 16 * i + j : 16 * i + j + 1], TILE) for i, j in TRIANGLE}
    low = {(i, j): jnp.broadcast_to(low_row[:, 16 * i + j : 16 * i + j + 1], TILE) for i, j in TRIANGLE}
    lower_one, inverse_one, rest = factor_pairs(high, low)
    half = {}
    for i in range(S):
        for j in range(i + 1):
            total = None
            for k in range(i + 1):
                term = inverse_one[i, k] * rest[max(k, j), min(k, j)]
                total = term if total is None else total + term
            half[i, j] = total
    square = {}
    for i, j in TRIANGLE:
        total = half[i, 0] * inverse_one[j, 0]
        for k in range(1, j + 1):
            total = total + half[i, k] * inverse_one[j, k]
        square[i, j] = total + 1.0 if i == j else total
    lower_two, inverse_two = factor_plain(square)
    lower = product_of(lower_one, lower_two)
    weight = product_of(inverse_two, inverse_one)
    block = jnp.zeros(TILE, jnp.float32)
    for i, j in TRIANGLE:
        block = jnp.where((sub == j) & (lane == i), lower[i, j], block)
    factor_ref[...] = block[:, :S]
    for f in range(FIELDS):
        for part in range(2):
            for wide in range(2):
                place = (0, f, pl.ds(8 * part, 8), pl.ds(128 * wide, 128))
                v = [res_ref[place]] + [vec_ref[(s, *place)] for s in range(S - 1)]
                for a in range(S):
                    total = weight[a, 0] * v[0]
                    for b in range(1, a + 1):
                        total = total + weight[a, b] * v[b]
                    out_ref[(a, *place)] = total


def edge_kernel(res_ref, gain_ref, near_ref, far_ref, sems):
    odd = lax.rem(lax.axis_index("cell"), 2)
    copies = []
    for ref, start in ((near_ref, 8 * (1 - odd)), (far_ref, 8 * odd)):
        rows = pl.ds(pl.multiple_of(start, 8), 8)
        for source, target in ((res_ref.at[0, :, rows, :], ref.at[pl.ds(0, FIELDS)]), (gain_ref.at[:, rows, :], ref.at[pl.ds(FIELDS, 1)])):
            copies.append(pltpu.make_async_copy(source, target, sems.at[len(copies)]))
    for copy in copies:
        copy.start()
    for copy in copies:
        copy.wait()


def call(kernel, out_shape, in_specs, args, scratch=(), flops=10**6):
    shapes = jax.tree.map(lambda s: jax.ShapeDtypeStruct(s, jnp.float32), out_shape, is_leaf=lambda s: isinstance(s[0], int))
    return pl.pallas_call(
        kernel,
        out_shape=shapes,
        in_specs=in_specs,
        out_specs=jax.tree.map(lambda _: VMEM, shapes),
        scratch_shapes=scratch,
        compiler_params=pltpu.CompilerParams(vmem_limit_bytes=40 * 2**20),
        cost_estimate=pl.CostEstimate(flops=flops, transcendentals=0, bytes_accessed=2 * 10**6),
    )(*args)


def coupling_table():
    angles = np.pi * np.arange(1, 8) / INST
    return [float(c) for c in 0.5 * (-1.0) ** np.arange(1, 8) * np.cos(angles) / np.sin(angles)]


def on_device(residual, diag_gain, flux_jac, omega, shifts):
    pairs = [(i, i + 1) for i in range(CELLS - 1)]
    pairs = [pairs[0::2], pairs[1::2]]
    near, far = call(
        edge_kernel,
        ((STATE, 8, NC), (STATE, 8, NC)),
        [HBM] * 2,
        [pltpu.with_memory_space_constraint(x, pltpu.HBM) for x in (residual, diag_gain)],
        scratch=[pltpu.SemaphoreType.DMA((4,))],
    )
    far = lax.ppermute(far, "cell", pairs[1] + [(b, a) for a, b in pairs[1]])
    near = lax.ppermute(near, "cell", pairs[0] + [(b, a) for a, b in pairs[0]])
    chunks, numbers = call(
        functools.partial(pack_kernel, rotations(coupling_table())),
        ((INST, STATE * 8, 128), (NUMBERS + 6, 128)),
        [VMEM] * 6,
        (residual, diag_gain, near, far, flux_jac.transpose(1, 0, 2), jnp.concatenate([shifts, omega])[None]),
    )
    patches = lax.all_to_all(chunks, "inst", 0, 0, tiled=True)
    vectors = call(
        step_kernel,
        (INST, 72, 128),
        [VMEM, VMEM],
        (patches, numbers),
        scratch=[
            pltpu.VMEM((S, PITCH * (TILES + 1), 128), jnp.float32),
            pltpu.VMEM((JAC, *TILE), jnp.float32),
            pltpu.VMEM((INST, FIELDS, *TILE), jnp.float32),
            pltpu.VMEM((INST, *TILE), jnp.float32),
            pltpu.VMEM((S - 1, INST, FIELDS, *TILE), jnp.float32),
        ],
        flops=10**8,
    )
    back = lax.all_to_all(vectors, "inst", 0, 0, tiled=True)
    row = call(gram_kernel, (CELLS, 128), [VMEM], (back,))
    rows = lax.all_to_all(row, "cell", 0, 0, axis_index_groups=MEETING, tiled=True)
    others = call(unpack_kernel, (S - 1, 1, FIELDS, ROWS, NC), [VMEM], (back,))
    return call(
        finish_kernel,
        ((S, 1, FIELDS, ROWS, NC), (S, S)),
        [VMEM] * 3,
        (rows, residual, others),
    )


def solution(mesh):
    in_specs = (P("inst", None, "cell", None), P("inst", "cell", None), P(), P(), P())
    out_specs = (P(None, "inst", None, "cell", None), P())
    return jax.shard_map(
        on_device, mesh=mesh, in_specs=in_specs, out_specs=out_specs, check_vma=False
    )
```

```python
import functools

import jax
import jax.numpy as jnp
import numpy as np
from jax import lax
from jax.experimental import pallas as pl
from jax.experimental.pallas import tpu as pltpu
from jax.sharding import PartitionSpec as P


S = 8
FIELDS = 5
INST = 16
CELLS = 64
HALO = 8
ROWS = 16
COLS = 16
NC = 256
NR = 1024
STATE = FIELDS + 1
MEETING = [[(i + CELLS // 2) % CELLS for i in range(CELLS)]]
VMEM = pl.BlockSpec(memory_space=pltpu.VMEM)
HBM = pl.BlockSpec(memory_space=pltpu.HBM)
TILE = (8, 128)
JAC = 4 * FIELDS * FIELDS
NUMBERS = JAC + S - 1 + 7


def lanes():
    return lax.broadcasted_iota(jnp.int32, TILE, 1)


def sublanes():
    return lax.broadcasted_iota(jnp.int32, TILE, 0)


def two_sum(a, b):
    total = a + b
    part = total - a
    return total, (a - (total - part)) + (b - part)


def split(a):
    scaled = a * 4097.0
    high = scaled - (scaled - a)
    return high, a - high


def pack_kernel(rotation, res_ref, gain_ref, near_ref, far_ref, jac_ref, omega_ref, shift_ref, out_ref, coef_ref):
    lane = lanes()
    first = lax.rem(lax.axis_index("cell"), 2) == 0
    group, place = lane // 32, lane % 32
    for f in range(FIELDS):
        for e in range(FIELDS):
            at = 4 * (f * FIELDS + e)
            coef_ref[at : at + 4, :] = jnp.broadcast_to(jac_ref[f, :, e : e + 1], (4, 128))
    for n in range(S - 1):
        coef_ref[JAC + n : JAC + n + 1, :] = jnp.broadcast_to(shift_ref[:, n : n + 1], (1, 128))
    omega = jnp.full((1, 128), omega_ref[0])
    for at, weight in enumerate(rotation, JAC + S - 1):
        coef_ref[at : at + 1, :] = omega * weight
    for field in range(STATE):
        own = res_ref.at[0, field] if field < FIELDS else gain_ref.at[0]
        below = jnp.where(first, far_ref[field], near_ref[field])
        above = jnp.where(first, near_ref[field], far_ref[field])
        rows = [below, own[0:8, :], own[8:16, :], above]
        for parity in range(2):
            moved = []
            for part in range(4):
                shift = (32 * part + HALO - COLS * parity) % 128
                moved.append([pltpu.roll(rows[part][:, 128 * h : 128 * h + 128], shift, 1) for h in range(2)])
            for inst in range(parity, INST, 2):
                chunk = None
                for part in range(4):
                    left, right = moved[part]
                    piece = left if inst < 8 else right
                    if inst in (7, 8):
                        piece = jnp.where(place < (24 if inst == 7 else 8), left, right)
                    chunk = piece if chunk is None else jnp.where(group == (part + inst // 2) % 4, piece, chunk)
                out_ref[inst, field * 8 : field * 8 + 8, :] = chunk


def merge_pair(first, second, mask, shift, axis):
    high = [jnp.where(mask, second[0], first[0]), jnp.where(mask, first[0], second[0])]
    total, error = two_sum(high[0], pltpu.roll(high[1], shift, axis))
    if first[1] is None:
        return total, error
    low = jnp.where(mask, second[1], first[1]) + pltpu.roll(
        jnp.where(mask, first[1], second[1]), shift, axis
    )
    return total, error + low


def fold_pair(pair, shift, axis):
    total, error = two_sum(pair[0], pltpu.roll(pair[0], shift, axis))
    return total, error + (pair[1] + pltpu.roll(pair[1], shift, axis))


def rotations(table):
    c = [0.0, *table]
    plus = [None] + [c[d] - c[8 - d] for d in (1, 2, 3)]
    minus = [None] + [(c[d] + c[8 - d]) / 2 for d in (1, 2, 3, 4)]
    return ((plus[1] - plus[3]) / 4, (plus[1] + plus[3]) / 4, plus[2] / 2, *minus[1:])


def gap(x, i, d):
    n = len(x)
    before, after = x[(i - d) % n], x[(i + d) % n]
    if i - d < 0:
        return before + after, -1
    return (before - after if i + d < n else before + after), 1


def turned(x, i, weights):
    n = len(x)
    total = None
    for d, weight in enumerate(weights, 1):
        if 2 * d < n:
            value, sign = gap(x, i, d)
        else:
            value, sign = x[(i - d) % n], (1 if i >= d else -1)
        term = weight * value
        if total is None:
            total = term if sign > 0 else -term
        else:
            total = total + term if sign > 0 else total - term
    return total


def coupled(v, weights):
    inner, first, second = weights[:3]
    plus = [v[i] + v[i + 8] for i in range(8)]
    minus = [v[i] - v[i + 8] for i in range(8)]
    sums = [plus[i] + plus[i + 4] for i in range(4)]
    gaps = [plus[i] - plus[i + 4] for i in range(4)]
    even, odd = inner * (sums[3] - sums[1]), inner * (sums[0] - sums[2])
    circle = [even, odd, -even, -odd]
    twisted = [turned(gaps, i, (first, second)) for i in range(4)]
    outer = [circle[i] + twisted[i] for i in range(4)] + [circle[i] - twisted[i] for i in range(4)]
    flipped = [turned(minus, i, weights[3:]) for i in range(8)]
    return [outer[i] + flipped[i] for i in range(8)] + [outer[i] - flipped[i] for i in range(8)]


SLOTS = ((2, 4), (3, 5), (6, 0), (7, 1))
SLOT_MOVES = (0, 16, 64, 80)


def segments():
    return ((lanes() + 128 - HALO) % 128) // 16


def in_slot(seg, q):
    return (seg == SLOTS[q][0]) | (seg == SLOTS[q][1])


TILES = INST * FIELDS
PITCH = 16


def tile_at(i, f):
    return PITCH * (i * FIELDS + f) + 8


def step_kernel(in_ref, number_ref, out_ref, vec_ref, coef_ref, mix_ref, gain_ref, slot_ref):
    lane, sub = lanes(), sublanes()
    seg = segments()
    cell, inst = lax.axis_index("cell"), lax.axis_index("inst")
    turn = lax.rem(inst // 2, 4)
    part = (lane // 32 + 4 - turn) % 4
    row = cell * ROWS - HALO + part * 8 + sub
    col = inst * COLS - HALO + lane % 32
    inside = (row >= 0) & (row < NR) & (col >= 0) & (col < NC)
    for d in range(4):
        for f in range(FIELDS):
            for e in range(FIELDS):
                at = 4 * (f * FIELDS + e) + d
                coef_ref[(d * FIELDS + f) * FIELDS + e] = jnp.broadcast_to(number_ref[at : at + 1, :], TILE)
    for i in range(INST):
        for f in range(FIELDS):
            vec_ref[0, pl.ds(tile_at(i, f), 8), :] = jnp.where(inside, in_ref[i, f * 8 : f * 8 + 8, :], 0.0)
        gain_ref[i] = in_ref[i, FIELDS * 8 : FIELDS * 8 + 8, :]

    weights = [jnp.broadcast_to(number_ref[at : at + 1, :], TILE) for at in range(JAC + S - 1, NUMBERS)]

    def step(n, carry):
        shift = jnp.broadcast_to(number_ref[pl.ds(JAC + n, 1), :], TILE)
        slot = lax.rem(n, 4)
        aligned = lax.rem(lax.rem(slot, 2) * 16 + (slot // 2) * 64 + 128 - 32 * turn, 128)
        now, later = vec_ref.at[n], vec_ref.at[n + 1]
        for group in range(TILES // 8):
            start = PITCH * 8 * group
            last = now[pl.ds(start + 15, 8, stride=PITCH), :]
            now[pl.ds(start + 7, 8, stride=PITCH), :] = pltpu.roll(last, 32, 1)
            first = now[pl.ds(start + 8, 8, stride=PITCH), :]
            now[pl.ds(start + 16, 8, stride=PITCH), :] = pltpu.roll(first, 96, 1)
        for f in range(FIELDS):
            mixed = coupled([now[pl.ds(tile_at(i, f), 8), :] for i in range(INST)], weights)
            for i in range(INST):
                mix_ref[i, f] = mixed[i]
        for pair in range(0, INST, 4):
            members = (pair, pair + 1, pair + 2, pair + 3)
            near, center, gain = {}, {}, {}
            for i in members:
                gain[i] = gain_ref[i] - shift
                for e in range(FIELDS):
                    at = tile_at(i, e)
                    v = now[pl.ds(at, 8), :]
                    center[i, e] = v
                    slot_ref[n, i, e] = pltpu.roll(v, aligned, 1)
                    near[i, 0, e] = now[pl.ds(at - 1, 8), :]
                    near[i, 1, e] = now[pl.ds(at + 1, 8), :]
                    near[i, 2, e] = pltpu.roll(v, 1, 1)
                    near[i, 3, e] = pltpu.roll(v, 127, 1)
            total = {(i, f): mix_ref[i, f] + gain[i] * center[i, f] for i in members for f in range(FIELDS)}
            for e in range(FIELDS):
                for d in range(4):
                    for f in range(FIELDS):
                        c = coef_ref[(d * FIELDS + f) * FIELDS + e]
                        for i in members:
                            total[i, f] = total[i, f] - c * near[i, d, e]
            for i in members:
                for f in range(FIELDS):
                    later[pl.ds(tile_at(i, f), 8), :] = jnp.where(inside, total[i, f], 0.0)
        return carry

    lax.fori_loop(0, S - 1, step, 0)

    packed = {}
    for x, y in ((0, 0), (1, 1), (0, 1)):
        for half in range(2):
            packed[x, y, half] = [(4 * x + q, 4 * y + (q + 2 * half) % 4, q) for q in range(4)]
    covered = {(min(a, b), max(a, b)) for entries in packed.values() for a, b, _ in entries}
    plain = [(a, b) for a in range(S) for b in range(a, S) if (a, b) not in covered]
    last_move = lax.rem(SLOT_MOVES[3] + 128 - 32 * turn, 128)

    def gather(quarter, sums):
        sums = list(sums)
        for i in [quarter * 4 + q for q in range(4)]:
            tiles = {}
            for f in range(FIELDS):
                at = pl.multiple_of(PITCH * FIELDS * i + tile_at(0, f), 8)
                v = [vec_ref[s, pl.ds(at, 8), :] for s in range(S)]
                moved = [slot_ref[s, i, f] for s in range(S - 1)] + [pltpu.roll(v[S - 1], last_move, 1)]
                for x in range(2):
                    a, b, c, d = moved[4 * x : 4 * x + 4]
                    tiles[x, f] = jnp.where(
                        in_slot(seg, 0), a, jnp.where(in_slot(seg, 1), b, jnp.where(in_slot(seg, 2), c, d))
                    )
                turned_tiles = [pltpu.roll(tiles[x, f], 64, 1) for x in range(2)]
                for p, (a, b) in enumerate(plain):
                    sums[p] = sums[p] + v[a] * v[b]
                for p, (x, y, half) in enumerate(packed, len(plain)):
                    sums[p] = sums[p] + tiles[x, f] * (turned_tiles[y] if half else tiles[y, f])
                out_ref[i, (4 + f) * 8 : (4 + f) * 8 + 8, :] = tiles[1, f]
            for f in range(4):
                tile = tiles[0, f]
                if f < 3:
                    move = (SLOT_MOVES[0] - SLOT_MOVES[f + 1]) % 128
                    tile = jnp.where(in_slot(seg, 0), pltpu.roll(tiles[0, 4], move, 1), tile)
                out_ref[i, f * 8 : f * 8 + 8, :] = tile
        return tuple(sums)

    start = tuple(jnp.zeros(TILE, jnp.float32) for _ in range(len(plain) + len(packed)))
    sums = lax.fori_loop(0, INST // 4, gather, start)
    column = lane % 32
    own = ((part == 1) | (part == 2)) & (column >= HALO) & (column < HALO + COLS)
    entry = {}
    for p, (a, b) in enumerate(plain):
        entry[a, b] = entry[b, a] = (jnp.where(own, sums[p], 0.0), None)
    for p, entries in enumerate(packed.values(), len(plain)):
        for a, b, q in entries:
            if (a, b) not in entry:
                entry[a, b] = entry[b, a] = (jnp.where(in_slot(seg, q), sums[p], 0.0), None)
    columns = []
    for b in range(S):
        level = [entry[a, b] for a in range(S)]
        for bit in (1, 2, 4):
            mask = (sub & bit) != 0
            level = [merge_pair(level[2 * q], level[2 * q + 1], mask, bit, 0) for q in range(len(level) // 2)]
        columns.append(level[0])
    for bit in (1, 2, 4):
        mask = (lane & bit) != 0
        columns = [merge_pair(columns[2 * q], columns[2 * q + 1], mask, bit, 1) for q in range(len(columns) // 2)]
    pair = columns[0]
    for shift in (64, 32, 16):
        pair = fold_pair(pair, shift, 1)
    pair = jnp.where(seg == SLOTS[0][0], pair[0], pair[1])
    for i in range(INST):
        out_ref[i, 24:32, :] = jnp.where(in_slot(seg, 0), pair, out_ref[i, 24:32, :])


def gram_kernel(in_ref, out_ref):
    lane, sub = lanes(), sublanes()
    total, error = sum_pairs([in_ref[i, 24:32, :] for i in range(INST)])
    high, low = fold_pair((total, error + pltpu.roll(total, 96, 1)), 8, 1)
    here = (lane >= 48) & (lane < 56)
    both = jnp.where(here, high, 0.0) + pltpu.roll(jnp.where(here, low, 0.0), 8, 1)
    for shift in (16, 32, 64):
        both = both + pltpu.roll(both, shift, 1)
    row = jnp.where(lane // 16 == sub, both, 0.0)
    row = jnp.broadcast_to(jnp.sum(row, axis=0, keepdims=True), TILE)
    for q in range(CELLS // 8):
        out_ref[q * 8 : q * 8 + 8, :] = row


def sum_pairs(values):
    level = [(v, None) for v in values]
    while len(level) > 1:
        merged = []
        for q in range(0, len(level), 2):
            total, error = two_sum(level[q][0], level[q + 1][0])
            if level[q][1] is not None:
                error = error + (level[q][1] + level[q + 1][1])
            merged.append((total, error))
        level = merged
    return level[0]


def unpack_kernel(in_ref, out_ref):
    seg = lanes() // 16
    places = {}
    for q, segs in enumerate(SLOTS):
        for part in range(2):
            places[segs[part]] = (q, part)
    for tile in range(9):
        for wide in range(2):
            tiles = [pltpu.roll(in_ref[8 * wide + q, tile * 8 : tile * 8 + 8, :], 128 - HALO, 1) for q in range(8)]
            for bit in (1, 2, 4):
                off = (seg & bit) == 0
                for q in range(8):
                    if q & bit:
                        continue
                    a, b = tiles[q], tiles[q + bit]
                    tiles[q] = jnp.where(off, a, pltpu.roll(b, 16 * bit, 1))
                    tiles[q + bit] = jnp.where(off, pltpu.roll(a, 128 - 16 * bit, 1), b)
            for q in range(8):
                s, part = places[q]
                if tile >= 4:
                    s, f = 4 + s, tile - 4
                elif s:
                    f = tile
                elif tile < 3:
                    s, f = tile + 1, 4
                else:
                    continue
                out_ref[s - 1, 0, f, 8 * part : 8 * part + 8, 128 * wide : 128 * wide + 128] = tiles[q]


TRIANGLE = [(i, j) for i in range(S) for j in range(i + 1)]


def inverse_of(lower, scale):
    inverse = {}
    for i in range(S):
        inverse[i, i] = scale[i]
        for j in range(i):
            total = lower[i, j] * inverse[j, j]
            for k in range(j + 1, i):
                total = total + lower[i, k] * inverse[k, j]
            inverse[i, j] = -(scale[i] * total)
    return inverse


def product_of(a, b):
    out = {}
    for i, j in TRIANGLE:
        total = a[i, j] * b[j, j]
        for k in range(j + 1, i + 1):
            total = total + a[i, k] * b[k, j]
        out[i, j] = total
    return out


def factor_pairs(high, low):
    lower, scale = {}, {}
    for k in range(S):
        full = {i: high[i, k] + low[i, k] for i in range(k, S)}
        scale[k] = lax.rsqrt(full[k])
        parts = {}
        for i in range(k, S):
            lower[i, k] = full[i] * scale[k]
            parts[i] = split(lower[i, k])
        for i in range(k, S):
            for j in range(k, i + 1):
                (a_high, a_low), (b_high, b_low) = parts[i], parts[j]
                high[i, j], rest = two_sum(high[i, j], -(a_high * b_high))
                low[i, j] = low[i, j] + (rest - (a_high * b_low + a_low * lower[j, k]))
    return lower, inverse_of(lower, scale), {at: high[at] + low[at] for at in TRIANGLE}


def factor_plain(matrix):
    lower, scale = {}, {}
    for k in range(S):
        scale[k] = lax.rsqrt(matrix[k, k])
        for i in range(k, S):
            lower[i, k] = matrix[i, k] * scale[k]
        for i in range(k + 1, S):
            for j in range(k + 1, i + 1):
                matrix[i, j] = matrix[i, j] - lower[i, k] * lower[j, k]
    return lower, inverse_of(lower, scale)


def finish_kernel(rows_ref, res_ref, vec_ref, out_ref, factor_ref):
    lane, sub = lanes(), sublanes()
    pair = sum_pairs([rows_ref[q * 8 : q * 8 + 8, :] for q in range(CELLS // 8)])
    for shift in (1, 2, 4):
        pair = fold_pair(pair, shift, 0)
    low_row = pair[1] + pltpu.roll(pair[0], 128 - S, 1)
    high = {(i, j): jnp.broadcast_to(pair[0][:, 16 * i + j : 16 * i + j + 1], TILE) for i, j in TRIANGLE}
    low = {(i, j): jnp.broadcast_to(low_row[:, 16 * i + j : 16 * i + j + 1], TILE) for i, j in TRIANGLE}
    lower_one, inverse_one, rest = factor_pairs(high, low)
    half = {}
    for i in range(S):
        for j in range(i + 1):
            total = None
            for k in range(i + 1):
                term = inverse_one[i, k] * rest[max(k, j), min(k, j)]
                total = term if total is None else total + term
            half[i, j] = total
    square = {}
    for i, j in TRIANGLE:
        total = half[i, 0] * inverse_one[j, 0]
        for k in range(1, j + 1):
            total = total + half[i, k] * inverse_one[j, k]
        square[i, j] = total + 1.0 if i == j else total
    lower_two, inverse_two = factor_plain(square)
    lower = product_of(lower_one, lower_two)
    weight = product_of(inverse_two, inverse_one)
    block = jnp.zeros(TILE, jnp.float32)
    for i, j in TRIANGLE:
        block = jnp.where((sub == j) & (lane == i), lower[i, j], block)
    factor_ref[...] = block[:, :S]
    for f in range(FIELDS):
        for part in range(2):
            for wide in range(2):
                place = (0, f, pl.ds(8 * part, 8), pl.ds(128 * wide, 128))
                v = [res_ref[place]] + [vec_ref[(s, *place)] for s in range(S - 1)]
                for a in range(S):
                    total = weight[a, 0] * v[0]
                    for b in range(1, a + 1):
                        total = total + weight[a, b] * v[b]
                    out_ref[(a, *place)] = total


def edge_kernel(res_ref, gain_ref, jac_ref, shift_ref, near_ref, far_ref, jac_out, shift_out, sems):
    odd = lax.rem(lax.axis_index("cell"), 2)
    moves = [(jac_ref, jac_out), (shift_ref, shift_out)]
    for ref, start in ((far_ref, 8 * odd), (near_ref, 8 * (1 - odd))):
        rows = pl.ds(pl.multiple_of(start, 8), 8)
        moves.append((res_ref.at[0, :, rows, :], ref.at[pl.ds(0, FIELDS)]))
        moves.append((gain_ref.at[:, rows, :], ref.at[pl.ds(FIELDS, 1)]))
    copies = [pltpu.make_async_copy(*move, sems.at[n]) for n, move in enumerate(moves)]
    for copy in copies:
        copy.start()
    for copy in copies:
        copy.wait()


def call(kernel, out_shape, in_specs, args, scratch=(), flops=10**6):
    shapes = jax.tree.map(lambda s: jax.ShapeDtypeStruct(s, jnp.float32), out_shape, is_leaf=lambda s: isinstance(s[0], int))
    return pl.pallas_call(
        kernel,
        out_shape=shapes,
        in_specs=in_specs,
        out_specs=jax.tree.map(lambda _: VMEM, shapes),
        scratch_shapes=scratch,
        compiler_params=pltpu.CompilerParams(vmem_limit_bytes=40 * 2**20),
        cost_estimate=pl.CostEstimate(flops=flops, transcendentals=0, bytes_accessed=2 * 10**6),
    )(*args)


def coupling_table():
    angles = np.pi * np.arange(1, 8) / INST
    return [float(c) for c in 0.5 * (-1.0) ** np.arange(1, 8) * np.cos(angles) / np.sin(angles)]


def on_device(residual, diag_gain, flux_jac, omega, shifts):
    pairs = [(i, i + 1) for i in range(CELLS - 1)]
    pairs = [pairs[0::2], pairs[1::2]]
    held = (residual, diag_gain, flux_jac.transpose(1, 0, 2), shifts[None])
    near, far, jac, shift = call(
        edge_kernel,
        ((STATE, 8, NC), (STATE, 8, NC), *[x.shape for x in held[2:]]),
        [HBM] * 4,
        [pltpu.with_memory_space_constraint(x, pltpu.HBM) for x in held],
        scratch=[pltpu.SemaphoreType.DMA((6,))],
    )
    far = lax.ppermute(far, "cell", pairs[1] + [(b, a) for a, b in pairs[1]])
    near = lax.ppermute(near, "cell", pairs[0] + [(b, a) for a, b in pairs[0]])
    chunks, numbers = call(
        functools.partial(pack_kernel, rotations(coupling_table())),
        ((INST, STATE * 8, 128), (NUMBERS + 6, 128)),
        [VMEM] * 5 + [pl.BlockSpec(memory_space=pltpu.SMEM), VMEM],
        (residual, diag_gain, near, far, jac, omega, shift),
    )
    patches = lax.all_to_all(chunks, "inst", 0, 0, tiled=True)
    vectors = call(
        step_kernel,
        (INST, 72, 128),
        [VMEM, VMEM],
        (patches, numbers),
        scratch=[
            pltpu.VMEM((S, PITCH * (TILES + 1), 128), jnp.float32),
            pltpu.VMEM((JAC, *TILE), jnp.float32),
            pltpu.VMEM((INST, FIELDS, *TILE), jnp.float32),
            pltpu.VMEM((INST, *TILE), jnp.float32),
            pltpu.VMEM((S - 1, INST, FIELDS, *TILE), jnp.float32),
        ],
        flops=10**8,
    )
    back = lax.all_to_all(vectors, "inst", 0, 0, tiled=True)
    row = call(gram_kernel, (CELLS, 128), [VMEM], (back,))
    rows = lax.all_to_all(row, "cell", 0, 0, axis_index_groups=MEETING, tiled=True)
    others = call(unpack_kernel, (S - 1, 1, FIELDS, ROWS, NC), [VMEM], (back,))
    return call(
        finish_kernel,
        ((S, 1, FIELDS, ROWS, NC), (S, S)),
        [VMEM] * 3,
        (rows, residual, others),
    )


def solution(mesh):
    in_specs = (P("inst", None, "cell", None), P("inst", "cell", None), P(), P(), P())
    out_specs = (P(None, "inst", None, "cell", None), P())
    return jax.shard_map(
        on_device, mesh=mesh, in_specs=in_specs, out_specs=out_specs, check_vma=False
    )
```

```python
import functools

import jax
import jax.numpy as jnp
import numpy as np
from jax import lax
from jax.experimental import pallas as pl
from jax.experimental.pallas import tpu as pltpu
from jax.sharding import PartitionSpec as P


S = 8
FIELDS = 5
INST = 16
CELLS = 64
HALO = 8
ROWS = 16
COLS = 16
NC = 256
NR = 1024
STATE = FIELDS + 1
MEETING = [[(i + CELLS // 2) % CELLS for i in range(CELLS)]]
TURN = [(i + INST - 1) % INST for i in range(INST)]
VMEM = pl.BlockSpec(memory_space=pltpu.VMEM)
HBM = pl.BlockSpec(memory_space=pltpu.HBM)
TILE = (8, 128)
JAC = 4 * FIELDS * FIELDS
NUMBERS = JAC + S - 1 + 7


def lanes():
    return lax.broadcasted_iota(jnp.int32, TILE, 1)


def sublanes():
    return lax.broadcasted_iota(jnp.int32, TILE, 0)


def two_sum(a, b):
    total = a + b
    part = total - a
    return total, (a - (total - part)) + (b - part)


def split(a):
    scaled = a * 4097.0
    high = scaled - (scaled - a)
    return high, a - high


def pack_kernel(rotation, res_ref, gain_ref, near_ref, far_ref, jac_ref, omega_ref, shift_ref, out_ref, coef_ref):
    lane = lanes()
    first = lax.rem(lax.axis_index("cell"), 2) == 0
    group, place = lane // 32, lane % 32
    for f in range(FIELDS):
        for e in range(FIELDS):
            at = 4 * (f * FIELDS + e)
            coef_ref[at : at + 4, :] = jnp.broadcast_to(jac_ref[f, :, e : e + 1], (4, 128))
    for n in range(S - 1):
        coef_ref[JAC + n : JAC + n + 1, :] = jnp.broadcast_to(shift_ref[:, n : n + 1], (1, 128))
    omega = jnp.full((1, 128), omega_ref[0])
    for at, weight in enumerate(rotation, JAC + S - 1):
        coef_ref[at : at + 1, :] = omega * weight
    for field in range(STATE):
        own = res_ref.at[0, field] if field < FIELDS else gain_ref.at[0]
        below = jnp.where(first, far_ref[field], near_ref[field])
        above = jnp.where(first, near_ref[field], far_ref[field])
        rows = [below, own[0:8, :], own[8:16, :], above]
        for parity in range(2):
            moved = []
            for part in range(4):
                shift = (32 * part + HALO - COLS * parity) % 128
                moved.append([pltpu.roll(rows[part][:, 128 * h : 128 * h + 128], shift, 1) for h in range(2)])
            for inst in range(parity, INST, 2):
                chunk = None
                for part in range(4):
                    left, right = moved[part]
                    piece = left if inst < 8 else right
                    if inst in (7, 8):
                        piece = jnp.where(place < (24 if inst == 7 else 8), left, right)
                    chunk = piece if chunk is None else jnp.where(group == (part + inst // 2) % 4, piece, chunk)
                out_ref[TURN.index(inst), field * 8 : field * 8 + 8, :] = chunk


def merge_pair(first, second, mask, shift, axis):
    high = [jnp.where(mask, second[0], first[0]), jnp.where(mask, first[0], second[0])]
    total, error = two_sum(high[0], pltpu.roll(high[1], shift, axis))
    if first[1] is None:
        return total, error
    low = jnp.where(mask, second[1], first[1]) + pltpu.roll(
        jnp.where(mask, first[1], second[1]), shift, axis
    )
    return total, error + low


def fold_pair(pair, shift, axis):
    total, error = two_sum(pair[0], pltpu.roll(pair[0], shift, axis))
    return total, error + (pair[1] + pltpu.roll(pair[1], shift, axis))


def rotations(table):
    c = [0.0, *table]
    plus = [None] + [c[d] - c[8 - d] for d in (1, 2, 3)]
    minus = [None] + [(c[d] + c[8 - d]) / 2 for d in (1, 2, 3, 4)]
    return ((plus[1] - plus[3]) / 4, (plus[1] + plus[3]) / 4, plus[2] / 2, *minus[1:])


def gap(x, i, d):
    n = len(x)
    before, after = x[(i - d) % n], x[(i + d) % n]
    if i - d < 0:
        return before + after, -1
    return (before - after if i + d < n else before + after), 1


def turned(x, i, weights):
    n = len(x)
    total = None
    for d, weight in enumerate(weights, 1):
        if 2 * d < n:
            value, sign = gap(x, i, d)
        else:
            value, sign = x[(i - d) % n], (1 if i >= d else -1)
        term = weight * value
        if total is None:
            total = term if sign > 0 else -term
        else:
            total = total + term if sign > 0 else total - term
    return total


def coupled(v, weights):
    inner, first, second = weights[:3]
    plus = [v[i] + v[i + 8] for i in range(8)]
    minus = [v[i] - v[i + 8] for i in range(8)]
    sums = [plus[i] + plus[i + 4] for i in range(4)]
    gaps = [plus[i] - plus[i + 4] for i in range(4)]
    even, odd = inner * (sums[3] - sums[1]), inner * (sums[0] - sums[2])
    circle = [even, odd, -even, -odd]
    twisted = [turned(gaps, i, (first, second)) for i in range(4)]
    outer = [circle[i] + twisted[i] for i in range(4)] + [circle[i] - twisted[i] for i in range(4)]
    flipped = [turned(minus, i, weights[3:]) for i in range(8)]
    return [outer[i] + flipped[i] for i in range(8)] + [outer[i] - flipped[i] for i in range(8)]


SLOTS = ((2, 4), (3, 5), (6, 0), (7, 1))
SLOT_MOVES = (0, 16, 64, 80)


def segments():
    return ((lanes() + 128 - HALO) % 128) // 16


def in_slot(seg, q):
    return (seg == SLOTS[q][0]) | (seg == SLOTS[q][1])


TILES = INST * FIELDS
PITCH = 16


def tile_at(i, f):
    return PITCH * (i * FIELDS + f) + 8


def step_kernel(in_ref, number_ref, out_ref, vec_ref, coef_ref, mix_ref, gain_ref, slot_ref):
    lane, sub = lanes(), sublanes()
    seg = segments()
    cell, inst = lax.axis_index("cell"), lax.axis_index("inst")
    turn = lax.rem(inst // 2, 4)
    part = (lane // 32 + 4 - turn) % 4
    row = cell * ROWS - HALO + part * 8 + sub
    col = inst * COLS - HALO + lane % 32
    inside = (row >= 0) & (row < NR) & (col >= 0) & (col < NC)
    for d in range(4):
        for f in range(FIELDS):
            for e in range(FIELDS):
                at = 4 * (f * FIELDS + e) + d
                coef_ref[(d * FIELDS + f) * FIELDS + e] = jnp.broadcast_to(number_ref[at : at + 1, :], TILE)
    for i in range(INST):
        for f in range(FIELDS):
            vec_ref[0, pl.ds(tile_at(i, f), 8), :] = jnp.where(inside, in_ref[TURN.index(i), f * 8 : f * 8 + 8, :], 0.0)
        gain_ref[i] = in_ref[TURN.index(i), FIELDS * 8 : FIELDS * 8 + 8, :]

    weights = [jnp.broadcast_to(number_ref[at : at + 1, :], TILE) for at in range(JAC + S - 1, NUMBERS)]

    def step(n, carry):
        shift = jnp.broadcast_to(number_ref[pl.ds(JAC + n, 1), :], TILE)
        slot = lax.rem(n, 4)
        aligned = lax.rem(lax.rem(slot, 2) * 16 + (slot // 2) * 64 + 128 - 32 * turn, 128)
        now, later = vec_ref.at[n], vec_ref.at[n + 1]
        for group in range(TILES // 8):
            start = PITCH * 8 * group
            last = now[pl.ds(start + 15, 8, stride=PITCH), :]
            now[pl.ds(start + 7, 8, stride=PITCH), :] = pltpu.roll(last, 32, 1)
            first = now[pl.ds(start + 8, 8, stride=PITCH), :]
            now[pl.ds(start + 16, 8, stride=PITCH), :] = pltpu.roll(first, 96, 1)
        for f in range(FIELDS):
            mixed = coupled([now[pl.ds(tile_at(i, f), 8), :] for i in range(INST)], weights)
            for i in range(INST):
                mix_ref[i, f] = mixed[i]
        for pair in range(0, INST, 4):
            members = (pair, pair + 1, pair + 2, pair + 3)
            near, center, gain = {}, {}, {}
            for i in members:
                gain[i] = gain_ref[i] - shift
                for e in range(FIELDS):
                    at = tile_at(i, e)
                    v = now[pl.ds(at, 8), :]
                    center[i, e] = v
                    slot_ref[n, i, e] = pltpu.roll(v, aligned, 1)
                    near[i, 0, e] = now[pl.ds(at - 1, 8), :]
                    near[i, 1, e] = now[pl.ds(at + 1, 8), :]
                    near[i, 2, e] = pltpu.roll(v, 1, 1)
                    near[i, 3, e] = pltpu.roll(v, 127, 1)
            total = {(i, f): mix_ref[i, f] + gain[i] * center[i, f] for i in members for f in range(FIELDS)}
            for e in range(FIELDS):
                for d in range(4):
                    for f in range(FIELDS):
                        c = coef_ref[(d * FIELDS + f) * FIELDS + e]
                        for i in members:
                            total[i, f] = total[i, f] - c * near[i, d, e]
            for i in members:
                for f in range(FIELDS):
                    later[pl.ds(tile_at(i, f), 8), :] = jnp.where(inside, total[i, f], 0.0)
        return carry

    lax.fori_loop(0, S - 1, step, 0)

    packed = {}
    for x, y in ((0, 0), (1, 1), (0, 1)):
        for half in range(2):
            packed[x, y, half] = [(4 * x + q, 4 * y + (q + 2 * half) % 4, q) for q in range(4)]
    covered = {(min(a, b), max(a, b)) for entries in packed.values() for a, b, _ in entries}
    plain = [(a, b) for a in range(S) for b in range(a, S) if (a, b) not in covered]
    last_move = lax.rem(SLOT_MOVES[3] + 128 - 32 * turn, 128)

    def gather(quarter, sums):
        sums = list(sums)
        for i in [quarter * 4 + q for q in range(4)]:
            tiles = {}
            for f in range(FIELDS):
                at = pl.multiple_of(PITCH * FIELDS * i + tile_at(0, f), 8)
                v = [vec_ref[s, pl.ds(at, 8), :] for s in range(S)]
                moved = [slot_ref[s, i, f] for s in range(S - 1)] + [pltpu.roll(v[S - 1], last_move, 1)]
                for x in range(2):
                    a, b, c, d = moved[4 * x : 4 * x + 4]
                    tiles[x, f] = jnp.where(
                        in_slot(seg, 0), a, jnp.where(in_slot(seg, 1), b, jnp.where(in_slot(seg, 2), c, d))
                    )
                turned_tiles = [pltpu.roll(tiles[x, f], 64, 1) for x in range(2)]
                for p, (a, b) in enumerate(plain):
                    sums[p] = sums[p] + v[a] * v[b]
                for p, (x, y, half) in enumerate(packed, len(plain)):
                    sums[p] = sums[p] + tiles[x, f] * (turned_tiles[y] if half else tiles[y, f])
                out_ref[i, (4 + f) * 8 : (4 + f) * 8 + 8, :] = tiles[1, f]
            for f in range(4):
                tile = tiles[0, f]
                if f < 3:
                    move = (SLOT_MOVES[0] - SLOT_MOVES[f + 1]) % 128
                    tile = jnp.where(in_slot(seg, 0), pltpu.roll(tiles[0, 4], move, 1), tile)
                out_ref[i, f * 8 : f * 8 + 8, :] = tile
        return tuple(sums)

    start = tuple(jnp.zeros(TILE, jnp.float32) for _ in range(len(plain) + len(packed)))
    sums = lax.fori_loop(0, INST // 4, gather, start)
    column = lane % 32
    own = ((part == 1) | (part == 2)) & (column >= HALO) & (column < HALO + COLS)
    entry = {}
    for p, (a, b) in enumerate(plain):
        entry[a, b] = entry[b, a] = (jnp.where(own, sums[p], 0.0), None)
    for p, entries in enumerate(packed.values(), len(plain)):
        for a, b, q in entries:
            if (a, b) not in entry:
                entry[a, b] = entry[b, a] = (jnp.where(in_slot(seg, q), sums[p], 0.0), None)
    columns = []
    for b in range(S):
        level = [entry[a, b] for a in range(S)]
        for bit in (1, 2, 4):
            mask = (sub & bit) != 0
            level = [merge_pair(level[2 * q], level[2 * q + 1], mask, bit, 0) for q in range(len(level) // 2)]
        columns.append(level[0])
    for bit in (1, 2, 4):
        mask = (lane & bit) != 0
        columns = [merge_pair(columns[2 * q], columns[2 * q + 1], mask, bit, 1) for q in range(len(columns) // 2)]
    pair = columns[0]
    for shift in (64, 32, 16):
        pair = fold_pair(pair, shift, 1)
    pair = jnp.where(seg == SLOTS[0][0], pair[0], pair[1])
    for i in range(INST):
        out_ref[i, 24:32, :] = jnp.where(in_slot(seg, 0), pair, out_ref[i, 24:32, :])


def gram_kernel(in_ref, out_ref):
    lane, sub = lanes(), sublanes()
    total, error = sum_pairs([in_ref[i, 24:32, :] for i in range(INST)])
    high, low = fold_pair((total, error + pltpu.roll(total, 96, 1)), 8, 1)
    here = (lane >= 48) & (lane < 56)
    both = jnp.where(here, high, 0.0) + pltpu.roll(jnp.where(here, low, 0.0), 8, 1)
    for shift in (16, 32, 64):
        both = both + pltpu.roll(both, shift, 1)
    row = jnp.where(lane // 16 == sub, both, 0.0)
    row = jnp.broadcast_to(jnp.sum(row, axis=0, keepdims=True), TILE)
    for q in range(CELLS // 8):
        out_ref[q * 8 : q * 8 + 8, :] = row


def sum_pairs(values):
    level = [(v, None) for v in values]
    while len(level) > 1:
        merged = []
        for q in range(0, len(level), 2):
            total, error = two_sum(level[q][0], level[q + 1][0])
            if level[q][1] is not None:
                error = error + (level[q][1] + level[q + 1][1])
            merged.append((total, error))
        level = merged
    return level[0]


def unpack_kernel(in_ref, out_ref):
    seg = lanes() // 16
    places = {}
    for q, segs in enumerate(SLOTS):
        for part in range(2):
            places[segs[part]] = (q, part)
    for tile in range(9):
        for wide in range(2):
            tiles = [pltpu.roll(in_ref[8 * wide + q, tile * 8 : tile * 8 + 8, :], 128 - HALO, 1) for q in range(8)]
            for bit in (1, 2, 4):
                off = (seg & bit) == 0
                for q in range(8):
                    if q & bit:
                        continue
                    a, b = tiles[q], tiles[q + bit]
                    tiles[q] = jnp.where(off, a, pltpu.roll(b, 16 * bit, 1))
                    tiles[q + bit] = jnp.where(off, pltpu.roll(a, 128 - 16 * bit, 1), b)
            for q in range(8):
                s, part = places[q]
                if tile >= 4:
                    s, f = 4 + s, tile - 4
                elif s:
                    f = tile
                elif tile < 3:
                    s, f = tile + 1, 4
                else:
                    continue
                out_ref[s - 1, 0, f, 8 * part : 8 * part + 8, 128 * wide : 128 * wide + 128] = tiles[q]


TRIANGLE = [(i, j) for i in range(S) for j in range(i + 1)]


def inverse_of(lower, scale):
    inverse = {}
    for i in range(S):
        inverse[i, i] = scale[i]
        for j in range(i):
            total = lower[i, j] * inverse[j, j]
            for k in range(j + 1, i):
                total = total + lower[i, k] * inverse[k, j]
            inverse[i, j] = -(scale[i] * total)
    return inverse


def product_of(a, b):
    out = {}
    for i, j in TRIANGLE:
        total = a[i, j] * b[j, j]
        for k in range(j + 1, i + 1):
            total = total + a[i, k] * b[k, j]
        out[i, j] = total
    return out


def factor_pairs(high, low):
    lower, scale = {}, {}
    for k in range(S):
        full = {i: high[i, k] + low[i, k] for i in range(k, S)}
        scale[k] = lax.rsqrt(full[k])
        parts = {}
        for i in range(k, S):
            lower[i, k] = full[i] * scale[k]
            parts[i] = split(lower[i, k])
        for i in range(k, S):
            for j in range(k, i + 1):
                (a_high, a_low), (b_high, b_low) = parts[i], parts[j]
                high[i, j], rest = two_sum(high[i, j], -(a_high * b_high))
                low[i, j] = low[i, j] + (rest - (a_high * b_low + a_low * lower[j, k]))
    return lower, inverse_of(lower, scale), {at: high[at] + low[at] for at in TRIANGLE}


def factor_plain(matrix):
    lower, scale = {}, {}
    for k in range(S):
        scale[k] = lax.rsqrt(matrix[k, k])
        for i in range(k, S):
            lower[i, k] = matrix[i, k] * scale[k]
        for i in range(k + 1, S):
            for j in range(k + 1, i + 1):
                matrix[i, j] = matrix[i, j] - lower[i, k] * lower[j, k]
    return lower, inverse_of(lower, scale)


def finish_kernel(rows_ref, res_ref, vec_ref, out_ref, factor_ref):
    lane, sub = lanes(), sublanes()
    pair = sum_pairs([rows_ref[q * 8 : q * 8 + 8, :] for q in range(CELLS // 8)])
    for shift in (1, 2, 4):
        pair = fold_pair(pair, shift, 0)
    low_row = pair[1] + pltpu.roll(pair[0], 128 - S, 1)
    high = {(i, j): jnp.broadcast_to(pair[0][:, 16 * i + j : 16 * i + j + 1], TILE) for i, j in TRIANGLE}
    low = {(i, j): jnp.broadcast_to(low_row[:, 16 * i + j : 16 * i + j + 1], TILE) for i, j in TRIANGLE}
    lower_one, inverse_one, rest = factor_pairs(high, low)
    half = {}
    for i in range(S):
        for j in range(i + 1):
            total = None
            for k in range(i + 1):
                term = inverse_one[i, k] * rest[max(k, j), min(k, j)]
                total = term if total is None else total + term
            half[i, j] = total
    square = {}
    for i, j in TRIANGLE:
        total = half[i, 0] * inverse_one[j, 0]
        for k in range(1, j + 1):
            total = total + half[i, k] * inverse_one[j, k]
        square[i, j] = total + 1.0 if i == j else total
    lower_two, inverse_two = factor_plain(square)
    lower = product_of(lower_one, lower_two)
    weight = product_of(inverse_two, inverse_one)
    block = jnp.zeros(TILE, jnp.float32)
    for i, j in TRIANGLE:
        block = jnp.where((sub == j) & (lane == i), lower[i, j], block)
    factor_ref[...] = block[:, :S]
    for f in range(FIELDS):
        for part in range(2):
            for wide in range(2):
                place = (0, f, pl.ds(8 * part, 8), pl.ds(128 * wide, 128))
                v = [res_ref[place]] + [vec_ref[(s, *place)] for s in range(S - 1)]
                for a in range(S):
                    total = weight[a, 0] * v[0]
                    for b in range(1, a + 1):
                        total = total + weight[a, b] * v[b]
                    out_ref[(a, *place)] = total


def edge_kernel(res_ref, gain_ref, jac_ref, shift_ref, near_ref, far_ref, jac_out, shift_out, sems):
    odd = lax.rem(lax.axis_index("cell"), 2)
    moves = [(jac_ref, jac_out), (shift_ref, shift_out)]
    for ref, start in ((far_ref, 8 * odd), (near_ref, 8 * (1 - odd))):
        rows = pl.ds(pl.multiple_of(start, 8), 8)
        moves.append((res_ref.at[0, :, rows, :], ref.at[pl.ds(0, FIELDS)]))
        moves.append((gain_ref.at[:, rows, :], ref.at[pl.ds(FIELDS, 1)]))
    copies = [pltpu.make_async_copy(*move, sems.at[n]) for n, move in enumerate(moves)]
    for copy in copies:
        copy.start()
    for copy in copies:
        copy.wait()


def call(kernel, out_shape, in_specs, args, scratch=(), flops=10**6):
    shapes = jax.tree.map(lambda s: jax.ShapeDtypeStruct(s, jnp.float32), out_shape, is_leaf=lambda s: isinstance(s[0], int))
    return pl.pallas_call(
        kernel,
        out_shape=shapes,
        in_specs=in_specs,
        out_specs=jax.tree.map(lambda _: VMEM, shapes),
        scratch_shapes=scratch,
        compiler_params=pltpu.CompilerParams(vmem_limit_bytes=40 * 2**20),
        cost_estimate=pl.CostEstimate(flops=flops, transcendentals=0, bytes_accessed=2 * 10**6),
    )(*args)


def coupling_table():
    angles = np.pi * np.arange(1, 8) / INST
    return [float(c) for c in 0.5 * (-1.0) ** np.arange(1, 8) * np.cos(angles) / np.sin(angles)]


def on_device(residual, diag_gain, flux_jac, omega, shifts):
    pairs = [(i, i + 1) for i in range(CELLS - 1)]
    pairs = [pairs[0::2], pairs[1::2]]
    held = (residual, diag_gain, flux_jac.transpose(1, 0, 2), shifts[None])
    near, far, jac, shift = call(
        edge_kernel,
        ((STATE, 8, NC), (STATE, 8, NC), *[x.shape for x in held[2:]]),
        [HBM] * 4,
        [pltpu.with_memory_space_constraint(x, pltpu.HBM) for x in held],
        scratch=[pltpu.SemaphoreType.DMA((6,))],
    )
    far = lax.ppermute(far, "cell", pairs[1] + [(b, a) for a, b in pairs[1]])
    near = lax.ppermute(near, "cell", pairs[0] + [(b, a) for a, b in pairs[0]])
    chunks, numbers = call(
        functools.partial(pack_kernel, rotations(coupling_table())),
        ((INST, STATE * 8, 128), (NUMBERS + 6, 128)),
        [VMEM] * 5 + [pl.BlockSpec(memory_space=pltpu.SMEM), VMEM],
        (residual, diag_gain, near, far, jac, omega, shift),
    )
    patches = lax.all_to_all(chunks, "inst", 0, 0, axis_index_groups=[TURN], tiled=True)
    vectors = call(
        step_kernel,
        (INST, 72, 128),
        [VMEM, VMEM],
        (patches, numbers),
        scratch=[
            pltpu.VMEM((S, PITCH * (TILES + 1), 128), jnp.float32),
            pltpu.VMEM((JAC, *TILE), jnp.float32),
            pltpu.VMEM((INST, FIELDS, *TILE), jnp.float32),
            pltpu.VMEM((INST, *TILE), jnp.float32),
            pltpu.VMEM((S - 1, INST, FIELDS, *TILE), jnp.float32),
        ],
        flops=10**8,
    )
    back = lax.all_to_all(vectors, "inst", 0, 0, tiled=True)
    row = call(gram_kernel, (CELLS, 128), [VMEM], (back,))
    rows = lax.all_to_all(row, "cell", 0, 0, axis_index_groups=MEETING, tiled=True)
    others = call(unpack_kernel, (S - 1, 1, FIELDS, ROWS, NC), [VMEM], (back,))
    return call(
        finish_kernel,
        ((S, 1, FIELDS, ROWS, NC), (S, S)),
        [VMEM] * 3,
        (rows, residual, others),
    )


def solution(mesh):
    in_specs = (P("inst", None, "cell", None), P("inst", "cell", None), P(), P(), P())
    out_specs = (P(None, "inst", None, "cell", None), P())
    return jax.shard_map(
        on_device, mesh=mesh, in_specs=in_specs, out_specs=out_specs, check_vma=False
    )
```

```python
import functools

import jax
import jax.numpy as jnp
import numpy as np
from jax import lax
from jax.experimental import pallas as pl
from jax.experimental.pallas import tpu as pltpu
from jax.sharding import PartitionSpec as P


S = 8
FIELDS = 5
INST = 16
CELLS = 64
HALO = 8
ROWS = 16
COLS = 16
NC = 256
NR = 1024
STATE = FIELDS + 1
MEETING = [[(i + CELLS // 2) % CELLS for i in range(CELLS)]]
TURN = [(i + INST - 1) % INST for i in range(INST)]
VMEM = pl.BlockSpec(memory_space=pltpu.VMEM)
HBM = pl.BlockSpec(memory_space=pltpu.HBM)
TILE = (8, 128)
JAC = 4 * FIELDS * FIELDS
NUMBERS = JAC + S - 1 + 7


def lanes():
    return lax.broadcasted_iota(jnp.int32, TILE, 1)


def sublanes():
    return lax.broadcasted_iota(jnp.int32, TILE, 0)


def two_sum(a, b):
    total = a + b
    part = total - a
    return total, (a - (total - part)) + (b - part)


def split(a):
    scaled = a * 4097.0
    high = scaled - (scaled - a)
    return high, a - high


def pack_kernel(rotation, res_ref, gain_ref, near_ref, far_ref, jac_ref, omega_ref, shift_ref, out_ref, coef_ref):
    lane = lanes()
    first = lax.rem(lax.axis_index("cell"), 2) == 0
    group, place = lane // 32, lane % 32
    for f in range(FIELDS):
        for e in range(FIELDS):
            at = 4 * (f * FIELDS + e)
            coef_ref[at : at + 4, :] = jnp.broadcast_to(jac_ref[f, :, e : e + 1], (4, 128))
    for n in range(S - 1):
        coef_ref[JAC + n : JAC + n + 1, :] = jnp.broadcast_to(shift_ref[:, n : n + 1], (1, 128))
    omega = jnp.full((1, 128), omega_ref[0])
    for at, weight in enumerate(rotation, JAC + S - 1):
        coef_ref[at : at + 1, :] = omega * weight
    for field in range(STATE):
        own = res_ref.at[0, field] if field < FIELDS else gain_ref.at[0]
        below = jnp.where(first, far_ref[field], near_ref[field])
        above = jnp.where(first, near_ref[field], far_ref[field])
        rows = [below, own[0:8, :], own[8:16, :], above]
        for parity in range(2):
            moved = []
            for part in range(4):
                shift = (32 * part + HALO - COLS * parity) % 128
                moved.append([pltpu.roll(rows[part][:, 128 * h : 128 * h + 128], shift, 1) for h in range(2)])
            for inst in range(parity, INST, 2):
                chunk = None
                for part in range(4):
                    left, right = moved[part]
                    piece = left if inst < 8 else right
                    if inst in (7, 8):
                        piece = jnp.where(place < (24 if inst == 7 else 8), left, right)
                    chunk = piece if chunk is None else jnp.where(group == (part + inst // 2) % 4, piece, chunk)
                out_ref[TURN.index(inst), field * 8 : field * 8 + 8, :] = chunk


def merge_pair(first, second, mask, shift, axis):
    high = [jnp.where(mask, second[0], first[0]), jnp.where(mask, first[0], second[0])]
    total, error = two_sum(high[0], pltpu.roll(high[1], shift, axis))
    if first[1] is None:
        return total, error
    low = jnp.where(mask, second[1], first[1]) + pltpu.roll(
        jnp.where(mask, first[1], second[1]), shift, axis
    )
    return total, error + low


def fold_pair(pair, shift, axis):
    total, error = two_sum(pair[0], pltpu.roll(pair[0], shift, axis))
    return total, error + (pair[1] + pltpu.roll(pair[1], shift, axis))


def rotations(table):
    c = [0.0, *table]
    plus = [None] + [c[d] - c[8 - d] for d in (1, 2, 3)]
    minus = [None] + [(c[d] + c[8 - d]) / 2 for d in (1, 2, 3, 4)]
    return ((plus[1] - plus[3]) / 4, (plus[1] + plus[3]) / 4, plus[2] / 2, *minus[1:])


def gap(x, i, d):
    n = len(x)
    before, after = x[(i - d) % n], x[(i + d) % n]
    if i - d < 0:
        return before + after, -1
    return (before - after if i + d < n else before + after), 1


def turned(x, i, weights):
    n = len(x)
    total = None
    for d, weight in enumerate(weights, 1):
        if 2 * d < n:
            value, sign = gap(x, i, d)
        else:
            value, sign = x[(i - d) % n], (1 if i >= d else -1)
        term = weight * value
        if total is None:
            total = term if sign > 0 else -term
        else:
            total = total + term if sign > 0 else total - term
    return total


def coupled(v, weights):
    inner, first, second = weights[:3]
    plus = [v[i] + v[i + 8] for i in range(8)]
    minus = [v[i] - v[i + 8] for i in range(8)]
    sums = [plus[i] + plus[i + 4] for i in range(4)]
    gaps = [plus[i] - plus[i + 4] for i in range(4)]
    even, odd = inner * (sums[3] - sums[1]), inner * (sums[0] - sums[2])
    circle = [even, odd, -even, -odd]
    twisted = [turned(gaps, i, (first, second)) for i in range(4)]
    outer = [circle[i] + twisted[i] for i in range(4)] + [circle[i] - twisted[i] for i in range(4)]
    flipped = [turned(minus, i, weights[3:]) for i in range(8)]
    return [outer[i] + flipped[i] for i in range(8)] + [outer[i] - flipped[i] for i in range(8)]


SLOTS = ((2, 4), (3, 5), (6, 0), (7, 1))
SLOT_MOVES = (0, 16, 64, 80)


def segments():
    return ((lanes() + 128 - HALO) % 128) // 16


def in_slot(seg, q):
    return (seg == SLOTS[q][0]) | (seg == SLOTS[q][1])


TILES = INST * FIELDS
PITCH = 16


def tile_at(i, f):
    return PITCH * (i * FIELDS + f) + 8


def step_kernel(in_ref, number_ref, out_ref, vec_ref, coef_ref, mix_ref, gain_ref, slot_ref):
    lane, sub = lanes(), sublanes()
    seg = segments()
    cell, inst = lax.axis_index("cell"), lax.axis_index("inst")
    turn = lax.rem(inst // 2, 4)
    part = (lane // 32 + 4 - turn) % 4
    row = cell * ROWS - HALO + part * 8 + sub
    col = inst * COLS - HALO + lane % 32
    inside = (row >= 0) & (row < NR) & (col >= 0) & (col < NC)
    for d in range(4):
        for f in range(FIELDS):
            for e in range(FIELDS):
                at = 4 * (f * FIELDS + e) + d
                coef_ref[(d * FIELDS + f) * FIELDS + e] = jnp.broadcast_to(number_ref[at : at + 1, :], TILE)
    for i in range(INST):
        for f in range(FIELDS):
            vec_ref[0, pl.ds(tile_at(i, f), 8), :] = jnp.where(inside, in_ref[TURN.index(i), f * 8 : f * 8 + 8, :], 0.0)
        gain_ref[i] = in_ref[TURN.index(i), FIELDS * 8 : FIELDS * 8 + 8, :]

    weights = [jnp.broadcast_to(number_ref[at : at + 1, :], TILE) for at in range(JAC + S - 1, NUMBERS)]

    def step(n, carry):
        shift = jnp.broadcast_to(number_ref[pl.ds(JAC + n, 1), :], TILE)
        slot = lax.rem(n, 4)
        aligned = lax.rem(lax.rem(slot, 2) * 16 + (slot // 2) * 64 + 128 - 32 * turn, 128)
        now, later = vec_ref.at[n], vec_ref.at[n + 1]
        for group in range(TILES // 8):
            start = PITCH * 8 * group
            last = now[pl.ds(start + 15, 8, stride=PITCH), :]
            now[pl.ds(start + 7, 8, stride=PITCH), :] = pltpu.roll(last, 32, 1)
            first = now[pl.ds(start + 8, 8, stride=PITCH), :]
            now[pl.ds(start + 16, 8, stride=PITCH), :] = pltpu.roll(first, 96, 1)
        for f in range(FIELDS):
            mixed = coupled([now[pl.ds(tile_at(i, f), 8), :] for i in range(INST)], weights)
            for i in range(INST):
                mix_ref[i, f] = mixed[i]
        for pair in range(0, INST, 4):
            members = (pair, pair + 1, pair + 2, pair + 3)
            near, center, gain = {}, {}, {}
            for i in members:
                gain[i] = gain_ref[i] - shift
                for e in range(FIELDS):
                    at = tile_at(i, e)
                    v = now[pl.ds(at, 8), :]
                    center[i, e] = v
                    slot_ref[n, i, e] = pltpu.roll(v, aligned, 1)
                    near[i, 0, e] = now[pl.ds(at - 1, 8), :]
                    near[i, 1, e] = now[pl.ds(at + 1, 8), :]
                    near[i, 2, e] = pltpu.roll(v, 1, 1)
                    near[i, 3, e] = pltpu.roll(v, 127, 1)
            total = {(i, f): mix_ref[i, f] + gain[i] * center[i, f] for i in members for f in range(FIELDS)}
            for e in range(FIELDS):
                for d in range(4):
                    for f in range(FIELDS):
                        c = coef_ref[(d * FIELDS + f) * FIELDS + e]
                        for i in members:
                            total[i, f] = total[i, f] - c * near[i, d, e]
            for i in members:
                for f in range(FIELDS):
                    later[pl.ds(tile_at(i, f), 8), :] = jnp.where(inside, total[i, f], 0.0)
        return carry

    lax.fori_loop(0, S - 1, step, 0)

    packed = {}
    for x, y in ((0, 0), (1, 1), (0, 1)):
        for half in range(2):
            packed[x, y, half] = [(4 * x + q, 4 * y + (q + 2 * half) % 4, q) for q in range(4)]
    covered = {(min(a, b), max(a, b)) for entries in packed.values() for a, b, _ in entries}
    plain = [(a, b) for a in range(S) for b in range(a, S) if (a, b) not in covered]
    last_move = lax.rem(SLOT_MOVES[3] + 128 - 32 * turn, 128)

    def gather(quarter, sums):
        sums = list(sums)
        for i in [quarter * 4 + q for q in range(4)]:
            chunk = lax.rem(i + 1, INST)
            tiles = {}
            for f in range(FIELDS):
                at = pl.multiple_of(PITCH * FIELDS * i + tile_at(0, f), 8)
                v = [vec_ref[s, pl.ds(at, 8), :] for s in range(S)]
                moved = [slot_ref[s, i, f] for s in range(S - 1)] + [pltpu.roll(v[S - 1], last_move, 1)]
                for x in range(2):
                    a, b, c, d = moved[4 * x : 4 * x + 4]
                    tiles[x, f] = jnp.where(
                        in_slot(seg, 0), a, jnp.where(in_slot(seg, 1), b, jnp.where(in_slot(seg, 2), c, d))
                    )
                turned_tiles = [pltpu.roll(tiles[x, f], 64, 1) for x in range(2)]
                for p, (a, b) in enumerate(plain):
                    sums[p] = sums[p] + v[a] * v[b]
                for p, (x, y, half) in enumerate(packed, len(plain)):
                    sums[p] = sums[p] + tiles[x, f] * (turned_tiles[y] if half else tiles[y, f])
                out_ref[chunk, (4 + f) * 8 : (4 + f) * 8 + 8, :] = tiles[1, f]
            for f in range(4):
                tile = tiles[0, f]
                if f < 3:
                    move = (SLOT_MOVES[0] - SLOT_MOVES[f + 1]) % 128
                    tile = jnp.where(in_slot(seg, 0), pltpu.roll(tiles[0, 4], move, 1), tile)
                out_ref[chunk, f * 8 : f * 8 + 8, :] = tile
        return tuple(sums)

    start = tuple(jnp.zeros(TILE, jnp.float32) for _ in range(len(plain) + len(packed)))
    sums = lax.fori_loop(0, INST // 4, gather, start)
    column = lane % 32
    own = ((part == 1) | (part == 2)) & (column >= HALO) & (column < HALO + COLS)
    entry = {}
    for p, (a, b) in enumerate(plain):
        entry[a, b] = entry[b, a] = (jnp.where(own, sums[p], 0.0), None)
    for p, entries in enumerate(packed.values(), len(plain)):
        for a, b, q in entries:
            if (a, b) not in entry:
                entry[a, b] = entry[b, a] = (jnp.where(in_slot(seg, q), sums[p], 0.0), None)
    columns = []
    for b in range(S):
        level = [entry[a, b] for a in range(S)]
        for bit in (1, 2, 4):
            mask = (sub & bit) != 0
            level = [merge_pair(level[2 * q], level[2 * q + 1], mask, bit, 0) for q in range(len(level) // 2)]
        columns.append(level[0])
    for bit in (1, 2, 4):
        mask = (lane & bit) != 0
        columns = [merge_pair(columns[2 * q], columns[2 * q + 1], mask, bit, 1) for q in range(len(columns) // 2)]
    pair = columns[0]
    for shift in (64, 32, 16):
        pair = fold_pair(pair, shift, 1)
    pair = jnp.where(seg == SLOTS[0][0], pair[0], pair[1])
    for i in range(INST):
        out_ref[i, 24:32, :] = jnp.where(in_slot(seg, 0), pair, out_ref[i, 24:32, :])


def gram_kernel(in_ref, out_ref):
    lane, sub = lanes(), sublanes()
    total, error = sum_pairs([in_ref[i, 24:32, :] for i in range(INST)])
    high, low = fold_pair((total, error + pltpu.roll(total, 96, 1)), 8, 1)
    here = (lane >= 48) & (lane < 56)
    both = jnp.where(here, high, 0.0) + pltpu.roll(jnp.where(here, low, 0.0), 8, 1)
    for shift in (16, 32, 64):
        both = both + pltpu.roll(both, shift, 1)
    row = jnp.where(lane // 16 == sub, both, 0.0)
    row = jnp.broadcast_to(jnp.sum(row, axis=0, keepdims=True), TILE)
    for q in range(CELLS // 8):
        out_ref[q * 8 : q * 8 + 8, :] = row


def sum_pairs(values):
    level = [(v, None) for v in values]
    while len(level) > 1:
        merged = []
        for q in range(0, len(level), 2):
            total, error = two_sum(level[q][0], level[q + 1][0])
            if level[q][1] is not None:
                error = error + (level[q][1] + level[q + 1][1])
            merged.append((total, error))
        level = merged
    return level[0]


def unpack_kernel(in_ref, out_ref):
    seg = lanes() // 16
    places = {}
    for q, segs in enumerate(SLOTS):
        for part in range(2):
            places[segs[part]] = (q, part)
    for tile in range(9):
        for wide in range(2):
            tiles = [pltpu.roll(in_ref[TURN.index(8 * wide + q), tile * 8 : tile * 8 + 8, :], 128 - HALO, 1) for q in range(8)]
            for bit in (1, 2, 4):
                off = (seg & bit) == 0
                for q in range(8):
                    if q & bit:
                        continue
                    a, b = tiles[q], tiles[q + bit]
                    tiles[q] = jnp.where(off, a, pltpu.roll(b, 16 * bit, 1))
                    tiles[q + bit] = jnp.where(off, pltpu.roll(a, 128 - 16 * bit, 1), b)
            for q in range(8):
                s, part = places[q]
                if tile >= 4:
                    s, f = 4 + s, tile - 4
                elif s:
                    f = tile
                elif tile < 3:
                    s, f = tile + 1, 4
                else:
                    continue
                out_ref[s - 1, 0, f, 8 * part : 8 * part + 8, 128 * wide : 128 * wide + 128] = tiles[q]


TRIANGLE = [(i, j) for i in range(S) for j in range(i + 1)]


def inverse_of(lower, scale):
    inverse = {}
    for i in range(S):
        inverse[i, i] = scale[i]
        for j in range(i):
            total = lower[i, j] * inverse[j, j]
            for k in range(j + 1, i):
                total = total + lower[i, k] * inverse[k, j]
            inverse[i, j] = -(scale[i] * total)
    return inverse


def product_of(a, b):
    out = {}
    for i, j in TRIANGLE:
        total = a[i, j] * b[j, j]
        for k in range(j + 1, i + 1):
            total = total + a[i, k] * b[k, j]
        out[i, j] = total
    return out


def factor_pairs(high, low):
    lower, scale = {}, {}
    for k in range(S):
        full = {i: high[i, k] + low[i, k] for i in range(k, S)}
        scale[k] = lax.rsqrt(full[k])
        parts = {}
        for i in range(k, S):
            lower[i, k] = full[i] * scale[k]
            parts[i] = split(lower[i, k])
        for i in range(k, S):
            for j in range(k, i + 1):
                (a_high, a_low), (b_high, b_low) = parts[i], parts[j]
                high[i, j], rest = two_sum(high[i, j], -(a_high * b_high))
                low[i, j] = low[i, j] + (rest - (a_high * b_low + a_low * lower[j, k]))
    return lower, inverse_of(lower, scale), {at: high[at] + low[at] for at in TRIANGLE}


def factor_plain(matrix):
    lower, scale = {}, {}
    for k in range(S):
        scale[k] = lax.rsqrt(matrix[k, k])
        for i in range(k, S):
            lower[i, k] = matrix[i, k] * scale[k]
        for i in range(k + 1, S):
            for j in range(k + 1, i + 1):
                matrix[i, j] = matrix[i, j] - lower[i, k] * lower[j, k]
    return lower, inverse_of(lower, scale)


def finish_kernel(rows_ref, res_ref, vec_ref, out_ref, factor_ref):
    lane, sub = lanes(), sublanes()
    pair = sum_pairs([rows_ref[q * 8 : q * 8 + 8, :] for q in range(CELLS // 8)])
    for shift in (1, 2, 4):
        pair = fold_pair(pair, shift, 0)
    low_row = pair[1] + pltpu.roll(pair[0], 128 - S, 1)
    high = {(i, j): jnp.broadcast_to(pair[0][:, 16 * i + j : 16 * i + j + 1], TILE) for i, j in TRIANGLE}
    low = {(i, j): jnp.broadcast_to(low_row[:, 16 * i + j : 16 * i + j + 1], TILE) for i, j in TRIANGLE}
    lower_one, inverse_one, rest = factor_pairs(high, low)
    half = {}
    for i in range(S):
        for j in range(i + 1):
            total = None
            for k in range(i + 1):
                term = inverse_one[i, k] * rest[max(k, j), min(k, j)]
                total = term if total is None else total + term
            half[i, j] = total
    square = {}
    for i, j in TRIANGLE:
        total = half[i, 0] * inverse_one[j, 0]
        for k in range(1, j + 1):
            total = total + half[i, k] * inverse_one[j, k]
        square[i, j] = total + 1.0 if i == j else total
    lower_two, inverse_two = factor_plain(square)
    lower = product_of(lower_one, lower_two)
    weight = product_of(inverse_two, inverse_one)
    block = jnp.zeros(TILE, jnp.float32)
    for i, j in TRIANGLE:
        block = jnp.where((sub == j) & (lane == i), lower[i, j], block)
    factor_ref[...] = block[:, :S]
    for f in range(FIELDS):
        for part in range(2):
            for wide in range(2):
                place = (0, f, pl.ds(8 * part, 8), pl.ds(128 * wide, 128))
                v = [res_ref[place]] + [vec_ref[(s, *place)] for s in range(S - 1)]
                for a in range(S):
                    total = weight[a, 0] * v[0]
                    for b in range(1, a + 1):
                        total = total + weight[a, b] * v[b]
                    out_ref[(a, *place)] = total


def edge_kernel(res_ref, gain_ref, jac_ref, shift_ref, near_ref, far_ref, jac_out, shift_out, sems):
    odd = lax.rem(lax.axis_index("cell"), 2)
    moves = [(jac_ref, jac_out), (shift_ref, shift_out)]
    for ref, start in ((far_ref, 8 * odd), (near_ref, 8 * (1 - odd))):
        rows = pl.ds(pl.multiple_of(start, 8), 8)
        moves.append((res_ref.at[0, :, rows, :], ref.at[pl.ds(0, FIELDS)]))
        moves.append((gain_ref.at[:, rows, :], ref.at[pl.ds(FIELDS, 1)]))
    copies = [pltpu.make_async_copy(*move, sems.at[n]) for n, move in enumerate(moves)]
    for copy in copies:
        copy.start()
    for copy in copies:
        copy.wait()


def call(kernel, out_shape, in_specs, args, scratch=(), flops=10**6):
    shapes = jax.tree.map(lambda s: jax.ShapeDtypeStruct(s, jnp.float32), out_shape, is_leaf=lambda s: isinstance(s[0], int))
    return pl.pallas_call(
        kernel,
        out_shape=shapes,
        in_specs=in_specs,
        out_specs=jax.tree.map(lambda _: VMEM, shapes),
        scratch_shapes=scratch,
        compiler_params=pltpu.CompilerParams(vmem_limit_bytes=40 * 2**20),
        cost_estimate=pl.CostEstimate(flops=flops, transcendentals=0, bytes_accessed=2 * 10**6),
    )(*args)


def coupling_table():
    angles = np.pi * np.arange(1, 8) / INST
    return [float(c) for c in 0.5 * (-1.0) ** np.arange(1, 8) * np.cos(angles) / np.sin(angles)]


def on_device(residual, diag_gain, flux_jac, omega, shifts):
    pairs = [(i, i + 1) for i in range(CELLS - 1)]
    pairs = [pairs[0::2], pairs[1::2]]
    held = (residual, diag_gain, flux_jac.transpose(1, 0, 2), shifts[None])
    near, far, jac, shift = call(
        edge_kernel,
        ((STATE, 8, NC), (STATE, 8, NC), *[x.shape for x in held[2:]]),
        [HBM] * 4,
        [pltpu.with_memory_space_constraint(x, pltpu.HBM) for x in held],
        scratch=[pltpu.SemaphoreType.DMA((6,))],
    )
    far = lax.ppermute(far, "cell", pairs[1] + [(b, a) for a, b in pairs[1]])
    near = lax.ppermute(near, "cell", pairs[0] + [(b, a) for a, b in pairs[0]])
    chunks, numbers = call(
        functools.partial(pack_kernel, rotations(coupling_table())),
        ((INST, STATE * 8, 128), (NUMBERS + 6, 128)),
        [VMEM] * 5 + [pl.BlockSpec(memory_space=pltpu.SMEM), VMEM],
        (residual, diag_gain, near, far, jac, omega, shift),
    )
    patches = lax.all_to_all(chunks, "inst", 0, 0, axis_index_groups=[TURN], tiled=True)
    vectors = call(
        step_kernel,
        (INST, 72, 128),
        [VMEM, VMEM],
        (patches, numbers),
        scratch=[
            pltpu.VMEM((S, PITCH * (TILES + 1), 128), jnp.float32),
            pltpu.VMEM((JAC, *TILE), jnp.float32),
            pltpu.VMEM((INST, FIELDS, *TILE), jnp.float32),
            pltpu.VMEM((INST, *TILE), jnp.float32),
            pltpu.VMEM((S - 1, INST, FIELDS, *TILE), jnp.float32),
        ],
        flops=10**8,
    )
    back = lax.all_to_all(vectors, "inst", 0, 0, axis_index_groups=[TURN], tiled=True)
    row = call(gram_kernel, (CELLS, 128), [VMEM], (back,))
    rows = lax.all_to_all(row, "cell", 0, 0, axis_index_groups=MEETING, tiled=True)
    others = call(unpack_kernel, (S - 1, 1, FIELDS, ROWS, NC), [VMEM], (back,))
    return call(
        finish_kernel,
        ((S, 1, FIELDS, ROWS, NC), (S, S)),
        [VMEM] * 3,
        (rows, residual, others),
    )


def solution(mesh):
    in_specs = (P("inst", None, "cell", None), P("inst", "cell", None), P(), P(), P())
    out_specs = (P(None, "inst", None, "cell", None), P())
    return jax.shard_map(
        on_device, mesh=mesh, in_specs=in_specs, out_specs=out_specs, check_vma=False
    )
```

```python
import functools

import jax
import jax.numpy as jnp
import numpy as np
from jax import lax
from jax.experimental import pallas as pl
from jax.experimental.pallas import tpu as pltpu
from jax.sharding import PartitionSpec as P


S = 8
FIELDS = 5
INST = 16
CELLS = 64
HALO = 8
ROWS = 16
COLS = 16
NC = 256
NR = 1024
STATE = FIELDS + 1
MEETING = [[(i + CELLS // 2) % CELLS for i in range(CELLS)]]
TURN = [(i + INST - 1) % INST for i in range(INST)]
VMEM = pl.BlockSpec(memory_space=pltpu.VMEM)
HBM = pl.BlockSpec(memory_space=pltpu.HBM)
TILE = (8, 128)
JAC = 4 * FIELDS * FIELDS
NUMBERS = JAC + S - 1 + 7


def lanes():
    return lax.broadcasted_iota(jnp.int32, TILE, 1)


def sublanes():
    return lax.broadcasted_iota(jnp.int32, TILE, 0)


def two_sum(a, b):
    total = a + b
    part = total - a
    return total, (a - (total - part)) + (b - part)


def split(a):
    scaled = a * 4097.0
    high = scaled - (scaled - a)
    return high, a - high


def pack_kernel(rotation, res_ref, gain_ref, near_ref, far_ref, jac_ref, omega_ref, shift_ref, out_ref, coef_ref):
    lane = lanes()
    first = lax.rem(lax.axis_index("cell"), 2) == 0
    group, place = lane // 32, lane % 32
    for f in range(FIELDS):
        for e in range(FIELDS):
            at = 4 * (f * FIELDS + e)
            coef_ref[at : at + 4, :] = jnp.broadcast_to(jac_ref[f, :, e : e + 1], (4, 128))
    for n in range(S - 1):
        coef_ref[JAC + n : JAC + n + 1, :] = jnp.broadcast_to(shift_ref[:, n : n + 1], (1, 128))
    omega = jnp.full((1, 128), omega_ref[0])
    for at, weight in enumerate(rotation, JAC + S - 1):
        coef_ref[at : at + 1, :] = omega * weight
    for field in range(STATE):
        own = res_ref.at[0, field] if field < FIELDS else gain_ref.at[0]
        below = jnp.where(first, far_ref[field], near_ref[field])
        above = jnp.where(first, near_ref[field], far_ref[field])
        rows = [below, own[0:8, :], own[8:16, :], above]
        for parity in range(2):
            moved = []
            for part in range(4):
                shift = (32 * part + HALO - COLS * parity) % 128
                moved.append([pltpu.roll(rows[part][:, 128 * h : 128 * h + 128], shift, 1) for h in range(2)])
            for inst in range(parity, INST, 2):
                chunk = None
                for part in range(4):
                    left, right = moved[part]
                    piece = left if inst < 8 else right
                    if inst in (7, 8):
                        piece = jnp.where(place < (24 if inst == 7 else 8), left, right)
                    chunk = piece if chunk is None else jnp.where(group == (part + inst // 2) % 4, piece, chunk)
                out_ref[TURN.index(inst), field * 8 : field * 8 + 8, :] = chunk


def merge_pair(first, second, mask, shift, axis):
    high = [jnp.where(mask, second[0], first[0]), jnp.where(mask, first[0], second[0])]
    total, error = two_sum(high[0], pltpu.roll(high[1], shift, axis))
    if first[1] is None:
        return total, error
    low = jnp.where(mask, second[1], first[1]) + pltpu.roll(
        jnp.where(mask, first[1], second[1]), shift, axis
    )
    return total, error + low


def fold_pair(pair, shift, axis):
    total, error = two_sum(pair[0], pltpu.roll(pair[0], shift, axis))
    return total, error + (pair[1] + pltpu.roll(pair[1], shift, axis))


def rotations(table):
    c = [0.0, *table]
    plus = [None] + [c[d] - c[8 - d] for d in (1, 2, 3)]
    minus = [None] + [(c[d] + c[8 - d]) / 2 for d in (1, 2, 3, 4)]
    return ((plus[1] - plus[3]) / 4, (plus[1] + plus[3]) / 4, plus[2] / 2, *minus[1:])


def gap(x, i, d):
    n = len(x)
    before, after = x[(i - d) % n], x[(i + d) % n]
    if i - d < 0:
        return before + after, -1
    return (before - after if i + d < n else before + after), 1


def turned(x, i, weights):
    n = len(x)
    total = None
    for d, weight in enumerate(weights, 1):
        if 2 * d < n:
            value, sign = gap(x, i, d)
        else:
            value, sign = x[(i - d) % n], (1 if i >= d else -1)
        term = weight * value
        if total is None:
            total = term if sign > 0 else -term
        else:
            total = total + term if sign > 0 else total - term
    return total


def coupled(v, weights):
    inner, first, second = weights[:3]
    plus = [v[i] + v[i + 8] for i in range(8)]
    minus = [v[i] - v[i + 8] for i in range(8)]
    sums = [plus[i] + plus[i + 4] for i in range(4)]
    gaps = [plus[i] - plus[i + 4] for i in range(4)]
    even, odd = inner * (sums[3] - sums[1]), inner * (sums[0] - sums[2])
    circle = [even, odd, -even, -odd]
    twisted = [turned(gaps, i, (first, second)) for i in range(4)]
    outer = [circle[i] + twisted[i] for i in range(4)] + [circle[i] - twisted[i] for i in range(4)]
    flipped = [turned(minus, i, weights[3:]) for i in range(8)]
    return [outer[i] + flipped[i] for i in range(8)] + [outer[i] - flipped[i] for i in range(8)]


SLOTS = ((2, 4), (3, 5), (6, 0), (7, 1))
SLOT_MOVES = (0, 16, 64, 80)


def segments():
    return ((lanes() + 128 - HALO) % 128) // 16


def in_slot(seg, q):
    return (seg == SLOTS[q][0]) | (seg == SLOTS[q][1])


TILES = INST * FIELDS
PITCH = 16


def tile_at(i, f):
    return PITCH * (i * FIELDS + f) + 8


def step_kernel(in_ref, number_ref, out_ref, vec_ref, coef_ref, mix_ref, gain_ref, slot_ref):
    lane, sub = lanes(), sublanes()
    seg = segments()
    cell, inst = lax.axis_index("cell"), lax.axis_index("inst")
    turn = lax.rem(inst // 2, 4)
    part = (lane // 32 + 4 - turn) % 4
    row = cell * ROWS - HALO + part * 8 + sub
    col = inst * COLS - HALO + lane % 32
    inside = (row >= 0) & (row < NR) & (col >= 0) & (col < NC)
    for d in range(4):
        for f in range(FIELDS):
            for e in range(FIELDS):
                at = 4 * (f * FIELDS + e) + d
                coef_ref[(d * FIELDS + f) * FIELDS + e] = jnp.broadcast_to(number_ref[at : at + 1, :], TILE)
    for i in range(INST):
        for f in range(FIELDS):
            vec_ref[0, pl.ds(tile_at(i, f), 8), :] = jnp.where(inside, in_ref[TURN.index(i), f * 8 : f * 8 + 8, :], 0.0)
        gain_ref[i] = in_ref[TURN.index(i), FIELDS * 8 : FIELDS * 8 + 8, :]

    weights = [jnp.broadcast_to(number_ref[at : at + 1, :], TILE) for at in range(JAC + S - 1, NUMBERS)]

    def step(n, carry):
        shift = jnp.broadcast_to(number_ref[pl.ds(JAC + n, 1), :], TILE)
        slot = lax.rem(n, 4)
        aligned = lax.rem(lax.rem(slot, 2) * 16 + (slot // 2) * 64 + 128 - 32 * turn, 128)
        now, later = vec_ref.at[n], vec_ref.at[n + 1]
        for group in range(TILES // 8):
            start = PITCH * 8 * group
            last = now[pl.ds(start + 15, 8, stride=PITCH), :]
            now[pl.ds(start + 7, 8, stride=PITCH), :] = pltpu.roll(last, 32, 1)
            first = now[pl.ds(start + 8, 8, stride=PITCH), :]
            now[pl.ds(start + 16, 8, stride=PITCH), :] = pltpu.roll(first, 96, 1)
        for f in range(FIELDS):
            mixed = coupled([now[pl.ds(tile_at(i, f), 8), :] for i in range(INST)], weights)
            for i in range(INST):
                mix_ref[i, f] = mixed[i]
        for pair in range(0, INST, 4):
            members = (pair, pair + 1, pair + 2, pair + 3)
            near, center, gain = {}, {}, {}
            for i in members:
                gain[i] = gain_ref[i] - shift
                for e in range(FIELDS):
                    at = tile_at(i, e)
                    v = now[pl.ds(at, 8), :]
                    center[i, e] = v
                    slot_ref[n, i, e] = pltpu.roll(v, aligned, 1)
                    near[i, 0, e] = now[pl.ds(at - 1, 8), :]
                    near[i, 1, e] = now[pl.ds(at + 1, 8), :]
                    near[i, 2, e] = pltpu.roll(v, 1, 1)
                    near[i, 3, e] = pltpu.roll(v, 127, 1)
            total = {(i, f): mix_ref[i, f] + gain[i] * center[i, f] for i in members for f in range(FIELDS)}
            for e in range(FIELDS):
                for d in range(4):
                    for f in range(FIELDS):
                        c = coef_ref[(d * FIELDS + f) * FIELDS + e]
                        for i in members:
                            total[i, f] = total[i, f] - c * near[i, d, e]
            for i in members:
                for f in range(FIELDS):
                    later[pl.ds(tile_at(i, f), 8), :] = jnp.where(inside, total[i, f], 0.0)
        return carry

    lax.fori_loop(0, S - 1, step, 0)

    packed = {}
    for x, y in ((0, 0), (1, 1), (0, 1)):
        for half in range(2):
            packed[x, y, half] = [(4 * x + q, 4 * y + (q + 2 * half) % 4, q) for q in range(4)]
    covered = {(min(a, b), max(a, b)) for entries in packed.values() for a, b, _ in entries}
    plain = [(a, b) for a in range(S) for b in range(a, S) if (a, b) not in covered]
    last_move = lax.rem(SLOT_MOVES[3] + 128 - 32 * turn, 128)

    def gather(quarter, sums):
        sums = list(sums)
        for i in [quarter * 4 + q for q in range(4)]:
            chunk = (i + 1) % INST
            tiles = {}
            for f in range(FIELDS):
                at = tile_at(i, f)
                v = [vec_ref[s, pl.ds(at, 8), :] for s in range(S)]
                moved = [slot_ref[s, i, f] for s in range(S - 1)] + [pltpu.roll(v[S - 1], last_move, 1)]
                for x in range(2):
                    a, b, c, d = moved[4 * x : 4 * x + 4]
                    tiles[x, f] = jnp.where(
                        in_slot(seg, 0), a, jnp.where(in_slot(seg, 1), b, jnp.where(in_slot(seg, 2), c, d))
                    )
                turned_tiles = [pltpu.roll(tiles[x, f], 64, 1) for x in range(2)]
                for p, (a, b) in enumerate(plain):
                    sums[p] = sums[p] + v[a] * v[b]
                for p, (x, y, half) in enumerate(packed, len(plain)):
                    sums[p] = sums[p] + tiles[x, f] * (turned_tiles[y] if half else tiles[y, f])
                out_ref[chunk, (4 + f) * 8 : (4 + f) * 8 + 8, :] = tiles[1, f]
            for f in range(4):
                tile = tiles[0, f]
                if f < 3:
                    move = (SLOT_MOVES[0] - SLOT_MOVES[f + 1]) % 128
                    tile = jnp.where(in_slot(seg, 0), pltpu.roll(tiles[0, 4], move, 1), tile)
                out_ref[chunk, f * 8 : f * 8 + 8, :] = tile
        return tuple(sums)

    start = tuple(jnp.zeros(TILE, jnp.float32) for _ in range(len(plain) + len(packed)))
    sums = start
    for quarter in range(INST // 4):
        sums = gather(quarter, sums)
    column = lane % 32
    own = ((part == 1) | (part == 2)) & (column >= HALO) & (column < HALO + COLS)
    entry = {}
    for p, (a, b) in enumerate(plain):
        entry[a, b] = entry[b, a] = (jnp.where(own, sums[p], 0.0), None)
    for p, entries in enumerate(packed.values(), len(plain)):
        for a, b, q in entries:
            if (a, b) not in entry:
                entry[a, b] = entry[b, a] = (jnp.where(in_slot(seg, q), sums[p], 0.0), None)
    columns = []
    for b in range(S):
        level = [entry[a, b] for a in range(S)]
        for bit in (1, 2, 4):
            mask = (sub & bit) != 0
            level = [merge_pair(level[2 * q], level[2 * q + 1], mask, bit, 0) for q in range(len(level) // 2)]
        columns.append(level[0])
    for bit in (1, 2, 4):
        mask = (lane & bit) != 0
        columns = [merge_pair(columns[2 * q], columns[2 * q + 1], mask, bit, 1) for q in range(len(columns) // 2)]
    pair = columns[0]
    for shift in (64, 32, 16):
        pair = fold_pair(pair, shift, 1)
    pair = jnp.where(seg == SLOTS[0][0], pair[0], pair[1])
    for i in range(INST):
        out_ref[i, 24:32, :] = jnp.where(in_slot(seg, 0), pair, out_ref[i, 24:32, :])


def gram_kernel(in_ref, out_ref):
    lane, sub = lanes(), sublanes()
    total, error = sum_pairs([in_ref[i, 24:32, :] for i in range(INST)])
    high, low = fold_pair((total, error + pltpu.roll(total, 96, 1)), 8, 1)
    here = (lane >= 48) & (lane < 56)
    both = jnp.where(here, high, 0.0) + pltpu.roll(jnp.where(here, low, 0.0), 8, 1)
    for shift in (16, 32, 64):
        both = both + pltpu.roll(both, shift, 1)
    row = jnp.where(lane // 16 == sub, both, 0.0)
    row = jnp.broadcast_to(jnp.sum(row, axis=0, keepdims=True), TILE)
    for q in range(CELLS // 8):
        out_ref[q * 8 : q * 8 + 8, :] = row


def sum_pairs(values):
    level = [(v, None) for v in values]
    while len(level) > 1:
        merged = []
        for q in range(0, len(level), 2):
            total, error = two_sum(level[q][0], level[q + 1][0])
            if level[q][1] is not None:
                error = error + (level[q][1] + level[q + 1][1])
            merged.append((total, error))
        level = merged
    return level[0]


def unpack_kernel(in_ref, out_ref):
    seg = lanes() // 16
    places = {}
    for q, segs in enumerate(SLOTS):
        for part in range(2):
            places[segs[part]] = (q, part)
    for tile in range(9):
        for wide in range(2):
            tiles = [pltpu.roll(in_ref[TURN.index(8 * wide + q), tile * 8 : tile * 8 + 8, :], 128 - HALO, 1) for q in range(8)]
            for bit in (1, 2, 4):
                off = (seg & bit) == 0
                for q in range(8):
                    if q & bit:
                        continue
                    a, b = tiles[q], tiles[q + bit]
                    tiles[q] = jnp.where(off, a, pltpu.roll(b, 16 * bit, 1))
                    tiles[q + bit] = jnp.where(off, pltpu.roll(a, 128 - 16 * bit, 1), b)
            for q in range(8):
                s, part = places[q]
                if tile >= 4:
                    s, f = 4 + s, tile - 4
                elif s:
                    f = tile
                elif tile < 3:
                    s, f = tile + 1, 4
                else:
                    continue
                out_ref[s - 1, 0, f, 8 * part : 8 * part + 8, 128 * wide : 128 * wide + 128] = tiles[q]


TRIANGLE = [(i, j) for i in range(S) for j in range(i + 1)]


def inverse_of(lower, scale):
    inverse = {}
    for i in range(S):
        inverse[i, i] = scale[i]
        for j in range(i):
            total = lower[i, j] * inverse[j, j]
            for k in range(j + 1, i):
                total = total + lower[i, k] * inverse[k, j]
            inverse[i, j] = -(scale[i] * total)
    return inverse


def product_of(a, b):
    out = {}
    for i, j in TRIANGLE:
        total = a[i, j] * b[j, j]
        for k in range(j + 1, i + 1):
            total = total + a[i, k] * b[k, j]
        out[i, j] = total
    return out


def factor_pairs(high, low):
    lower, scale = {}, {}
    for k in range(S):
        full = {i: high[i, k] + low[i, k] for i in range(k, S)}
        scale[k] = lax.rsqrt(full[k])
        parts = {}
        for i in range(k, S):
            lower[i, k] = full[i] * scale[k]
            parts[i] = split(lower[i, k])
        for i in range(k, S):
            for j in range(k, i + 1):
                (a_high, a_low), (b_high, b_low) = parts[i], parts[j]
                high[i, j], rest = two_sum(high[i, j], -(a_high * b_high))
                low[i, j] = low[i, j] + (rest - (a_high * b_low + a_low * lower[j, k]))
    return lower, inverse_of(lower, scale), {at: high[at] + low[at] for at in TRIANGLE}


def factor_plain(matrix):
    lower, scale = {}, {}
    for k in range(S):
        scale[k] = lax.rsqrt(matrix[k, k])
        for i in range(k, S):
            lower[i, k] = matrix[i, k] * scale[k]
        for i in range(k + 1, S):
            for j in range(k + 1, i + 1):
                matrix[i, j] = matrix[i, j] - lower[i, k] * lower[j, k]
    return lower, inverse_of(lower, scale)


def finish_kernel(rows_ref, res_ref, vec_ref, out_ref, factor_ref):
    lane, sub = lanes(), sublanes()
    pair = sum_pairs([rows_ref[q * 8 : q * 8 + 8, :] for q in range(CELLS // 8)])
    for shift in (1, 2, 4):
        pair = fold_pair(pair, shift, 0)
    low_row = pair[1] + pltpu.roll(pair[0], 128 - S, 1)
    high = {(i, j): jnp.broadcast_to(pair[0][:, 16 * i + j : 16 * i + j + 1], TILE) for i, j in TRIANGLE}
    low = {(i, j): jnp.broadcast_to(low_row[:, 16 * i + j : 16 * i + j + 1], TILE) for i, j in TRIANGLE}
    lower_one, inverse_one, rest = factor_pairs(high, low)
    half = {}
    for i in range(S):
        for j in range(i + 1):
            total = None
            for k in range(i + 1):
                term = inverse_one[i, k] * rest[max(k, j), min(k, j)]
                total = term if total is None else total + term
            half[i, j] = total
    square = {}
    for i, j in TRIANGLE:
        total = half[i, 0] * inverse_one[j, 0]
        for k in range(1, j + 1):
            total = total + half[i, k] * inverse_one[j, k]
        square[i, j] = total + 1.0 if i == j else total
    lower_two, inverse_two = factor_plain(square)
    lower = product_of(lower_one, lower_two)
    weight = product_of(inverse_two, inverse_one)
    block = jnp.zeros(TILE, jnp.float32)
    for i, j in TRIANGLE:
        block = jnp.where((sub == j) & (lane == i), lower[i, j], block)
    factor_ref[...] = block[:, :S]
    for f in range(FIELDS):
        for part in range(2):
            for wide in range(2):
                place = (0, f, pl.ds(8 * part, 8), pl.ds(128 * wide, 128))
                v = [res_ref[place]] + [vec_ref[(s, *place)] for s in range(S - 1)]
                for a in range(S):
                    total = weight[a, 0] * v[0]
                    for b in range(1, a + 1):
                        total = total + weight[a, b] * v[b]
                    out_ref[(a, *place)] = total


def edge_kernel(res_ref, gain_ref, jac_ref, shift_ref, near_ref, far_ref, jac_out, shift_out, sems):
    odd = lax.rem(lax.axis_index("cell"), 2)
    moves = [(jac_ref, jac_out), (shift_ref, shift_out)]
    for ref, start in ((far_ref, 8 * odd), (near_ref, 8 * (1 - odd))):
        rows = pl.ds(pl.multiple_of(start, 8), 8)
        moves.append((res_ref.at[0, :, rows, :], ref.at[pl.ds(0, FIELDS)]))
        moves.append((gain_ref.at[:, rows, :], ref.at[pl.ds(FIELDS, 1)]))
    copies = [pltpu.make_async_copy(*move, sems.at[n]) for n, move in enumerate(moves)]
    for copy in copies:
        copy.start()
    for copy in copies:
        copy.wait()


def call(kernel, out_shape, in_specs, args, scratch=(), flops=10**6):
    shapes = jax.tree.map(lambda s: jax.ShapeDtypeStruct(s, jnp.float32), out_shape, is_leaf=lambda s: isinstance(s[0], int))
    return pl.pallas_call(
        kernel,
        out_shape=shapes,
        in_specs=in_specs,
        out_specs=jax.tree.map(lambda _: VMEM, shapes),
        scratch_shapes=scratch,
        compiler_params=pltpu.CompilerParams(vmem_limit_bytes=40 * 2**20),
        cost_estimate=pl.CostEstimate(flops=flops, transcendentals=0, bytes_accessed=2 * 10**6),
    )(*args)


def coupling_table():
    angles = np.pi * np.arange(1, 8) / INST
    return [float(c) for c in 0.5 * (-1.0) ** np.arange(1, 8) * np.cos(angles) / np.sin(angles)]


def on_device(residual, diag_gain, flux_jac, omega, shifts):
    pairs = [(i, i + 1) for i in range(CELLS - 1)]
    pairs = [pairs[0::2], pairs[1::2]]
    held = (residual, diag_gain, flux_jac.transpose(1, 0, 2), shifts[None])
    near, far, jac, shift = call(
        edge_kernel,
        ((STATE, 8, NC), (STATE, 8, NC), *[x.shape for x in held[2:]]),
        [HBM] * 4,
        [pltpu.with_memory_space_constraint(x, pltpu.HBM) for x in held],
        scratch=[pltpu.SemaphoreType.DMA((6,))],
    )
    far = lax.ppermute(far, "cell", pairs[1] + [(b, a) for a, b in pairs[1]])
    near = lax.ppermute(near, "cell", pairs[0] + [(b, a) for a, b in pairs[0]])
    chunks, numbers = call(
        functools.partial(pack_kernel, rotations(coupling_table())),
        ((INST, STATE * 8, 128), (NUMBERS + 6, 128)),
        [VMEM] * 5 + [pl.BlockSpec(memory_space=pltpu.SMEM), VMEM],
        (residual, diag_gain, near, far, jac, omega, shift),
    )
    patches = lax.all_to_all(chunks, "inst", 0, 0, axis_index_groups=[TURN], tiled=True)
    vectors = call(
        step_kernel,
        (INST, 72, 128),
        [VMEM, VMEM],
        (patches, numbers),
        scratch=[
            pltpu.VMEM((S, PITCH * (TILES + 1), 128), jnp.float32),
            pltpu.VMEM((JAC, *TILE), jnp.float32),
            pltpu.VMEM((INST, FIELDS, *TILE), jnp.float32),
            pltpu.VMEM((INST, *TILE), jnp.float32),
            pltpu.VMEM((S - 1, INST, FIELDS, *TILE), jnp.float32),
        ],
        flops=10**8,
    )
    back = lax.all_to_all(vectors, "inst", 0, 0, axis_index_groups=[TURN], tiled=True)
    row = call(gram_kernel, (CELLS, 128), [VMEM], (back,))
    rows = lax.all_to_all(row, "cell", 0, 0, axis_index_groups=MEETING, tiled=True)
    others = call(unpack_kernel, (S - 1, 1, FIELDS, ROWS, NC), [VMEM], (back,))
    return call(
        finish_kernel,
        ((S, 1, FIELDS, ROWS, NC), (S, S)),
        [VMEM] * 3,
        (rows, residual, others),
    )


def solution(mesh):
    in_specs = (P("inst", None, "cell", None), P("inst", "cell", None), P(), P(), P())
    out_specs = (P(None, "inst", None, "cell", None), P())
    return jax.shard_map(
        on_device, mesh=mesh, in_specs=in_specs, out_specs=out_specs, check_vma=False
    )
```
